256 devices in a mesh: pole: 8 (over x_hi, y), row: 32 (over x_lo, z, core).
Axes of the slice: x: 4 (x_hi: 2, x_lo: 2; x = x_hi * 2 + x_lo), y: 4, z: 8, core: 2. Of those that a mesh axis runs over, the one named last changes fastest.
Arguments:
- basis: bfloat16 [131072, 128], P('row'), may hold values from -24 to 24
- inverses: bfloat16 [8, 256, 512, 512], P('pole', 'row'), may hold values from -1.5 to 1.5
- lower: bfloat16 [256, 512, 512], P('row'), may hold values from -0.03955078 to 0.03955078
- upper: bfloat16 [256, 512, 512], P('row'), may hold values from -0.03955078 to 0.03955078
- pole_weights: float32 [8], P('pole'), may hold values from 0.5 to 1.5
Outputs:
- new_basis: float32 [131072, 128], P(('row', 'pole'))
The draws below stay inside these ranges and needn't reach their ends.
All inputs are finite; a program needn't handle non-finite values.
Results may differ from the reference program's by a relative error of at most 0.003.
Values may be sent and summed in bfloat16 or wider, within the bound.
No kernel may reach another device: no remote copies, remote signals or barrier semaphores. Data moves between devices by JAX's collectives and lax.ppermute only.
A program may use at most 64 MiB of HBM per device.

```python
import math
import jax
import jax.numpy as jnp
from jax import lax

VECTORS = 128
BLOCK = 512
SWEEPS = 4
POLES = 8
NBLK = 256
NROWS = 131072


def draw_basis(key, part):
    first, second = jax.random.split(jax.random.fold_in(key, 11), 2)
    place = jnp.arange(NROWS, dtype=jnp.float32) / (NROWS - 1)
    factor = jnp.exp(jax.random.uniform(second, (NROWS,), jnp.float32, 0.0, math.log(4.0)))
    scales = (1.0 + 2.0 * place) * factor
    values = jnp.clip(jax.random.normal(first, (NROWS, VECTORS), jnp.float32), -6.0, 6.0)
    return (values * scales[:, None] / 3.0).astype(jnp.bfloat16)


def draw_inverses(key, part):
    first, second = jax.random.split(jax.random.fold_in(key, 23), 2)
    diag_values = jnp.exp(jax.random.uniform(first, (POLES, NBLK, BLOCK), jnp.float32, math.log(0.4), 0.0))
    spread = 0.15 / math.sqrt(BLOCK)
    rough = spread * jnp.clip(jax.random.normal(second, (POLES, NBLK, BLOCK, BLOCK), jnp.float32), -6.0, 6.0)
    eye = jnp.eye(BLOCK, dtype=jnp.float32)
    return (rough + eye * diag_values[..., None, :]).astype(jnp.bfloat16)


def steps_of(key, extent, cuts, smallest, largest):
    def one(dim, blocks):
        steps = jax.random.uniform(jax.random.fold_in(jax.random.fold_in(key, 6), dim), (blocks,), jnp.float32, smallest / len(cuts), largest / len(cuts))
        return jnp.repeat(jnp.exp(steps), extent[dim] // blocks).reshape((-1,) + (1,) * (len(extent) - dim - 1))

    level = one(*cuts[0])
    for cut in cuts[1:]:
        level = level * one(*cut)
    return level


def noise(rng, dims, scale, reach, shards=(), kind=jnp.bfloat16):
    values = jax.random.normal(rng, dims, jnp.float32) * scale
    if len(shards) > 0:
        values = steps_of(rng, dims, shards, -0.22, 0.18) * values
    return jnp.clip(values, min=-reach, max=reach).astype(kind)


def setup_inputs(seed: int = 0) -> dict:
    arg_keys = jax.random.split(jax.random.key(seed), 6)
    basis = draw_basis(jax.random.fold_in(arg_keys[5], 71), 0)
    inverses = draw_inverses(jax.random.fold_in(arg_keys[5], 71), 0)
    lower = noise(arg_keys[2], (NBLK, BLOCK, BLOCK), (0.3 / BLOCK ** 0.5), 0.03955078, ((0, 32),))
    upper = noise(arg_keys[3], (NBLK, BLOCK, BLOCK), (0.3 / BLOCK ** 0.5), 0.03955078, ((0, 32),))
    pole_weights = jnp.clip(0.5 + 1.0 * jax.random.uniform(arg_keys[4], (POLES,), jnp.float32) ** steps_of(arg_keys[4], (POLES,), ((0, 8),), -0.2, 0.2), 0.5, 1.5)
    return dict(basis=basis, inverses=inverses, lower=lower, upper=upper, pole_weights=pole_weights)


def reference(basis, inverses, lower, upper, pole_weights):
    blocks = basis.reshape(NBLK, BLOCK, VECTORS).astype(jnp.float32)
    lower_f = lower.astype(jnp.float32)
    upper_f = upper.astype(jnp.float32)

    def one_pole(total, item):
        inverse_f = item[0].astype(jnp.float32)
        state = jnp.einsum('bij,bjk->bik', inverse_f, blocks).astype(jnp.bfloat16)
        zero_block = jnp.zeros((1, BLOCK, VECTORS), jnp.bfloat16)
        for sweep in range(SWEEPS):
            before = jnp.concatenate([zero_block, state[:-1]], axis=0).astype(jnp.float32)
            after = jnp.concatenate([state[1:], zero_block], axis=0).astype(jnp.float32)
            rhs = blocks + jnp.einsum('bij,bjk->bik', lower_f, before) + jnp.einsum('bij,bjk->bik', upper_f, after)
            rhs = rhs.astype(jnp.bfloat16).astype(jnp.float32)
            state = jnp.einsum('bij,bjk->bik', inverse_f, rhs).astype(jnp.bfloat16)
        return (total + item[1] * state.astype(jnp.float32), None)
    start = jnp.zeros((NBLK, BLOCK, VECTORS), jnp.float32)
    total, unused = lax.scan(one_pole, start, (inverses, pole_weights))
    filtered = total.reshape(NROWS, VECTORS)
    gram = jnp.dot(filtered.T, filtered, precision=lax.Precision.HIGHEST) / NROWS
    factor = jnp.linalg.cholesky(gram)
    solved = jax.scipy.linalg.solve_triangular(factor, filtered.T, lower=True)
    return solved.T
```

```python
import functools

import jax
import jax.numpy as jnp
from jax import lax
from jax.experimental import pallas as pl
from jax.experimental.pallas import tpu as pltpu
from jax.sharding import Mesh, PartitionSpec as P

SWEEPS = 4
EXTRA = 16
F32 = jnp.float32
BF16 = jnp.bfloat16
HI = lax.Precision.HIGHEST
VM = pl.BlockSpec(memory_space=pltpu.VMEM)
SM = pl.BlockSpec(memory_space=pltpu.SMEM)
LIMIT = 50 << 20


def dot(a, b):
    return jnp.dot(a, b, preferred_element_type=F32)


def params():
    return pltpu.CompilerParams(vmem_limit_bytes=LIMIT)


def cost(flops, moved):
    return pl.CostEstimate(flops=int(flops), bytes_accessed=int(moved), transcendentals=0)


def first_edges_kernel(inv_a, inv_b, basis_a, basis_b, first, last):
    first[...] = dot(inv_a[0, 0], basis_a[...]).astype(BF16)
    last[...] = dot(inv_b[0, 0], basis_b[...]).astype(BF16)


def first_edges(inverses, basis, count, size, width):
    edge = count - 1
    out = jax.ShapeDtypeStruct((size, width), BF16)
    return pl.pallas_call(
        first_edges_kernel,
        grid=(1,),
        out_shape=(out, out),
        in_specs=[
            pl.BlockSpec((1, 1, size, size), lambda i: (0, 0, 0, 0)),
            pl.BlockSpec((1, 1, size, size), lambda i: (0, edge, 0, 0)),
            pl.BlockSpec((size, width), lambda i: (0, 0)),
            pl.BlockSpec((size, width), lambda i: (edge, 0)),
        ],
        out_specs=(
            pl.BlockSpec((size, width), lambda i: (0, 0)),
            pl.BlockSpec((size, width), lambda i: (0, 0)),
        ),
        compiler_params=params(),
        name="first_edges",
    )(inverses, inverses, basis, basis)


def advance(count, left, right, start, first, middle, last, out, partial):
    def state(b):
        if b == 0:
            return first
        if b == count - 1:
            return last
        return middle[b - 1]

    for b in range(1, count - 1):
        value = start[b] + dot(left[b], state(b - 1)) + dot(right[b], state(b + 1))
        out[b - 1, : value.shape[0]] = value.astype(BF16)
    partial[0] = start[0] + dot(right[0], state(1))
    partial[1] = start[count - 1] + dot(left[count - 1], state(count - 2))


def setup_kernel(count, inv, lower, upper, basis, left, right, start, middle, partial, held):
    b = pl.program_id(0)
    inverse = inv[0, 0]
    left[b] = dot(inverse, lower[0]).astype(BF16)
    right[b] = dot(inverse, upper[0]).astype(BF16)
    value = dot(inverse, basis[...])
    start[b] = value
    held[b] = value.astype(BF16)

    @pl.when(b == count - 1)
    def _():
        advance(
            count, left, right, start, held[0],
            [held[i] for i in range(1, count - 1)], held[count - 1], middle, partial,
        )


def setup(inverses, lower, upper, basis, count, size, width):
    flops = 2 * count * size * size * (2 * size + 3 * width)
    return pl.pallas_call(
        functools.partial(setup_kernel, count),
        grid=(count,),
        out_shape=(
            jax.ShapeDtypeStruct((count, size, size), BF16),
            jax.ShapeDtypeStruct((count, size, size), BF16),
            jax.ShapeDtypeStruct((count, size, width), F32),
            jax.ShapeDtypeStruct((count - 2, size, width), BF16),
            jax.ShapeDtypeStruct((2, size, width), F32),
        ),
        in_specs=[
            pl.BlockSpec((1, 1, size, size), lambda b: (0, b, 0, 0)),
            pl.BlockSpec((1, size, size), lambda b: (b, 0, 0)),
            pl.BlockSpec((1, size, size), lambda b: (b, 0, 0)),
            pl.BlockSpec((size, width), lambda b: (b, 0)),
        ],
        out_specs=(VM, VM, VM, VM, VM),
        scratch_shapes=[pltpu.VMEM((count, size, width), BF16)],
        compiler_params=params(),
        cost_estimate=cost(flops, 6 * count * size * size),
        name="setup",
    )(inverses, lower, upper, basis)


def edges_kernel(count, left, right, partial, before, after, first, last):
    first[...] = (partial[0] + dot(left[0], before[...])).astype(BF16)
    last[...] = (partial[1] + dot(right[count - 1], after[...])).astype(BF16)


def edges(left, right, partial, before, after):
    count, size, _ = left.shape
    width = before.shape[-1]
    out = jax.ShapeDtypeStruct((size, width), BF16)
    return pl.pallas_call(
        functools.partial(edges_kernel, count),
        out_shape=(out, out),
        in_specs=[VM] * 5,
        out_specs=(VM, VM),
        compiler_params=params(),
        cost_estimate=cost(4 * size * size * width, 4 * size * size),
        name="edges",
    )(left, right, partial, before, after)


def sweep_kernel(count, left, right, start, first, middle, last, out, partial):
    advance(count, left, right, start, first[...], middle, last[...], out, partial)


def sweep(left, right, start, first, middle, last):
    count, size, _ = left.shape
    width = first.shape[-1]
    return pl.pallas_call(
        functools.partial(sweep_kernel, count),
        out_shape=(
            jax.ShapeDtypeStruct((count - 2, size, width), BF16),
            jax.ShapeDtypeStruct((2, size, width), F32),
        ),
        in_specs=[VM] * 6,
        out_specs=(VM, VM),
        compiler_params=params(),
        cost_estimate=cost(4 * count * size * size * width, 4 * count * size * size),
        name="sweep",
    )(left, right, start, first, middle, last)


def finish_kernel(count, size, weight, left, right, partial, before, after, middle, out):
    out[0, :size] = (partial[0] + dot(left[0], before[...])).astype(BF16)
    for b in range(1, count - 1):
        out[b, :size] = middle[b - 1]
    out[count - 1, :size] = (partial[1] + dot(right[count - 1], after[...])).astype(BF16)
    width = out.shape[-1]
    full = jnp.full((EXTRA, width), weight[0], F32)
    high = full.astype(BF16)
    rest = full - high.astype(F32)
    mid = rest.astype(BF16)
    low = (rest - mid.astype(F32)).astype(BF16)
    place = lax.broadcasted_iota(jnp.int32, (EXTRA, width), 0)
    rows = jnp.where(
        place == 0, high.astype(F32), jnp.where(place == 1, mid.astype(F32), low.astype(F32))
    ).astype(BF16)
    for b in range(count):
        out[b, size:] = rows


def finish(weight, left, right, partial, before, after, middle):
    count, size, _ = left.shape
    width = before.shape[-1]
    return pl.pallas_call(
        functools.partial(finish_kernel, count, size),
        out_shape=jax.ShapeDtypeStruct((count, size + EXTRA, width), BF16),
        in_specs=[SM] + [VM] * 6,
        out_specs=VM,
        compiler_params=params(),
        cost_estimate=cost(4 * size * size * width, 4 * size * size),
        name="finish",
    )(weight, left, right, partial, before, after, middle)


def gram_kernel(size, parts, received, filtered, gram):
    total = None
    for p in range(received.shape[0]):
        rows = received[p, size : size + 3].astype(F32)
        weight = rows[0:1] + rows[1:2] + rows[2:3]
        term = weight * received[p, :size].astype(F32)
        total = term if total is None else total + term
    filtered[...] = total
    value = lax.dot_general(
        total, total, (((0,), (0,)), ((), ())), precision=HI, preferred_element_type=F32
    )
    gram[...] = value.reshape(gram.shape)


def partial_gram(received, parts):
    poles, rows, width = received.shape
    size = rows - EXTRA
    return pl.pallas_call(
        functools.partial(gram_kernel, size, parts),
        out_shape=(
            jax.ShapeDtypeStruct((size, width), F32),
            jax.ShapeDtypeStruct((parts, width // parts, width), F32),
        ),
        in_specs=[VM],
        out_specs=(VM, VM),
        compiler_params=params(),
        name="gram",
    )(received)


def orthonormal_kernel(total_rows, gram, filtered, out, work):
    n = out.shape[-1]
    lanes = lax.broadcasted_iota(jnp.int32, (8, 2 * n), 1)
    subs = lax.broadcasted_iota(jnp.int32, (8, 2 * n), 0)
    work[:, :n] = gram[...].reshape(n, n) / total_rows
    work[:, n:] = (
        lax.broadcasted_iota(jnp.int32, (n, n), 0) == lax.broadcasted_iota(jnp.int32, (n, n), 1)
    ).astype(F32)
    for p in range(n // 8):
        rows = work[8 * p : 8 * p + 8, :]
        for j in range(8):
            column = rows[:, 8 * p + j : 8 * p + j + 1]
            scale = lax.rsqrt(column[j : j + 1])
            pivot = rows[j : j + 1] * scale
            rows = jnp.where(subs == j, pivot, jnp.where(subs > j, rows - (column * scale) * pivot, rows))
        work[8 * p : 8 * p + 8, :] = rows
        if 8 * p + 8 < n:
            change = lax.dot_general(
                rows[:, :n], rows, (((0,), (0,)), ((), ())), precision=HI, preferred_element_type=F32
            )
            work[8 * p + 8 :, :] = work[8 * p + 8 :, :] - change[8 * p + 8 :, :]
    out[...] = lax.dot_general(
        filtered[...], work[:, n:], (((1,), (1,)), ((), ())), precision=HI, preferred_element_type=F32
    )


def orthonormal(gram, filtered, total_rows):
    n = filtered.shape[-1]
    return pl.pallas_call(
        functools.partial(orthonormal_kernel, float(total_rows)),
        out_shape=jax.ShapeDtypeStruct(filtered.shape, F32),
        in_specs=[VM, VM],
        out_specs=VM,
        scratch_shapes=[pltpu.VMEM((n, 2 * n), F32)],
        compiler_params=params(),
        name="orthonormal",
    )(gram, filtered)


POLE = ("x_hi", "y")
ROW = ("x_lo", "z", "core")
PLANE = ("x_hi", "y", "x_lo")
LINE = ("z", "core")


def neighbours(first, last):
    peers = lax.axis_size(ROW)
    up = [(i, i + 1) for i in range(peers - 1)]
    down = [(j, i) for i, j in up]
    return lax.ppermute(last, ROW, up), lax.ppermute(first, ROW, down)


def exchange(value, axes):
    return lax.all_to_all(value, axes, split_axis=0, concat_axis=0, tiled=True)


def shards(basis, inverses, lower, upper, pole_weights):
    rows, width = basis.shape
    count = inverses.shape[1]
    size = inverses.shape[-1]
    first, last = first_edges(inverses, basis, count, size, width)
    before, after = neighbours(first, last)
    left, right, start, middle, partial = setup(inverses, lower, upper, basis, count, size, width)
    for _ in range(SWEEPS - 1):
        first, last = edges(left, right, partial, before, after)
        before, after = neighbours(first, last)
        middle, partial = sweep(left, right, start, first, middle, last)
    solved = finish(pole_weights, left, right, partial, before, after, middle)
    received = exchange(solved, POLE)
    plane = lax.axis_size(PLANE)
    filtered, gram = partial_gram(received, plane)
    gram = exchange(gram, PLANE).sum(0, keepdims=True)
    line = lax.axis_size(LINE)
    gram = exchange(jnp.broadcast_to(gram, (line, *gram.shape[1:])), LINE).sum(0, keepdims=True)
    gram = exchange(jnp.broadcast_to(gram, (plane, *gram.shape[1:])), PLANE)
    return orthonormal(gram, filtered, rows * lax.axis_size(ROW))


def solution(mesh):
    devices = mesh.devices.reshape(2, 4, 2, 8, 2)
    inner = Mesh(devices, ("x_hi", "y", "x_lo", "z", "core"))
    return jax.shard_map(
        shards,
        mesh=inner,
        in_specs=(
            P(ROW, None),
            P(POLE, ROW, None, None),
            P(ROW, None, None),
            P(ROW, None, None),
            P(POLE),
        ),
        out_specs=P(ROW + POLE, None),
        check_vma=False,
    )
```

```python
import functools

import jax
import jax.numpy as jnp
from jax import lax
from jax.experimental import pallas as pl
from jax.experimental.pallas import tpu as pltpu
from jax.sharding import Mesh, PartitionSpec as P

SWEEPS = 4
EXTRA = 16
F32 = jnp.float32
BF16 = jnp.bfloat16
HI = lax.Precision.HIGHEST
VM = pl.BlockSpec(memory_space=pltpu.VMEM)
HBM = pl.BlockSpec(memory_space=pltpu.HBM)
SM = pl.BlockSpec(memory_space=pltpu.SMEM)
LIMIT = 16 << 20


def dot(a, b):
    return jnp.dot(a, b, preferred_element_type=F32)


def in_hbm(value):
    return pltpu.with_memory_space_constraint(value, pltpu.HBM)


def params():
    return pltpu.CompilerParams(vmem_limit_bytes=LIMIT)


def cost(flops, moved):
    return pl.CostEstimate(flops=int(flops), bytes_accessed=int(moved), transcendentals=0)


def first_edges_kernel(count, inverses, basis, first, last, inverse, block, sem):
    size = first.shape[0]
    copies = []
    for slot, b in enumerate((0, count - 1)):
        copies.append(pltpu.make_async_copy(inverses.at[0, b], inverse.at[slot], sem.at[2 * slot]))
        copies.append(
            pltpu.make_async_copy(basis.at[pl.ds(b * size, size)], block.at[slot], sem.at[2 * slot + 1])
        )
    for copy in copies:
        copy.start()
    for slot, out in enumerate((first, last)):
        copies[2 * slot].wait()
        copies[2 * slot + 1].wait()
        out[...] = dot(inverse[slot], block[slot]).astype(BF16)


def first_edges(inverses, basis, count, size, width):
    out = jax.ShapeDtypeStruct((size, width), BF16)
    return pl.pallas_call(
        functools.partial(first_edges_kernel, count),
        out_shape=(out, out),
        in_specs=[HBM] * 2,
        out_specs=(VM, VM),
        scratch_shapes=[
            pltpu.VMEM((2, size, size), BF16),
            pltpu.VMEM((2, size, width), BF16),
            pltpu.SemaphoreType.DMA((4,)),
        ],
        compiler_params=params(),
        name="first_edges",
    )(in_hbm(inverses), in_hbm(basis))


def advance(count, left, right, start, first, middle, last, out, partial):
    def state(b):
        if b == 0:
            return first
        if b == count - 1:
            return last
        return middle[b - 1]

    for b in range(1, count - 1):
        value = start[b] + dot(left[b], state(b - 1)[...]) + dot(right[b], state(b + 1)[...])
        out[b - 1] = value.astype(BF16)
    partial[0] = start[0] + dot(right[0], state(1)[...])
    partial[1] = start[count - 1] + dot(left[count - 1], state(count - 2)[...])


def setup_kernel(
    count, inv, lower, upper, basis, left, right, start, middle, partial, held, below, above, sem
):
    size = inv.shape[-1]
    copies = []
    for b in range(count):
        copies.append(pltpu.make_async_copy(lower.at[b], below.at[b], sem.at[2 * b]))
        copies.append(pltpu.make_async_copy(upper.at[b], above.at[b], sem.at[2 * b + 1]))
    for copy in copies:
        copy.start()
    for b in range(count):
        value = dot(inv[0, b], basis[b * size : (b + 1) * size])
        start[b] = value
        held[b] = value.astype(BF16)
    for b in range(count):
        copies[2 * b].wait()
        left[b] = dot(inv[0, b], below[b]).astype(BF16)
        copies[2 * b + 1].wait()
        right[b] = dot(inv[0, b], above[b]).astype(BF16)
    advance(
        count, left, right, start, held.at[0],
        [held.at[i] for i in range(1, count - 1)], held.at[count - 1], middle, partial,
    )


def setup(inverses, lower, upper, basis, count, size, width):
    flops = 2 * count * size * size * (2 * size + 3 * width)
    return pl.pallas_call(
        functools.partial(setup_kernel, count),
        out_shape=(
            jax.ShapeDtypeStruct((count, size, size), BF16),
            jax.ShapeDtypeStruct((count, size, size), BF16),
            jax.ShapeDtypeStruct((count, size, width), F32),
            jax.ShapeDtypeStruct((count - 2, size, width), BF16),
            jax.ShapeDtypeStruct((2, size, width), F32),
        ),
        in_specs=[VM, HBM, HBM, VM],
        out_specs=(VM, VM, VM, VM, VM),
        scratch_shapes=[
            pltpu.VMEM((count, size, width), BF16),
            pltpu.VMEM((count, size, size), BF16),
            pltpu.VMEM((count, size, size), BF16),
            pltpu.SemaphoreType.DMA((2 * count,)),
        ],
        compiler_params=params(),
        cost_estimate=cost(flops, 6 * count * size * size),
        name="setup",
    )(inverses, in_hbm(lower), in_hbm(upper), basis)


def edges_kernel(count, left, right, partial, before, after, first, last):
    first[...] = (partial[0] + dot(left[0], before[...])).astype(BF16)
    last[...] = (partial[1] + dot(right[count - 1], after[...])).astype(BF16)


def edges(left, right, partial, before, after):
    count, size, _ = left.shape
    width = before.shape[-1]
    out = jax.ShapeDtypeStruct((size, width), BF16)
    return pl.pallas_call(
        functools.partial(edges_kernel, count),
        out_shape=(out, out),
        in_specs=[VM] * 5,
        out_specs=(VM, VM),
        compiler_params=params(),
        cost_estimate=cost(4 * size * size * width, 4 * size * size),
        name="edges",
    )(left, right, partial, before, after)


def sweep_kernel(count, left, right, start, first, middle, last, out, partial):
    middles = [middle.at[i] for i in range(count - 2)]
    advance(count, left, right, start, first, middles, last, out, partial)


def sweep(left, right, start, first, middle, last):
    count, size, _ = left.shape
    width = first.shape[-1]
    return pl.pallas_call(
        functools.partial(sweep_kernel, count),
        out_shape=(
            jax.ShapeDtypeStruct((count - 2, size, width), BF16),
            jax.ShapeDtypeStruct((2, size, width), F32),
        ),
        in_specs=[VM] * 6,
        out_specs=(VM, VM),
        compiler_params=params(),
        cost_estimate=cost(4 * count * size * size * width, 4 * count * size * size),
        name="sweep",
    )(left, right, start, first, middle, last)


def finish_kernel(count, size, weight, left, right, partial, before, after, middle, out):
    out[0, :size] = (partial[0] + dot(left[0], before[...])).astype(BF16)
    for b in range(1, count - 1):
        out[b, :size] = middle[b - 1]
    out[count - 1, :size] = (partial[1] + dot(right[count - 1], after[...])).astype(BF16)
    width = out.shape[-1]
    full = jnp.full((EXTRA, width), weight[0], F32)
    high = full.astype(BF16)
    rest = full - high.astype(F32)
    mid = rest.astype(BF16)
    low = (rest - mid.astype(F32)).astype(BF16)
    place = lax.broadcasted_iota(jnp.int32, (EXTRA, width), 0)
    rows = jnp.where(
        place == 0, high.astype(F32), jnp.where(place == 1, mid.astype(F32), low.astype(F32))
    ).astype(BF16)
    for b in range(count):
        out[b, size:] = rows


def finish(weight, left, right, partial, before, after, middle):
    count, size, _ = left.shape
    width = before.shape[-1]
    return pl.pallas_call(
        functools.partial(finish_kernel, count, size),
        out_shape=jax.ShapeDtypeStruct((count, size + EXTRA, width), BF16),
        in_specs=[SM] + [VM] * 6,
        out_specs=VM,
        compiler_params=params(),
        cost_estimate=cost(4 * size * size * width, 4 * size * size),
        name="finish",
    )(weight, left, right, partial, before, after, middle)


def gram_kernel(size, parts, received, filtered, gram):
    total = None
    for p in range(received.shape[0]):
        rows = received[p, size : size + 3].astype(F32)
        weight = rows[0:1] + rows[1:2] + rows[2:3]
        term = weight * received[p, :size].astype(F32)
        total = term if total is None else total + term
    filtered[...] = total
    value = lax.dot_general(
        total, total, (((0,), (0,)), ((), ())), precision=HI, preferred_element_type=F32
    )
    gram[...] = value.reshape(gram.shape)


def partial_gram(received, parts):
    poles, rows, width = received.shape
    size = rows - EXTRA
    return pl.pallas_call(
        functools.partial(gram_kernel, size, parts),
        out_shape=(
            jax.ShapeDtypeStruct((size, width), F32),
            jax.ShapeDtypeStruct((parts, width // parts, width), F32),
        ),
        in_specs=[VM],
        out_specs=(VM, VM),
        compiler_params=params(),
        name="gram",
    )(received)


def orthonormal_kernel(total_rows, gram, filtered, out, work):
    n = out.shape[-1]
    lanes = lax.broadcasted_iota(jnp.int32, (8, 2 * n), 1)
    subs = lax.broadcasted_iota(jnp.int32, (8, 2 * n), 0)
    work[:, :n] = gram[...].reshape(n, n) / total_rows
    work[:, n:] = (
        lax.broadcasted_iota(jnp.int32, (n, n), 0) == lax.broadcasted_iota(jnp.int32, (n, n), 1)
    ).astype(F32)
    for p in range(n // 8):
        rows = work[8 * p : 8 * p + 8, :]
        for j in range(8):
            column = rows[:, 8 * p + j : 8 * p + j + 1]
            scale = lax.rsqrt(column[j : j + 1])
            pivot = rows[j : j + 1] * scale
            rows = jnp.where(subs == j, pivot, jnp.where(subs > j, rows - (column * scale) * pivot, rows))
        work[8 * p : 8 * p + 8, :] = rows
        if 8 * p + 8 < n:
            change = lax.dot_general(
                rows[:, :n], rows, (((0,), (0,)), ((), ())), precision=HI, preferred_element_type=F32
            )
            work[8 * p + 8 :, :] = work[8 * p + 8 :, :] - change[8 * p + 8 :, :]
    out[...] = lax.dot_general(
        filtered[...], work[:, n:], (((1,), (1,)), ((), ())), precision=HI, preferred_element_type=F32
    )


def orthonormal(gram, filtered, total_rows):
    n = filtered.shape[-1]
    return pl.pallas_call(
        functools.partial(orthonormal_kernel, float(total_rows)),
        out_shape=jax.ShapeDtypeStruct(filtered.shape, F32),
        in_specs=[VM, VM],
        out_specs=VM,
        scratch_shapes=[pltpu.VMEM((n, 2 * n), F32)],
        compiler_params=params(),
        name="orthonormal",
    )(gram, filtered)


POLE = ("x_hi", "y")
ROW = ("x_lo", "z", "core")
PLANE = ("x_hi", "y", "x_lo")
LINE = ("z", "core")


def neighbours(first, last):
    peers = lax.axis_size(ROW)
    up = [(i, i + 1) for i in range(peers - 1)]
    down = [(j, i) for i, j in up]
    return lax.ppermute(last, ROW, up), lax.ppermute(first, ROW, down)


def exchange(value, axes):
    return lax.all_to_all(value, axes, split_axis=0, concat_axis=0, tiled=True)


def shards(basis, inverses, lower, upper, pole_weights):
    rows, width = basis.shape
    count = inverses.shape[1]
    size = inverses.shape[-1]
    first, last = first_edges(inverses, basis, count, size, width)
    before, after = neighbours(first, last)
    left, right, start, middle, partial = setup(inverses, lower, upper, basis, count, size, width)
    for _ in range(SWEEPS - 1):
        first, last = edges(left, right, partial, before, after)
        before, after = neighbours(first, last)
        middle, partial = sweep(left, right, start, first, middle, last)
    solved = finish(pole_weights, left, right, partial, before, after, middle)
    received = exchange(solved, POLE)
    plane = lax.axis_size(PLANE)
    filtered, gram = partial_gram(received, plane)
    gram = exchange(gram, PLANE).sum(0, keepdims=True)
    line = lax.axis_size(LINE)
    gram = exchange(jnp.broadcast_to(gram, (line, *gram.shape[1:])), LINE).sum(0, keepdims=True)
    gram = exchange(jnp.broadcast_to(gram, (plane, *gram.shape[1:])), PLANE)
    return orthonormal(gram, filtered, rows * lax.axis_size(ROW))


def solution(mesh):
    devices = mesh.devices.reshape(2, 4, 2, 8, 2)
    inner = Mesh(devices, ("x_hi", "y", "x_lo", "z", "core"))
    return jax.shard_map(
        shards,
        mesh=inner,
        in_specs=(
            P(ROW, None),
            P(POLE, ROW, None, None),
            P(ROW, None, None),
            P(ROW, None, None),
            P(POLE),
        ),
        out_specs=P(ROW + POLE, None),
        check_vma=False,
    )
```

```python
import functools

import jax
import jax.numpy as jnp
from jax import lax
from jax.experimental import pallas as pl
from jax.experimental.pallas import tpu as pltpu
from jax.sharding import Mesh, PartitionSpec as P

SWEEPS = 4
EXTRA = 16
F32 = jnp.float32
BF16 = jnp.bfloat16
HI = lax.Precision.HIGHEST
VM = pl.BlockSpec(memory_space=pltpu.VMEM)
HBM = pl.BlockSpec(memory_space=pltpu.HBM)
SM = pl.BlockSpec(memory_space=pltpu.SMEM)
LIMIT = 16 << 20


def dot(a, b):
    return jnp.dot(a, b, preferred_element_type=F32)


def in_hbm(value):
    return pltpu.with_memory_space_constraint(value, pltpu.HBM)


def params():
    return pltpu.CompilerParams(vmem_limit_bytes=LIMIT)


def cost(flops, moved):
    return pl.CostEstimate(flops=int(flops), bytes_accessed=int(moved), transcendentals=0)


class Side:
    def __init__(self, low, count):
        self.low = low
        self.edge = 0 if low else count - 1
        self.inner = 1 if low else count - 2

    def outward(self, lower, upper):
        return lower if self.low else upper

    def inward(self, lower, upper):
        return upper if self.low else lower


def sides(count):
    return Side(True, count), Side(False, count)


def rounded(value):
    return value.astype(BF16)


def first_edges_kernel(
    count, inverses, lower, upper, basis, low, high, local, inv, outward, inward, block, sem
):
    size, width = block.shape[-2:]
    copies = []
    for k, side in enumerate(sides(count)):
        group = []
        for j, b in enumerate((side.edge, side.inner)):
            group.append((inverses.at[0, b], inv.at[k, j]))
            group.append((basis.at[pl.ds(b * size, size)], block.at[k, j]))
        group.append((side.outward(lower, upper).at[side.edge], outward.at[k]))
        group.append((side.inward(lower, upper).at[side.edge], inward.at[k]))
        copies.append(
            [pltpu.make_async_copy(a, b, sem.at[6 * k + i]) for i, (a, b) in enumerate(group)]
        )
    for copy in copies[0] + copies[1]:
        copy.start()
    for k, out in enumerate((low, high)):
        for copy in copies[k]:
            copy.wait()
        out[:, :width] = rounded(dot(inv[k, 0], block[k, 0]))
        inner = rounded(dot(inv[k, 1], block[k, 1]))
        out[:, 2 * width :] = rounded(dot(inv[k, 0], outward[k]))
        rhs = block[k, 0].astype(F32) + dot(inward[k], inner)
        value = dot(inv[k, 0], rounded(rhs))
        out[:, width : 2 * width] = rounded(value)
        local[k] = value


def first_edges(inverses, lower, upper, basis, count, size, width):
    out = jax.ShapeDtypeStruct((size, 2 * width + size), BF16)
    return pl.pallas_call(
        functools.partial(first_edges_kernel, count),
        out_shape=(out, out, jax.ShapeDtypeStruct((2, size, width), F32)),
        in_specs=[HBM] * 4,
        out_specs=(VM, VM, VM),
        scratch_shapes=[
            pltpu.VMEM((2, 2, size, size), BF16),
            pltpu.VMEM((2, size, size), BF16),
            pltpu.VMEM((2, size, size), BF16),
            pltpu.VMEM((2, 2, size, width), BF16),
            pltpu.SemaphoreType.DMA((12,)),
        ],
        compiler_params=params(),
        name="first_edges",
    )(in_hbm(inverses), in_hbm(lower), in_hbm(upper), in_hbm(basis))


def right_side(basis, b, size):
    return basis[b * size : (b + 1) * size].astype(F32)


def two_sweeps(count, size, inv, lower, upper, basis, state, held, middle, known):
    for b in range(1, count - 1):
        rhs = right_side(basis, b, size) + dot(lower[b], state(b - 1)) + dot(upper[b], state(b + 1))
        held[b] = rounded(dot(inv[0, b], rounded(rhs)))
    for k, side in enumerate(sides(count)):
        step = 1 if side.low else -1
        for j, b in enumerate((side.edge, side.inner)):
            known[2 * k + j] = right_side(basis, b, size) + dot(
                side.inward(lower, upper)[b], held[b + step]
            )
    for b in range(2, count - 2):
        rhs = right_side(basis, b, size) + dot(lower[b], held[b - 1]) + dot(upper[b], held[b + 1])
        middle[b - 2] = rounded(dot(inv[0, b], rounded(rhs)))


def first_pair_kernel(
    count, inv, lower, upper, basis, low, high, below, above, middle, known, start, held, sem
):
    size, width = start.shape[1:]
    copies = []
    for b in range(count):
        copies.append(pltpu.make_async_copy(lower.at[b], below.at[b], sem.at[2 * b]))
        copies.append(pltpu.make_async_copy(upper.at[b], above.at[b], sem.at[2 * b + 1]))
    for copy in copies:
        copy.start()
    start[0] = low[:, :width]
    start[count - 1] = high[:, :width]
    for b in range(1, count - 1):
        start[b] = rounded(dot(inv[0, b], basis[b * size : (b + 1) * size]))
    for copy in copies:
        copy.wait()
    two_sweeps(count, size, inv, below, above, basis, lambda b: start[b], held, middle, known)


def pair_cost(count, size, width):
    return cost(12 * (count - 2) * size * size * width, 6 * count * size * size)


def first_pair(inverses, lower, upper, basis, low, high, count, size, width):
    couplings = jax.ShapeDtypeStruct((count, size, size), BF16)
    return pl.pallas_call(
        functools.partial(first_pair_kernel, count),
        out_shape=(
            couplings,
            couplings,
            jax.ShapeDtypeStruct((count - 4, size, width), BF16),
            jax.ShapeDtypeStruct((4, size, width), F32),
        ),
        in_specs=[VM, HBM, HBM, VM, VM, VM],
        out_specs=(VM, VM, VM, VM),
        scratch_shapes=[
            pltpu.VMEM((count, size, width), BF16),
            pltpu.VMEM((count, size, width), BF16),
            pltpu.SemaphoreType.DMA((2 * count,)),
        ],
        compiler_params=params(),
        cost_estimate=pair_cost(count, size, width),
        name="first_pair",
    )(inverses, in_hbm(lower), in_hbm(upper), basis, low, high)


def pair_kernel(count, inv, lower, upper, basis, low, high, inner, previous, middle, known, held):
    size, width = held.shape[1:]

    def state(b):
        if b == 0:
            return low[:, :width]
        if b == count - 1:
            return high[:, :width]
        if b == 1:
            return inner[0]
        if b == count - 2:
            return inner[1]
        return previous[b - 2]

    two_sweeps(count, size, inv, lower, upper, basis, state, held, middle, known)


def pair(inverses, lower, upper, basis, low, high, inner, previous):
    count, size, _ = lower.shape
    width = basis.shape[-1]
    return pl.pallas_call(
        functools.partial(pair_kernel, count),
        out_shape=(
            jax.ShapeDtypeStruct((count - 4, size, width), BF16),
            jax.ShapeDtypeStruct((4, size, width), F32),
        ),
        in_specs=[VM] * 8,
        out_specs=(VM, VM),
        scratch_shapes=[pltpu.VMEM((count, size, width), BF16)],
        compiler_params=params(),
        cost_estimate=pair_cost(count, size, width),
        name="pair",
    )(inverses, lower, upper, basis, low, high, inner, previous)


def absorbed(k, side, inv, lower, upper, known, joint, halo_joint, own, halo, local):
    width = known.shape[-1]
    halo_next = rounded(
        halo[:, width : 2 * width].astype(F32) + dot(halo_joint[:, 2 * width :], own[:, :width])
    )
    edge_next = rounded(local[k] + dot(joint[:, 2 * width :], halo[:, :width]))
    out = []
    for j, (b, value) in enumerate(((side.edge, halo_next), (side.inner, edge_next))):
        rhs = known[2 * k + j] + dot(side.outward(lower, upper)[b], value)
        out.append(rounded(dot(inv[0, b], rounded(rhs))))
    return out


def meet_kernel(
    count, inv, lower, upper, basis, known, low, high, local, before, after,
    low_out, high_out, local_out, inner_out,
):
    size, width = known.shape[1:]
    pieces = ((low, before, low_out), (high, after, high_out))
    for k, (side, (own, halo, out)) in enumerate(zip(sides(count), pieces)):
        edge, inner = absorbed(k, side, inv, lower, upper, known, own, halo, own, halo, local)
        rhs = right_side(basis, side.edge, size) + dot(
            side.inward(lower, upper)[side.edge], inner
        )
        value = dot(inv[0, side.edge], rounded(rhs))
        out[:, :width] = edge
        out[:, width:] = rounded(value)
        local_out[k] = value
        inner_out[k] = inner


def meet(inverses, lower, upper, basis, known, low, high, local, before, after):
    count, size, _ = lower.shape
    width = basis.shape[-1]
    out = jax.ShapeDtypeStruct((size, 2 * width), BF16)
    return pl.pallas_call(
        functools.partial(meet_kernel, count),
        out_shape=(
            out,
            out,
            jax.ShapeDtypeStruct((2, size, width), F32),
            jax.ShapeDtypeStruct((2, size, width), BF16),
        ),
        in_specs=[VM] * 10,
        out_specs=(VM, VM, VM, VM),
        compiler_params=params(),
        cost_estimate=cost(32 * size * size * width, 24 * size * size),
        name="meet",
    )(inverses, lower, upper, basis, known, low, high, local, before, after)


def finish_kernel(
    count, weight, inv, lower, upper, known, middle, low_joint, high_joint, before_joint,
    after_joint, low, high, local, before, after, out,
):
    size, width = known.shape[1:]
    pieces = (
        (low_joint, before_joint, low, before),
        (high_joint, after_joint, high, after),
    )
    for k, (side, parts) in enumerate(zip(sides(count), pieces)):
        edge, inner = absorbed(k, side, inv, lower, upper, known, *parts, local)
        out[side.edge, :size] = edge
        out[side.inner, :size] = inner
    for b in range(2, count - 2):
        out[b, :size] = middle[b - 2]
    full = jnp.full((EXTRA, width), weight[0], F32)
    high_part = rounded(full)
    rest = full - high_part.astype(F32)
    mid_part = rounded(rest)
    low_part = rounded(rest - mid_part.astype(F32))
    place = lax.broadcasted_iota(jnp.int32, (EXTRA, width), 0)
    rows = jnp.where(
        place == 0,
        high_part.astype(F32),
        jnp.where(place == 1, mid_part.astype(F32), low_part.astype(F32)),
    )
    for b in range(count):
        out[b, size:] = rounded(rows)


def finish(weight, inverses, lower, upper, known, middle, *pieces):
    count, size, _ = lower.shape
    width = known.shape[-1]
    return pl.pallas_call(
        functools.partial(finish_kernel, count),
        out_shape=jax.ShapeDtypeStruct((count, size + EXTRA, width), BF16),
        in_specs=[SM] + [VM] * (5 + len(pieces)),
        out_specs=VM,
        compiler_params=params(),
        cost_estimate=cost(24 * size * size * width, 24 * size * size),
        name="finish",
    )(weight, inverses, lower, upper, known, middle, *pieces)


def gram_kernel(size, parts, received, filtered, gram):
    total = None
    for p in range(received.shape[0]):
        rows = received[p, size : size + 3].astype(F32)
        weight = rows[0:1] + rows[1:2] + rows[2:3]
        term = weight * received[p, :size].astype(F32)
        total = term if total is None else total + term
    filtered[...] = total
    value = lax.dot_general(
        total, total, (((0,), (0,)), ((), ())), precision=HI, preferred_element_type=F32
    )
    gram[...] = value.reshape(gram.shape)


def partial_gram(received, parts):
    poles, rows, width = received.shape
    size = rows - EXTRA
    return pl.pallas_call(
        functools.partial(gram_kernel, size, parts),
        out_shape=(
            jax.ShapeDtypeStruct((size, width), F32),
            jax.ShapeDtypeStruct((parts, width // parts, width), F32),
        ),
        in_specs=[VM],
        out_specs=(VM, VM),
        compiler_params=params(),
        name="gram",
    )(received)


def eliminate(value, work, inverse):
    n = value.shape[-1]
    subs = lax.broadcasted_iota(jnp.int32, (8, 2 * n), 0)
    work[:, :n] = value
    work[:, n:] = (
        lax.broadcasted_iota(jnp.int32, (n, n), 0) == lax.broadcasted_iota(jnp.int32, (n, n), 1)
    ).astype(F32)
    for p in range(n // 8):
        rows = work[8 * p : 8 * p + 8, :]
        for j in range(8):
            column = rows[:, 8 * p + j : 8 * p + j + 1]
            scale = lax.rsqrt(column[j : j + 1])
            pivot = rows[j : j + 1] * scale
            rows = jnp.where(
                subs == j, pivot, jnp.where(subs > j, rows - (column * scale) * pivot, rows)
            )
        work[8 * p : 8 * p + 8, :] = rows
        if 8 * p + 8 < n:
            change = lax.dot_general(
                rows[:, :n], rows, (((0,), (0,)), ((), ())), precision=HI, preferred_element_type=F32
            )
            work[8 * p + 8 :, :] = work[8 * p + 8 :, :] - change[8 * p + 8 :, :]
    inverse[...] = work[:, n:]


def orthonormal_kernel(total_rows, gram, filtered, out, work, inverse):
    n = out.shape[-1]
    value = gram[...].reshape(n, n) / total_rows
    rows = lax.broadcasted_iota(jnp.int32, (n, n), 0)
    cols = lax.broadcasted_iota(jnp.int32, (n, n), 1)
    same = rows == cols

    def phi(x):
        return jnp.where(rows > cols, x, jnp.where(same, 0.5 * x, 0.0))

    def exact(a, b):
        return jnp.dot(a, b, precision=HI, preferred_element_type=F32)

    def short(a, b):
        return dot(rounded(a), rounded(b))

    diagonal = jnp.where(same, value, 0.0)
    across = lax.rsqrt(jnp.sum(diagonal, axis=0, keepdims=True))
    down = lax.rsqrt(jnp.sum(diagonal, axis=1, keepdims=True))
    excess = jnp.where(same, 0.0, value * across * down)
    first = jnp.where(rows > cols, excess, 0.0)
    first_t = excess - first
    product = exact(first, excess)
    second_excess = -product - exact(first_t - product, first_t)
    second = phi(second_excess)
    second_t = second_excess - second
    product = short(second, second_excess)
    third_excess = -product - short(second_t - product, second_t)
    third = phi(third_excess)
    factor = exact(second, first) - first - second
    factor = jnp.where(same, 1.0 + factor, factor)
    factor = factor - short(third, factor)
    inverse[...] = factor * across
    error = jnp.sum(third_excess * third_excess)

    @pl.when(jnp.logical_not(error < 1e-7))
    def _():
        eliminate(value, work, inverse)

    out[...] = lax.dot_general(
        filtered[...], inverse[...], (((1,), (1,)), ((), ())), precision=HI, preferred_element_type=F32
    )


def orthonormal(gram, filtered, total_rows):
    n = filtered.shape[-1]
    return pl.pallas_call(
        functools.partial(orthonormal_kernel, float(total_rows)),
        out_shape=jax.ShapeDtypeStruct(filtered.shape, F32),
        in_specs=[VM, VM],
        out_specs=VM,
        scratch_shapes=[pltpu.VMEM((n, 2 * n), F32), pltpu.VMEM((n, n), F32)],
        compiler_params=params(),
        name="orthonormal",
    )(gram, filtered)


POLE = ("x_hi", "y")
ROW = ("x_lo", "z", "core")
PLANE = ("x_hi", "y", "x_lo")
LINE = ("z", "core")


def neighbours(first, last):
    peers = lax.axis_size(ROW)
    up = [(i, i + 1) for i in range(peers - 1)]
    down = [(j, i) for i, j in up]
    return lax.ppermute(last, ROW, up), lax.ppermute(first, ROW, down)


def exchange(value, axes):
    return lax.all_to_all(value, axes, split_axis=0, concat_axis=0, tiled=True)


def shards(basis, inverses, lower, upper, pole_weights):
    rows, width = basis.shape
    count = inverses.shape[1]
    size = inverses.shape[-1]
    low, high, local = first_edges(inverses, lower, upper, basis, count, size, width)
    joints = (low, high)
    before, after = halo_joints = neighbours(low, high)
    lower, upper, middle, known = first_pair(
        inverses, lower, upper, basis, low, high, count, size, width
    )
    for _ in range(SWEEPS // 2 - 1):
        low, high, local, inner = meet(
            inverses, lower, upper, basis, known, low, high, local, before, after
        )
        before, after = neighbours(low, high)
        middle, known = pair(inverses, lower, upper, basis, low, high, inner, middle)
    solved = finish(
        pole_weights, inverses, lower, upper, known, middle, *joints, *halo_joints,
        low, high, local, before, after,
    )
    received = exchange(solved, POLE)
    plane = lax.axis_size(PLANE)
    filtered, gram = partial_gram(received, plane)
    gram = exchange(gram, PLANE).sum(0, keepdims=True)
    line = lax.axis_size(LINE)
    gram = exchange(jnp.broadcast_to(gram, (line, *gram.shape[1:])), LINE).sum(0, keepdims=True)
    gram = exchange(jnp.broadcast_to(gram, (plane, *gram.shape[1:])), PLANE)
    return orthonormal(gram, filtered, rows * lax.axis_size(ROW))


def solution(mesh):
    devices = mesh.devices.reshape(2, 4, 2, 8, 2)
    inner = Mesh(devices, ("x_hi", "y", "x_lo", "z", "core"))
    return jax.shard_map(
        shards,
        mesh=inner,
        in_specs=(
            P(ROW, None),
            P(POLE, ROW, None, None),
            P(ROW, None, None),
            P(ROW, None, None),
            P(POLE),
        ),
        out_specs=P(ROW + POLE, None),
        check_vma=False,
    )
```

```python
import functools

import jax
import jax.numpy as jnp
from jax import lax
from jax.experimental import pallas as pl
from jax.experimental.pallas import tpu as pltpu
from jax.sharding import Mesh, PartitionSpec as P

SWEEPS = 4
EXTRA = 16
F32 = jnp.float32
BF16 = jnp.bfloat16
HI = lax.Precision.HIGHEST
VM = pl.BlockSpec(memory_space=pltpu.VMEM)
HBM = pl.BlockSpec(memory_space=pltpu.HBM)
SM = pl.BlockSpec(memory_space=pltpu.SMEM)
LIMIT = 16 << 20


def dot(a, b):
    return jnp.dot(a, b, preferred_element_type=F32)


def in_hbm(value):
    return pltpu.with_memory_space_constraint(value, pltpu.HBM)


def params():
    return pltpu.CompilerParams(vmem_limit_bytes=LIMIT)


def cost(flops, moved):
    return pl.CostEstimate(flops=int(flops), bytes_accessed=int(moved), transcendentals=0)


class Side:
    def __init__(self, low, count):
        self.low = low
        self.edge = 0 if low else count - 1
        self.inner = 1 if low else count - 2

    def outward(self, lower, upper):
        return lower if self.low else upper

    def inward(self, lower, upper):
        return upper if self.low else lower


def sides(count):
    return Side(True, count), Side(False, count)


def rounded(value):
    return value.astype(BF16)


def first_edges_kernel(
    count, inverses, lower, upper, basis, low, high, local, inv, outward, inward, block, sem
):
    size, width = block.shape[-2:]
    both = list(enumerate(sides(count)))
    outs = (low, high)
    copies = {}

    def begin(name, k, source, target):
        copies[name, k] = pltpu.make_async_copy(source, target, sem.at[len(copies)])
        copies[name, k].start()

    for j in range(2):
        for k, side in both:
            b = side.inner if j else side.edge
            begin(("basis", j), k, basis.at[pl.ds(b * size, size)], block.at[k, j])
            begin(("inverse", j), k, inverses.at[0, b], inv.at[k, j])
    for k, side in both:
        begin("inward", k, side.inward(lower, upper).at[side.edge], inward.at[k])
    for k, side in both:
        begin("outward", k, side.outward(lower, upper).at[side.edge], outward.at[k])
    inner = []
    for j in range(2):
        for k, side in both:
            copies[("basis", j), k].wait()
            copies[("inverse", j), k].wait()
            value = rounded(dot(inv[k, j], block[k, j]))
            if j:
                inner.append(value)
            else:
                outs[k][:, :width] = value
    rhs = []
    for k, side in both:
        copies["inward", k].wait()
        rhs.append(rounded(block[k, 0].astype(F32) + dot(inward[k], inner[k])))
    for k, side in both:
        copies["outward", k].wait()
        outs[k][:, 2 * width :] = rounded(dot(inv[k, 0], outward[k]))
    for k, side in both:
        value = dot(inv[k, 0], rhs[k])
        outs[k][:, width : 2 * width] = rounded(value)
        local[k] = value


def first_edges(inverses, lower, upper, basis, count, size, width):
    out = jax.ShapeDtypeStruct((size, 2 * width + size), BF16)
    return pl.pallas_call(
        functools.partial(first_edges_kernel, count),
        out_shape=(out, out, jax.ShapeDtypeStruct((2, size, width), F32)),
        in_specs=[HBM] * 4,
        out_specs=(VM, VM, VM),
        scratch_shapes=[
            pltpu.VMEM((2, 2, size, size), BF16),
            pltpu.VMEM((2, size, size), BF16),
            pltpu.VMEM((2, size, size), BF16),
            pltpu.VMEM((2, 2, size, width), BF16),
            pltpu.SemaphoreType.DMA((12,)),
        ],
        compiler_params=params(),
        name="first_edges",
    )(in_hbm(inverses), in_hbm(lower), in_hbm(upper), in_hbm(basis))


def right_side(basis, b, size):
    return basis[b * size : (b + 1) * size].astype(F32)


def two_sweeps(count, size, inv, lower, upper, basis, state, held, rhs, middle, known):
    for b in range(1, count - 1):
        value = right_side(basis, b, size) + dot(lower[b], state(b - 1)) + dot(upper[b], state(b + 1))
        rhs[b] = rounded(value)
    for b in range(1, count - 1):
        held[b] = rounded(dot(inv[0, b], rhs[b]))
    for b in range(2, count - 2):
        value = right_side(basis, b, size) + dot(lower[b], held[b - 1]) + dot(upper[b], held[b + 1])
        rhs[b] = rounded(value)
    for k, side in enumerate(sides(count)):
        step = 1 if side.low else -1
        for j, b in enumerate((side.edge, side.inner)):
            known[2 * k + j] = right_side(basis, b, size) + dot(
                side.inward(lower, upper)[b], held[b + step]
            )
    for b in range(2, count - 2):
        middle[b - 2] = rounded(dot(inv[0, b], rhs[b]))


def first_pair_kernel(
    count, inverses, lower, upper, basis, low, high, inv, below, above, base, middle, known,
    start, held, rhs, sem,
):
    size, width = start.shape[1:]
    blocks = [slice(b * size, (b + 1) * size) for b in range(count)]
    loads = [
        pltpu.make_async_copy(inverses.at[0, b], inv.at[0, b], sem.at[b]) for b in range(count)
    ]
    base_load = pltpu.make_async_copy(basis, base, sem.at[3 * count])
    couplings = []
    for b in range(count):
        couplings.append(pltpu.make_async_copy(lower.at[b], below.at[b], sem.at[count + 2 * b]))
        couplings.append(pltpu.make_async_copy(upper.at[b], above.at[b], sem.at[count + 2 * b + 1]))
    base_load.start()
    for copy in loads + couplings:
        copy.start()
    start[0] = low[:, :width]
    start[count - 1] = high[:, :width]
    base_load.wait()
    for b in range(count):
        loads[b].wait()
        if 0 < b < count - 1:
            start[b] = rounded(dot(inv[0, b], base[blocks[b]]))
    for copy in couplings:
        copy.wait()
    two_sweeps(count, size, inv, below, above, base, lambda b: start[b], held, rhs, middle, known)


def pair_cost(count, size, width):
    return cost(12 * (count - 2) * size * size * width, 6 * count * size * size)


def first_pair(inverses, lower, upper, basis, low, high, count, size, width):
    couplings = jax.ShapeDtypeStruct((count, size, size), BF16)
    return pl.pallas_call(
        functools.partial(first_pair_kernel, count),
        out_shape=(
            jax.ShapeDtypeStruct(inverses.shape, BF16),
            couplings,
            couplings,
            jax.ShapeDtypeStruct(basis.shape, BF16),
            jax.ShapeDtypeStruct((count - 4, size, width), BF16),
            jax.ShapeDtypeStruct((4, size, width), F32),
        ),
        in_specs=[HBM, HBM, HBM, HBM, VM, VM],
        out_specs=(VM,) * 6,
        scratch_shapes=[
            pltpu.VMEM((count, size, width), BF16),
            pltpu.VMEM((count, size, width), BF16),
            pltpu.VMEM((count, size, width), BF16),
            pltpu.SemaphoreType.DMA((3 * count + 1,)),
        ],
        compiler_params=params(),
        cost_estimate=pair_cost(count, size, width),
        name="first_pair",
    )(in_hbm(inverses), in_hbm(lower), in_hbm(upper), in_hbm(basis), low, high)


def pair_kernel(count, inv, lower, upper, basis, low, high, inner, previous, middle, known, held, rhs):
    size, width = held.shape[1:]

    def state(b):
        if b == 0:
            return low[:, :width]
        if b == count - 1:
            return high[:, :width]
        if b == 1:
            return inner[0]
        if b == count - 2:
            return inner[1]
        return previous[b - 2]

    two_sweeps(count, size, inv, lower, upper, basis, state, held, rhs, middle, known)


def pair(inverses, lower, upper, basis, low, high, inner, previous):
    count, size, _ = lower.shape
    width = basis.shape[-1]
    return pl.pallas_call(
        functools.partial(pair_kernel, count),
        out_shape=(
            jax.ShapeDtypeStruct((count - 4, size, width), BF16),
            jax.ShapeDtypeStruct((4, size, width), F32),
        ),
        in_specs=[VM] * 8,
        out_specs=(VM, VM),
        scratch_shapes=[pltpu.VMEM((count, size, width), BF16)] * 2,
        compiler_params=params(),
        cost_estimate=pair_cost(count, size, width),
        name="pair",
    )(inverses, lower, upper, basis, low, high, inner, previous)


def absorbed(count, inv, lower, upper, known, pieces, local):
    width = known.shape[-1]
    both = list(enumerate(sides(count)))
    values = []
    for k, side in both:
        joint, halo_joint, own, halo = pieces[k]
        halo_next = halo[:, width : 2 * width].astype(F32) + dot(
            halo_joint[:, 2 * width :], own[:, :width]
        )
        edge_next = local[k] + dot(joint[:, 2 * width :], halo[:, :width])
        values.append((rounded(halo_next), rounded(edge_next)))
    rhs = []
    for j in (1, 0):
        for k, side in both:
            b = side.inner if j else side.edge
            value = known[2 * k + j] + dot(side.outward(lower, upper)[b], values[k][j])
            rhs.append((b, rounded(value)))
    inner_low, inner_high, edge_low, edge_high = [rounded(dot(inv[0, b], value)) for b, value in rhs]
    return (edge_low, edge_high), (inner_low, inner_high)


def meet_kernel(
    count, inv, lower, upper, basis, known, low, high, local, before, after,
    low_out, high_out, local_out, inner_out,
):
    size, width = known.shape[1:]
    pieces = ((low, before, low, before), (high, after, high, after))
    edge, inner = absorbed(count, inv, lower, upper, known, pieces, local)
    both = list(enumerate(sides(count)))
    outs = (low_out, high_out)
    rhs = []
    for k, side in both:
        value = right_side(basis, side.edge, size) + dot(
            side.inward(lower, upper)[side.edge], inner[k]
        )
        rhs.append(rounded(value))
        outs[k][:, :width] = edge[k]
        inner_out[k] = inner[k]
    for k, side in both:
        value = dot(inv[0, side.edge], rhs[k])
        outs[k][:, width:] = rounded(value)
        local_out[k] = value


def meet(inverses, lower, upper, basis, known, low, high, local, before, after):
    count, size, _ = lower.shape
    width = basis.shape[-1]
    out = jax.ShapeDtypeStruct((size, 2 * width), BF16)
    return pl.pallas_call(
        functools.partial(meet_kernel, count),
        out_shape=(
            out,
            out,
            jax.ShapeDtypeStruct((2, size, width), F32),
            jax.ShapeDtypeStruct((2, size, width), BF16),
        ),
        in_specs=[VM] * 10,
        out_specs=(VM, VM, VM, VM),
        compiler_params=params(),
        cost_estimate=cost(32 * size * size * width, 24 * size * size),
        name="meet",
    )(inverses, lower, upper, basis, known, low, high, local, before, after)


def finish_kernel(
    count, weight, inv, lower, upper, known, middle, low_joint, high_joint, before_joint,
    after_joint, low, high, local, before, after, out,
):
    size, width = known.shape[1:]
    pieces = (
        (low_joint, before_joint, low, before),
        (high_joint, after_joint, high, after),
    )
    edge, inner = absorbed(count, inv, lower, upper, known, pieces, local)
    for k, side in enumerate(sides(count)):
        out[side.edge, :size] = edge[k]
        out[side.inner, :size] = inner[k]
    for b in range(2, count - 2):
        out[b, :size] = middle[b - 2]
    full = jnp.full((EXTRA, width), weight[0], F32)
    high_part = rounded(full)
    rest = full - high_part.astype(F32)
    mid_part = rounded(rest)
    low_part = rounded(rest - mid_part.astype(F32))
    place = lax.broadcasted_iota(jnp.int32, (EXTRA, width), 0)
    rows = jnp.where(
        place == 0,
        high_part.astype(F32),
        jnp.where(place == 1, mid_part.astype(F32), low_part.astype(F32)),
    )
    for b in range(count):
        out[b, size:] = rounded(rows)


def finish(weight, inverses, lower, upper, known, middle, *pieces):
    count, size, _ = lower.shape
    width = known.shape[-1]
    return pl.pallas_call(
        functools.partial(finish_kernel, count),
        out_shape=jax.ShapeDtypeStruct((count, size + EXTRA, width), BF16),
        in_specs=[SM] + [VM] * (5 + len(pieces)),
        out_specs=VM,
        compiler_params=params(),
        cost_estimate=cost(24 * size * size * width, 24 * size * size),
        name="finish",
    )(weight, inverses, lower, upper, known, middle, *pieces)


def gram_kernel(size, parts, received, filtered, gram):
    total = None
    for p in range(received.shape[0]):
        rows = received[p, size : size + 3].astype(F32)
        weight = rows[0:1] + rows[1:2] + rows[2:3]
        term = weight * received[p, :size].astype(F32)
        total = term if total is None else total + term
    filtered[...] = total
    value = lax.dot_general(
        total, total, (((0,), (0,)), ((), ())), precision=HI, preferred_element_type=F32
    )
    gram[...] = value.reshape(gram.shape)


def partial_gram(received, parts):
    poles, rows, width = received.shape
    size = rows - EXTRA
    return pl.pallas_call(
        functools.partial(gram_kernel, size, parts),
        out_shape=(
            jax.ShapeDtypeStruct((size, width), F32),
            jax.ShapeDtypeStruct((parts, width // parts, width), F32),
        ),
        in_specs=[VM],
        out_specs=(VM, VM),
        compiler_params=params(),
        name="gram",
    )(received)


def eliminate(value, work, inverse):
    n = value.shape[-1]
    subs = lax.broadcasted_iota(jnp.int32, (8, 2 * n), 0)
    work[:, :n] = value
    work[:, n:] = (
        lax.broadcasted_iota(jnp.int32, (n, n), 0) == lax.broadcasted_iota(jnp.int32, (n, n), 1)
    ).astype(F32)
    for p in range(n // 8):
        rows = work[8 * p : 8 * p + 8, :]
        for j in range(8):
            column = rows[:, 8 * p + j : 8 * p + j + 1]
            scale = lax.rsqrt(column[j : j + 1])
            pivot = rows[j : j + 1] * scale
            rows = jnp.where(
                subs == j, pivot, jnp.where(subs > j, rows - (column * scale) * pivot, rows)
            )
        work[8 * p : 8 * p + 8, :] = rows
        if 8 * p + 8 < n:
            change = lax.dot_general(
                rows[:, :n], rows, (((0,), (0,)), ((), ())), precision=HI, preferred_element_type=F32
            )
            work[8 * p + 8 :, :] = work[8 * p + 8 :, :] - change[8 * p + 8 :, :]
    inverse[...] = work[:, n:]


def orthonormal_kernel(total_rows, gram, filtered, out, work, inverse):
    n = out.shape[-1]
    value = gram[...].reshape(n, n) / total_rows
    rows = lax.broadcasted_iota(jnp.int32, (n, n), 0)
    cols = lax.broadcasted_iota(jnp.int32, (n, n), 1)
    same = rows == cols

    def phi(x):
        return jnp.where(rows > cols, x, jnp.where(same, 0.5 * x, 0.0))

    def exact(a, b):
        return jnp.dot(a, b, precision=HI, preferred_element_type=F32)

    def short(a, b):
        return dot(rounded(a), rounded(b))

    diagonal = jnp.where(same, value, 0.0)
    across = lax.rsqrt(jnp.sum(diagonal, axis=0, keepdims=True))
    down = lax.rsqrt(jnp.sum(diagonal, axis=1, keepdims=True))
    excess = jnp.where(same, 0.0, value * across * down)
    first = jnp.where(rows > cols, excess, 0.0)
    first_t = excess - first
    product = exact(first, excess)
    second_excess = -product - exact(first_t - product, first_t)
    second = phi(second_excess)
    second_t = second_excess - second
    product = short(second, second_excess)
    third_excess = -product - short(second_t - product, second_t)
    third = phi(third_excess)
    factor = exact(second, first) - first - second
    factor = jnp.where(same, 1.0 + factor, factor)
    factor = factor - short(third, factor)
    inverse[...] = factor * across
    error = jnp.sum(third_excess * third_excess)

    @pl.when(jnp.logical_not(error < 1e-7))
    def _():
        eliminate(value, work, inverse)

    out[...] = lax.dot_general(
        filtered[...], inverse[...], (((1,), (1,)), ((), ())), precision=HI, preferred_element_type=F32
    )


def orthonormal(gram, filtered, total_rows):
    n = filtered.shape[-1]
    return pl.pallas_call(
        functools.partial(orthonormal_kernel, float(total_rows)),
        out_shape=jax.ShapeDtypeStruct(filtered.shape, F32),
        in_specs=[VM, VM],
        out_specs=VM,
        scratch_shapes=[pltpu.VMEM((n, 2 * n), F32), pltpu.VMEM((n, n), F32)],
        compiler_params=params(),
        name="orthonormal",
    )(gram, filtered)


POLE = ("x_hi", "y")
ROW = ("x_lo", "z", "core")
PLANE = ("x_hi", "y", "x_lo")
LINE = ("z", "core")


def neighbours(first, last):
    peers = lax.axis_size(ROW)
    up = [(i, i + 1) for i in range(peers - 1)]
    down = [(j, i) for i, j in up]
    return lax.ppermute(last, ROW, up), lax.ppermute(first, ROW, down)


def exchange(value, axes):
    return lax.all_to_all(value, axes, split_axis=0, concat_axis=0, tiled=True)


def shards(basis, inverses, lower, upper, pole_weights):
    rows, width = basis.shape
    count = inverses.shape[1]
    size = inverses.shape[-1]
    low, high, local = first_edges(inverses, lower, upper, basis, count, size, width)
    joints = (low, high)
    before, after = halo_joints = neighbours(low, high)
    inverses, lower, upper, basis, middle, known = first_pair(
        inverses, lower, upper, basis, low, high, count, size, width
    )
    for _ in range(SWEEPS // 2 - 1):
        low, high, local, inner = meet(
            inverses, lower, upper, basis, known, low, high, local, before, after
        )
        before, after = neighbours(low, high)
        middle, known = pair(inverses, lower, upper, basis, low, high, inner, middle)
    solved = finish(
        pole_weights, inverses, lower, upper, known, middle, *joints, *halo_joints,
        low, high, local, before, after,
    )
    received = exchange(solved, POLE)
    plane = lax.axis_size(PLANE)
    filtered, gram = partial_gram(received, plane)
    gram = exchange(gram, PLANE).sum(0, keepdims=True)
    line = lax.axis_size(LINE)
    gram = exchange(jnp.broadcast_to(gram, (line, *gram.shape[1:])), LINE).sum(0, keepdims=True)
    gram = exchange(jnp.broadcast_to(gram, (plane, *gram.shape[1:])), PLANE)
    return orthonormal(gram, filtered, rows * lax.axis_size(ROW))


def solution(mesh):
    devices = mesh.devices.reshape(2, 4, 2, 8, 2)
    inner = Mesh(devices, ("x_hi", "y", "x_lo", "z", "core"))
    return jax.shard_map(
        shards,
        mesh=inner,
        in_specs=(
            P(ROW, None),
            P(POLE, ROW, None, None),
            P(ROW, None, None),
            P(ROW, None, None),
            P(POLE),
        ),
        out_specs=P(ROW + POLE, None),
        check_vma=False,
    )
```

```python
import functools

import jax
import jax.numpy as jnp
from jax import lax
from jax.experimental import pallas as pl
from jax.experimental.pallas import tpu as pltpu
from jax.sharding import Mesh, PartitionSpec as P

SWEEPS = 4
EXTRA = 16
F32 = jnp.float32
BF16 = jnp.bfloat16
HI = lax.Precision.HIGHEST
VM = pl.BlockSpec(memory_space=pltpu.VMEM)
HBM = pl.BlockSpec(memory_space=pltpu.HBM)
SM = pl.BlockSpec(memory_space=pltpu.SMEM)
LIMIT = 16 << 20


def dot(a, b):
    return jnp.dot(a, b, preferred_element_type=F32)


def in_hbm(value):
    return pltpu.with_memory_space_constraint(value, pltpu.HBM)


def params():
    return pltpu.CompilerParams(vmem_limit_bytes=LIMIT)


def cost(flops, moved):
    return pl.CostEstimate(flops=int(flops), bytes_accessed=int(moved), transcendentals=0)


class Side:
    def __init__(self, which, count):
        self.low = lax.axis_index("core") == which
        self.edge = jnp.where(self.low, 0, count - 1)
        self.inner = jnp.where(self.low, 1, count - 2)
        self.third = jnp.where(self.low, 2, count - 3)
        self.outward = jnp.where(self.low, 0, 1)
        self.inward = 1 - self.outward


def sides(count):
    return Side(0, count), Side(1, count)


def rounded(value):
    return value.astype(BF16)


def first_edges_kernel(
    count, inverses, lower, upper, basis, cross, chip, local, inv, coupling, base, sem
):
    width = base.shape[-1]
    last = count - 1
    copies = {}

    def begin(name, source, target):
        copies[name] = pltpu.make_async_copy(source, target, sem.at[len(copies)])
        copies[name].start()

    def finished(*names):
        for name in names:
            copies[name].wait()

    def begin_coupling(direction, b):
        begin(("coupling", direction, b), (lower, upper)[direction].at[b], coupling.at[direction, b])

    for b in (0, last, 1, last - 1):
        begin(("basis", b), basis.at[b], base.at[b])
        begin(("inverse", b), inverses.at[0, b], inv.at[b])
    begin_coupling(1, 0)
    begin_coupling(0, last)
    begin_coupling(0, 0)
    begin_coupling(1, last)
    early = list(copies)
    for b in range(2, last - 1):
        begin(("basis", b), basis.at[b], base.at[b])
        begin(("inverse", b), inverses.at[0, b], inv.at[b])
    for b in range(1, last):
        begin_coupling(0, b)
        begin_coupling(1, b)
    both = list(enumerate(sides(count)))
    outs = (cross, chip)
    finished(("basis", 0), ("inverse", 0), ("basis", last), ("inverse", last))
    for k, side in both:
        outs[k][:, :width] = rounded(dot(inv[side.edge], base[side.edge]))
    finished(("basis", 1), ("inverse", 1), ("basis", last - 1), ("inverse", last - 1))
    inner = [rounded(dot(inv[side.inner], base[side.inner])) for k, side in both]
    finished(("coupling", 1, 0), ("coupling", 0, last))
    rhs = []
    for k, side in both:
        value = dot(coupling[side.inward, side.edge], inner[k])
        rhs.append(rounded(base[side.edge].astype(F32) + value))
    finished(("coupling", 0, 0), ("coupling", 1, last))
    for k, side in both:
        outs[k][:, 2 * width :] = rounded(dot(inv[side.edge], coupling[side.outward, side.edge]))
    for k, side in both:
        value = dot(inv[side.edge], rhs[k])
        outs[k][:, width : 2 * width] = rounded(value)
        local[k] = value
    finished(*(name for name in copies if name not in early))


def first_edges(inverses, lower, upper, basis):
    count, size, width = basis.shape
    out = jax.ShapeDtypeStruct((size, 2 * width + size), BF16)
    return pl.pallas_call(
        functools.partial(first_edges_kernel, count),
        out_shape=(
            out,
            out,
            jax.ShapeDtypeStruct((2, size, width), F32),
            jax.ShapeDtypeStruct((count, size, size), BF16),
            jax.ShapeDtypeStruct((2, count, size, size), BF16),
            jax.ShapeDtypeStruct((count, size, width), BF16),
        ),
        in_specs=[HBM] * 4,
        out_specs=(VM,) * 6,
        scratch_shapes=[pltpu.SemaphoreType.DMA((4 * count,))],
        compiler_params=params(),
        name="first_edges",
    )(in_hbm(inverses), in_hbm(lower), in_hbm(upper), in_hbm(basis))


def two_sweeps(count, inv, coupling, base, state, held, rhs, middle, known):
    for b in range(1, count - 1):
        value = dot(coupling[0, b], state[b - 1]) + dot(coupling[1, b], state[b + 1])
        rhs[b] = rounded(base[b].astype(F32) + value)
    for b in range(1, count - 1):
        held[b] = rounded(dot(inv[b], rhs[b]))
    for b in range(2, count - 2):
        value = dot(coupling[0, b], held[b - 1]) + dot(coupling[1, b], held[b + 1])
        rhs[b] = rounded(base[b].astype(F32) + value)
    for k, side in enumerate(sides(count)):
        for j, (b, further) in enumerate(((side.edge, side.inner), (side.inner, side.third))):
            known[2 * k + j] = base[b].astype(F32) + dot(coupling[side.inward, b], held[further])
    for b in range(2, count - 2):
        middle[b - 2] = rounded(dot(inv[b], rhs[b]))


def first_pair_kernel(count, inv, coupling, base, cross, chip, middle, known, state, held, rhs):
    width = base.shape[-1]
    for side, payload in zip(sides(count), (cross, chip)):
        state[side.edge] = payload[:, :width]
    for b in range(1, count - 1):
        state[b] = rounded(dot(inv[b], base[b]))
    two_sweeps(count, inv, coupling, base, state, held, rhs, middle, known)


def pair_kernel(
    count, inv, coupling, base, cross, chip, inner, previous, middle, known, state, held, rhs
):
    width = base.shape[-1]
    for k, (side, payload) in enumerate(zip(sides(count), (cross, chip))):
        state[side.edge] = payload[:, :width]
        state[side.inner] = inner[k]
    for b in range(2, count - 2):
        state[b] = previous[b - 2]
    two_sweeps(count, inv, coupling, base, state, held, rhs, middle, known)


def pair_call(kernel, name, *operands):
    count, size, width = operands[2].shape
    flops = 12 * (count - 2) * size * size * width
    return pl.pallas_call(
        functools.partial(kernel, count),
        out_shape=(
            jax.ShapeDtypeStruct((count - 4, size, width), BF16),
            jax.ShapeDtypeStruct((4, size, width), F32),
        ),
        in_specs=[VM] * len(operands),
        out_specs=(VM, VM),
        scratch_shapes=[pltpu.VMEM((count, size, width), BF16)] * 3,
        compiler_params=params(),
        cost_estimate=cost(flops, 6 * count * size * size),
        name=name,
    )(*operands)


def absorbed(count, inv, coupling, known, pieces, local):
    width = known.shape[-1]
    both = list(enumerate(sides(count)))
    values = []
    for k, side in both:
        joint, halo_joint, own, halo = pieces[k]
        halo_next = halo[:, width : 2 * width].astype(F32) + dot(
            halo_joint[:, 2 * width :], own[:, :width]
        )
        edge_next = local[k] + dot(joint[:, 2 * width :], halo[:, :width])
        values.append((rounded(halo_next), rounded(edge_next)))
    rhs = []
    for j in (1, 0):
        for k, side in both:
            b = side.inner if j else side.edge
            value = known[2 * k + j] + dot(coupling[side.outward, b], values[k][j])
            rhs.append((b, rounded(value)))
    inner_a, inner_b, edge_a, edge_b = [rounded(dot(inv[b], value)) for b, value in rhs]
    return (edge_a, edge_b), (inner_a, inner_b)


def meet_kernel(
    count, inv, coupling, base, known, cross, chip, local, from_cross, from_chip,
    cross_out, chip_out, local_out, inner_out,
):
    width = known.shape[-1]
    pieces = ((cross, from_cross, cross, from_cross), (chip, from_chip, chip, from_chip))
    edge, inner = absorbed(count, inv, coupling, known, pieces, local)
    both = list(enumerate(sides(count)))
    outs = (cross_out, chip_out)
    rhs = []
    for k, side in both:
        value = base[side.edge].astype(F32) + dot(coupling[side.inward, side.edge], inner[k])
        rhs.append(rounded(value))
        outs[k][:, :width] = edge[k]
        inner_out[k] = inner[k]
    for k, side in both:
        value = dot(inv[side.edge], rhs[k])
        outs[k][:, width:] = rounded(value)
        local_out[k] = value


def meet(*operands):
    count, size, width = operands[2].shape
    out = jax.ShapeDtypeStruct((size, 2 * width), BF16)
    return pl.pallas_call(
        functools.partial(meet_kernel, count),
        out_shape=(
            out,
            out,
            jax.ShapeDtypeStruct((2, size, width), F32),
            jax.ShapeDtypeStruct((2, size, width), BF16),
        ),
        in_specs=[VM] * len(operands),
        out_specs=(VM, VM, VM, VM),
        compiler_params=params(),
        cost_estimate=cost(32 * size * size * width, 24 * size * size),
        name="meet",
    )(*operands)


def finish_kernel(
    count, weight, inv, coupling, known, middle, cross_joint, chip_joint, from_cross_joint,
    from_chip_joint, cross, chip, local, from_cross, from_chip, out,
):
    size, width = known.shape[1:]
    pieces = (
        (cross_joint, from_cross_joint, cross, from_cross),
        (chip_joint, from_chip_joint, chip, from_chip),
    )
    edge, inner = absorbed(count, inv, coupling, known, pieces, local)
    for k, side in enumerate(sides(count)):
        out[side.edge, :size] = edge[k]
        out[side.inner, :size] = inner[k]
    for b in range(2, count - 2):
        out[b, :size] = middle[b - 2]
    full = jnp.full((EXTRA, width), weight[0], F32)
    high_part = rounded(full)
    rest = full - high_part.astype(F32)
    mid_part = rounded(rest)
    low_part = rounded(rest - mid_part.astype(F32))
    place = lax.broadcasted_iota(jnp.int32, (EXTRA, width), 0)
    rows = jnp.where(
        place == 0,
        high_part.astype(F32),
        jnp.where(place == 1, mid_part.astype(F32), low_part.astype(F32)),
    )
    for b in range(count):
        out[b, size:] = rounded(rows)


def finish(weight, *operands):
    count, size, _ = operands[0].shape
    width = operands[2].shape[-1]
    return pl.pallas_call(
        functools.partial(finish_kernel, count),
        out_shape=jax.ShapeDtypeStruct((count, size + EXTRA, width), BF16),
        in_specs=[SM] + [VM] * len(operands),
        out_specs=VM,
        compiler_params=params(),
        cost_estimate=cost(24 * size * size * width, 24 * size * size),
        name="finish",
    )(weight, *operands)


def gram_kernel(size, parts, received, filtered, gram):
    total = None
    for p in range(received.shape[0]):
        rows = received[p, size : size + 3].astype(F32)
        weight = rows[0:1] + rows[1:2] + rows[2:3]
        term = weight * received[p, :size].astype(F32)
        total = term if total is None else total + term
    filtered[...] = total
    value = lax.dot_general(
        total, total, (((0,), (0,)), ((), ())), precision=HI, preferred_element_type=F32
    )
    gram[...] = value.reshape(gram.shape)


def partial_gram(received, parts):
    poles, rows, width = received.shape
    size = rows - EXTRA
    return pl.pallas_call(
        functools.partial(gram_kernel, size, parts),
        out_shape=(
            jax.ShapeDtypeStruct((size, width), F32),
            jax.ShapeDtypeStruct((parts, width // parts, width), F32),
        ),
        in_specs=[VM],
        out_specs=(VM, VM),
        compiler_params=params(),
        name="gram",
    )(received)


def eliminate(value, work, inverse):
    n = value.shape[-1]
    subs = lax.broadcasted_iota(jnp.int32, (8, 2 * n), 0)
    work[:, :n] = value
    work[:, n:] = (
        lax.broadcasted_iota(jnp.int32, (n, n), 0) == lax.broadcasted_iota(jnp.int32, (n, n), 1)
    ).astype(F32)
    for p in range(n // 8):
        rows = work[8 * p : 8 * p + 8, :]
        for j in range(8):
            column = rows[:, 8 * p + j : 8 * p + j + 1]
            scale = lax.rsqrt(column[j : j + 1])
            pivot = rows[j : j + 1] * scale
            rows = jnp.where(
                subs == j, pivot, jnp.where(subs > j, rows - (column * scale) * pivot, rows)
            )
        work[8 * p : 8 * p + 8, :] = rows
        if 8 * p + 8 < n:
            change = lax.dot_general(
                rows[:, :n], rows, (((0,), (0,)), ((), ())), precision=HI, preferred_element_type=F32
            )
            work[8 * p + 8 :, :] = work[8 * p + 8 :, :] - change[8 * p + 8 :, :]
    inverse[...] = work[:, n:]


def orthonormal_kernel(total_rows, gram, filtered, out, work, inverse):
    n = out.shape[-1]
    value = gram[...].reshape(n, n) / total_rows
    rows = lax.broadcasted_iota(jnp.int32, (n, n), 0)
    cols = lax.broadcasted_iota(jnp.int32, (n, n), 1)
    same = rows == cols

    def phi(x):
        return jnp.where(rows > cols, x, jnp.where(same, 0.5 * x, 0.0))

    def exact(a, b):
        return jnp.dot(a, b, precision=HI, preferred_element_type=F32)

    def short(a, b):
        return dot(rounded(a), rounded(b))

    diagonal = jnp.where(same, value, 0.0)
    across = lax.rsqrt(jnp.sum(diagonal, axis=0, keepdims=True))
    down = lax.rsqrt(jnp.sum(diagonal, axis=1, keepdims=True))
    excess = jnp.where(same, 0.0, value * across * down)
    first = jnp.where(rows > cols, excess, 0.0)
    first_t = excess - first
    product = exact(first, excess)
    second_excess = -product - exact(first_t - product, first_t)
    second = phi(second_excess)
    second_t = second_excess - second
    product = short(second, second_excess)
    third_excess = -product - short(second_t - product, second_t)
    third = phi(third_excess)
    factor = exact(second, first) - first - second
    factor = jnp.where(same, 1.0 + factor, factor)
    factor = factor - short(third, factor)
    inverse[...] = factor * across
    error = jnp.sum(third_excess * third_excess)

    @pl.when(jnp.logical_not(error < 1e-7))
    def _():
        eliminate(value, work, inverse)

    out[...] = lax.dot_general(
        filtered[...], inverse[...], (((1,), (1,)), ((), ())), precision=HI, preferred_element_type=F32
    )


def orthonormal(gram, filtered, total_rows):
    n = filtered.shape[-1]
    return pl.pallas_call(
        functools.partial(orthonormal_kernel, float(total_rows)),
        out_shape=jax.ShapeDtypeStruct(filtered.shape, F32),
        in_specs=[VM, VM],
        out_specs=VM,
        scratch_shapes=[pltpu.VMEM((n, 2 * n), F32), pltpu.VMEM((n, n), F32)],
        compiler_params=params(),
        name="orthonormal",
    )(gram, filtered)


POLE = ("x_hi", "y")
ROW = ("x_lo", "z", "core")
PLANE = ("x_hi", "y", "x_lo")
LINE = ("z", "core")


def swapped(cross, chip):
    peers = lax.axis_size(ROW)
    links = [(i, i + 1) for i in range(1, peers - 1, 2)]
    pairs = [(i, i + 1) for i in range(0, peers, 2)]
    return tuple(
        lax.ppermute(value, ROW, joined + [(j, i) for i, j in joined])
        for value, joined in ((cross, links), (chip, pairs))
    )


def exchange(value, axes):
    return lax.all_to_all(value, axes, split_axis=0, concat_axis=0, tiled=True)


def shards(basis, inverses, lower, upper, pole_weights):
    rows, width = basis.shape
    count, size = inverses.shape[1:3]
    cross, chip, local, inv, coupling, base = first_edges(
        inverses, lower, upper, basis.reshape(count, size, width)
    )
    joints = (cross, chip)
    received = halo_joints = swapped(cross, chip)
    middle, known = pair_call(first_pair_kernel, "first_pair", inv, coupling, base, cross, chip)
    for _ in range(SWEEPS // 2 - 1):
        cross, chip, local, inner = meet(
            inv, coupling, base, known, cross, chip, local, *received
        )
        received = swapped(cross, chip)
        middle, known = pair_call(
            pair_kernel, "pair", inv, coupling, base, cross, chip, inner, middle
        )
    solved = finish(
        pole_weights, inv, coupling, known, middle, *joints, *halo_joints, cross, chip, local, *received
    )
    received = exchange(solved, POLE)
    plane = lax.axis_size(PLANE)
    filtered, gram = partial_gram(received, plane)
    gram = exchange(gram, PLANE).sum(0, keepdims=True)
    line = lax.axis_size(LINE)
    gram = exchange(jnp.broadcast_to(gram, (line, *gram.shape[1:])), LINE).sum(0, keepdims=True)
    gram = exchange(jnp.broadcast_to(gram, (plane, *gram.shape[1:])), PLANE)
    return orthonormal(gram, filtered, rows * lax.axis_size(ROW))


def solution(mesh):
    devices = mesh.devices.reshape(2, 4, 2, 8, 2)
    inner = Mesh(devices, ("x_hi", "y", "x_lo", "z", "core"))
    return jax.shard_map(
        shards,
        mesh=inner,
        in_specs=(
            P(ROW, None),
            P(POLE, ROW, None, None),
            P(ROW, None, None),
            P(ROW, None, None),
            P(POLE),
        ),
        out_specs=P(ROW + POLE, None),
        check_vma=False,
    )
```

```python
import functools

import jax
import jax.numpy as jnp
from jax import lax
from jax.experimental import pallas as pl
from jax.experimental.pallas import tpu as pltpu
from jax.sharding import Mesh, PartitionSpec as P

SWEEPS = 4
EXTRA = 16
F32 = jnp.float32
BF16 = jnp.bfloat16
HI = lax.Precision.HIGHEST
VM = pl.BlockSpec(memory_space=pltpu.VMEM)
SM = pl.BlockSpec(memory_space=pltpu.SMEM)
HBM = pl.BlockSpec(memory_space=pltpu.HBM)
LIMIT = 16 << 20


def dot(a, b):
    return jnp.dot(a, b, preferred_element_type=F32)


def in_hbm(value):
    return pltpu.with_memory_space_constraint(value, pltpu.HBM)


def params():
    return pltpu.CompilerParams(vmem_limit_bytes=LIMIT)


def cost(flops, moved):
    return pl.CostEstimate(flops=int(flops), bytes_accessed=int(moved), transcendentals=0)


class Side:
    def __init__(self, which, count):
        self.low = lax.axis_index("core") == which
        self.edge = jnp.where(self.low, 0, count - 1)
        self.inner = jnp.where(self.low, 1, count - 2)
        self.outward = jnp.where(self.low, 0, 1)
        self.inward = 1 - self.outward


def sides(count):
    return Side(0, count), Side(1, count)


def rounded(value):
    return value.astype(BF16)


def weight_rows(weight, shape):
    full = jnp.full(shape, weight, F32)
    high = rounded(full)
    rest = full - high.astype(F32)
    mid = rounded(rest)
    low = rounded(rest - mid.astype(F32))
    place = lax.broadcasted_iota(jnp.int32, shape, 0)
    rows = jnp.where(
        place == 0, high.astype(F32), jnp.where(place == 1, mid.astype(F32), low.astype(F32))
    )
    return rounded(rows)


def first_edges_kernel(
    count, inverses, basis, cross, chip, inv, base, sem
):
    ends = (0, count - 1)
    pairs = [(basis.at[b], base.at[k]) for k, b in enumerate(ends)]
    pairs += [(inverses.at[b], inv.at[k]) for k, b in enumerate(ends)]
    copies = [pltpu.make_async_copy(a, b, sem.at[i]) for i, (a, b) in enumerate(pairs)]
    for copy in copies:
        copy.start()
    for copy in copies:
        copy.wait()
    for side, out in zip(sides(2), (cross, chip)):
        out[...] = rounded(dot(inv[side.edge], base[side.edge]))


def first_edges(inverses, basis):
    count, size, width = basis.shape
    out = jax.ShapeDtypeStruct((size, width), BF16)
    return pl.pallas_call(
        functools.partial(first_edges_kernel, count),
        out_shape=(out, out),
        in_specs=[HBM] * 2,
        out_specs=(VM, VM),
        scratch_shapes=[
            pltpu.VMEM((2, size, size), BF16),
            pltpu.VMEM((2, size, width), BF16),
            pltpu.SemaphoreType.DMA((4,)),
        ],
        compiler_params=params(),
        name="first_edges",
    )(in_hbm(inverses), in_hbm(basis))


def advance(count, inv, coupling, base, state, rhs, middle, known, ready=lambda b: None):
    for b in range(1, count - 1):
        ready(b)
        value = dot(coupling[0, b], state[b - 1]) + dot(coupling[1, b], state[b + 1])
        rhs[b] = rounded(base[b].astype(F32) + value)
    ready(0)
    ready(count - 1)
    for k, side in enumerate(sides(count)):
        value = dot(coupling[side.inward, side.edge], state[side.inner])
        known[k] = base[side.edge].astype(F32) + value
    for b in range(1, count - 1):
        middle[b - 1] = rounded(dot(inv[b], rhs[b]))


def first_sweep_kernel(
    count, inv, lower, upper, base, cross, chip, coupling, middle, known, state, rhs, sem
):
    copies = []
    for b in range(count):
        copies.append(
            [
                pltpu.make_async_copy(source.at[b], coupling.at[k, b], sem.at[2 * b + k])
                for k, source in enumerate((lower, upper))
            ]
        )
    for b in [*range(1, count - 1), 0, count - 1]:
        for copy in copies[b]:
            copy.start()
    for side, edge in zip(sides(count), (cross, chip)):
        state[side.edge] = edge[...]
    for b in range(1, count - 1):
        state[b] = rounded(dot(inv[b], base[b]))

    def ready(b):
        for copy in copies[b]:
            copy.wait()

    advance(count, inv, coupling, base, state, rhs, middle, known, ready)


def sweep_kernel(count, inv, coupling, base, cross, chip, previous, middle, known, state, rhs):
    for side, edge in zip(sides(count), (cross, chip)):
        state[side.edge] = edge[...]
    for b in range(1, count - 1):
        state[b] = previous[b - 1]
    advance(count, inv, coupling, base, state, rhs, middle, known)


def sweep_shapes(count, size, width):
    return (
        jax.ShapeDtypeStruct((count - 2, size, width), BF16),
        jax.ShapeDtypeStruct((2, size, width), F32),
    )


def sweep_cost(count, size, width):
    return cost(6 * count * size * size * width, 6 * count * size * size)


def first_sweep(inv, lower, upper, base, cross, chip):
    count, size, width = base.shape
    return pl.pallas_call(
        functools.partial(first_sweep_kernel, count),
        out_shape=(
            jax.ShapeDtypeStruct((2, count, size, size), BF16),
            *sweep_shapes(count, size, width),
        ),
        in_specs=[VM, HBM, HBM, VM, VM, VM],
        out_specs=(VM,) * 3,
        scratch_shapes=[
            pltpu.VMEM((count, size, width), BF16),
            pltpu.VMEM((count, size, width), BF16),
            pltpu.SemaphoreType.DMA((2 * count,)),
        ],
        compiler_params=params(),
        cost_estimate=sweep_cost(count, size, width),
        name="first_sweep",
    )(inv, in_hbm(lower), in_hbm(upper), base, cross, chip)


def sweep(inv, coupling, base, cross, chip, middle):
    count, size, width = base.shape
    return pl.pallas_call(
        functools.partial(sweep_kernel, count),
        out_shape=sweep_shapes(count, size, width),
        in_specs=[VM] * 6,
        out_specs=(VM,) * 2,
        scratch_shapes=[pltpu.VMEM((count, size, width), BF16)] * 2,
        compiler_params=params(),
        cost_estimate=sweep_cost(count, size, width),
        name="sweep",
    )(inv, coupling, base, cross, chip, middle)


def edge_blocks(count, inv, coupling, known, halos):
    both = list(enumerate(sides(count)))
    rhs = []
    for k, side in both:
        value = known[k] + dot(coupling[side.outward, side.edge], halos[k][...])
        rhs.append(rounded(value))
    return [rounded(dot(inv[side.edge], rhs[k])) for k, side in both]


def edges_kernel(count, inv, coupling, known, from_cross, from_chip, cross, chip):
    cross[...], chip[...] = edge_blocks(count, inv, coupling, known, (from_cross, from_chip))


def edges(inv, coupling, known, from_cross, from_chip):
    count, size, _ = inv.shape
    width = known.shape[-1]
    out = jax.ShapeDtypeStruct((size, width), BF16)
    return pl.pallas_call(
        functools.partial(edges_kernel, count),
        out_shape=(out, out),
        in_specs=[VM] * 5,
        out_specs=(VM, VM),
        compiler_params=params(),
        cost_estimate=cost(8 * size * size * width, 8 * size * size),
        name="edges",
    )(inv, coupling, known, from_cross, from_chip)


def finish_kernel(count, weight, inv, coupling, known, from_cross, from_chip, middle, out):
    size, width = known.shape[1:]
    rows = weight_rows(weight[0], (EXTRA, width))
    for b in range(1, count - 1):
        out[b, :size] = middle[b - 1]
    for b in range(count):
        out[b, size:] = rows
    values = edge_blocks(count, inv, coupling, known, (from_cross, from_chip))
    for side, value in zip(sides(count), values):
        out[side.edge, :size] = value


def finish(weight, inv, coupling, known, from_cross, from_chip, middle):
    count, size, _ = inv.shape
    width = known.shape[-1]
    return pl.pallas_call(
        functools.partial(finish_kernel, count),
        out_shape=jax.ShapeDtypeStruct((count, size + EXTRA, width), BF16),
        in_specs=[SM] + [VM] * 6,
        out_specs=VM,
        compiler_params=params(),
        cost_estimate=cost(8 * size * size * width, 8 * size * size),
        name="finish",
    )(weight, inv, coupling, known, from_cross, from_chip, middle)


def gram_kernel(size, parts, received, filtered, gram):
    total = None
    for p in range(received.shape[0]):
        rows = received[p, size : size + 3].astype(F32)
        weight = rows[0:1] + rows[1:2] + rows[2:3]
        term = weight * received[p, :size].astype(F32)
        total = term if total is None else total + term
    filtered[...] = total
    value = lax.dot_general(
        total, total, (((0,), (0,)), ((), ())), precision=HI, preferred_element_type=F32
    )
    gram[...] = value.reshape(gram.shape)


def partial_gram(received, parts):
    poles, rows, width = received.shape
    size = rows - EXTRA
    return pl.pallas_call(
        functools.partial(gram_kernel, size, parts),
        out_shape=(
            jax.ShapeDtypeStruct((size, width), F32),
            jax.ShapeDtypeStruct((parts, width // parts, width), F32),
        ),
        in_specs=[VM],
        out_specs=(VM, VM),
        compiler_params=params(),
        name="gram",
    )(received)


def eliminate(value, work, inverse):
    n = value.shape[-1]
    subs = lax.broadcasted_iota(jnp.int32, (8, 2 * n), 0)
    work[:, :n] = value
    work[:, n:] = (
        lax.broadcasted_iota(jnp.int32, (n, n), 0) == lax.broadcasted_iota(jnp.int32, (n, n), 1)
    ).astype(F32)
    for p in range(n // 8):
        rows = work[8 * p : 8 * p + 8, :]
        for j in range(8):
            column = rows[:, 8 * p + j : 8 * p + j + 1]
            scale = lax.rsqrt(column[j : j + 1])
            pivot = rows[j : j + 1] * scale
            rows = jnp.where(
                subs == j, pivot, jnp.where(subs > j, rows - (column * scale) * pivot, rows)
            )
        work[8 * p : 8 * p + 8, :] = rows
        if 8 * p + 8 < n:
            change = lax.dot_general(
                rows[:, :n], rows, (((0,), (0,)), ((), ())), precision=HI, preferred_element_type=F32
            )
            work[8 * p + 8 :, :] = work[8 * p + 8 :, :] - change[8 * p + 8 :, :]
    inverse[...] = work[:, n:]


def orthonormal_kernel(total_rows, gram, filtered, out, work, inverse):
    n = out.shape[-1]
    value = gram[...].reshape(n, n) / total_rows
    rows = lax.broadcasted_iota(jnp.int32, (n, n), 0)
    cols = lax.broadcasted_iota(jnp.int32, (n, n), 1)
    same = rows == cols

    def phi(x):
        return jnp.where(rows > cols, x, jnp.where(same, 0.5 * x, 0.0))

    def exact(a, b):
        return jnp.dot(a, b, precision=HI, preferred_element_type=F32)

    def short(a, b):
        return dot(rounded(a), rounded(b))

    diagonal = jnp.where(same, value, 0.0)
    across = lax.rsqrt(jnp.sum(diagonal, axis=0, keepdims=True))
    down = lax.rsqrt(jnp.sum(diagonal, axis=1, keepdims=True))
    excess = jnp.where(same, 0.0, value * across * down)
    first = jnp.where(rows > cols, excess, 0.0)
    first_t = excess - first
    product = exact(first, excess)
    second_excess = -product - exact(first_t - product, first_t)
    second = phi(second_excess)
    second_t = second_excess - second
    product = short(second, second_excess)
    third_excess = -product - short(second_t - product, second_t)
    third = phi(third_excess)
    factor = exact(second, first) - first - second
    factor = jnp.where(same, 1.0 + factor, factor)
    factor = factor - short(third, factor)
    inverse[...] = factor * across
    error = jnp.sum(third_excess * third_excess)

    @pl.when(jnp.logical_not(error < 1e-7))
    def _():
        eliminate(value, work, inverse)

    out[...] = lax.dot_general(
        filtered[...], inverse[...], (((1,), (1,)), ((), ())), precision=HI, preferred_element_type=F32
    )


def orthonormal(gram, filtered, total_rows):
    n = filtered.shape[-1]
    return pl.pallas_call(
        functools.partial(orthonormal_kernel, float(total_rows)),
        out_shape=jax.ShapeDtypeStruct(filtered.shape, F32),
        in_specs=[VM, VM],
        out_specs=VM,
        scratch_shapes=[pltpu.VMEM((n, 2 * n), F32), pltpu.VMEM((n, n), F32)],
        compiler_params=params(),
        name="orthonormal",
    )(gram, filtered)


POLE = ("x_hi", "y")
ROW = ("x_lo", "z", "core")
PLANE = ("x_hi", "y", "x_lo")
LINE = ("z", "core")


def swapped(cross, chip):
    peers = lax.axis_size(ROW)
    links = [(i, i + 1) for i in range(1, peers - 1, 2)]
    pairs = [(i, i + 1) for i in range(0, peers, 2)]
    return tuple(
        lax.ppermute(value, ROW, joined + [(j, i) for i, j in joined])
        for value, joined in ((cross, links), (chip, pairs))
    )


def exchange(value, axes):
    return lax.all_to_all(value, axes, split_axis=0, concat_axis=0, tiled=True)


def shards(basis, inverses, lower, upper, pole_weights):
    rows, width = basis.shape
    count, size = inverses.shape[1:3]
    inv = inverses.reshape(count, size, size)
    base = basis.reshape(count, size, width)
    cross, chip = first_edges(inv, base)
    halos = swapped(cross, chip)
    coupling, middle, known = first_sweep(inv, lower, upper, base, cross, chip)
    for _ in range(SWEEPS - 1):
        cross, chip = edges(inv, coupling, known, *halos)
        halos = swapped(cross, chip)
        middle, known = sweep(inv, coupling, base, cross, chip, middle)
    solved = finish(pole_weights, inv, coupling, known, *halos, middle)
    received = exchange(solved, POLE)
    plane = lax.axis_size(PLANE)
    filtered, gram = partial_gram(received, plane)
    gram = exchange(gram, PLANE).sum(0, keepdims=True)
    line = lax.axis_size(LINE)
    gram = exchange(jnp.broadcast_to(gram, (line, *gram.shape[1:])), LINE).sum(0, keepdims=True)
    gram = exchange(jnp.broadcast_to(gram, (plane, *gram.shape[1:])), PLANE)
    return orthonormal(gram, filtered, rows * lax.axis_size(ROW))


def solution(mesh):
    devices = mesh.devices.reshape(2, 4, 2, 8, 2)
    inner = Mesh(devices, ("x_hi", "y", "x_lo", "z", "core"))
    return jax.shard_map(
        shards,
        mesh=inner,
        in_specs=(
            P(ROW, None),
            P(POLE, ROW, None, None),
            P(ROW, None, None),
            P(ROW, None, None),
            P(POLE),
        ),
        out_specs=P(ROW + POLE, None),
        check_vma=False,
    )
```

```python
import functools

import jax
import jax.numpy as jnp
from jax import lax
from jax.experimental import pallas as pl
from jax.experimental.pallas import tpu as pltpu
from jax.sharding import Mesh, PartitionSpec as P

F32 = jnp.float32
BF16 = jnp.bfloat16
HI = lax.Precision.HIGHEST
VM = pl.BlockSpec(memory_space=pltpu.VMEM)
HBM = pl.BlockSpec(memory_space=pltpu.HBM)
SM = pl.BlockSpec(memory_space=pltpu.SMEM)
LIMIT = 16 << 20


def dot(a, b):
    return jnp.dot(a, b, preferred_element_type=F32)


def in_hbm(value):
    return pltpu.with_memory_space_constraint(value, pltpu.HBM)


def params():
    return pltpu.CompilerParams(vmem_limit_bytes=LIMIT)


def cost(flops, moved):
    return pl.CostEstimate(flops=int(flops), bytes_accessed=int(moved), transcendentals=0)


class Side:
    def __init__(self, which, count):
        self.low = lax.axis_index("core") == which
        self.edge = jnp.where(self.low, 0, count - 1)
        self.inner = jnp.where(self.low, 1, count - 2)
        self.third = jnp.where(self.low, 2, count - 3)
        self.outward = jnp.where(self.low, 0, 1)
        self.inward = 1 - self.outward


def sides(count):
    return Side(0, count), Side(1, count)


def rounded(value):
    return value.astype(BF16)


class Loads:
    def __init__(self, arguments, arrays, sem):
        inverses, lower, upper, basis = arguments
        inv, coupling, base = arrays
        self.pairs = {
            "inverse": (inverses, inv),
            "basis": (basis, base),
            "lower": (lower, coupling.at[0]),
            "upper": (upper, coupling.at[1]),
        }
        self.sem = sem
        self.copies = {}

    def begin(self, name, *blocks):
        source, target = self.pairs[name]
        for b in blocks:
            copy = pltpu.make_async_copy(source.at[b], target.at[b], self.sem.at[len(self.copies)])
            self.copies[name, b] = copy
            copy.start()

    def wait(self, name, *blocks):
        for b in blocks:
            self.copies[name, b].wait()


def first_edges_kernel(
    count, inverses, lower, upper, basis, cross, chip, local, inv, coupling, base, sem
):
    width = base.shape[-1]
    last = count - 1
    loads = Loads((inverses, lower, upper, basis), (inv, coupling, base), sem)
    loads.begin("inverse", 0, last)
    loads.begin("lower", 0)
    loads.begin("upper", last)
    loads.begin("basis", 0, last, 1, last - 1)
    loads.begin("inverse", 1, last - 1)
    loads.begin("upper", 0)
    loads.begin("lower", last)
    both = list(enumerate(sides(count)))
    outs = (cross, chip)
    loads.wait("inverse", 0, last)
    loads.wait("lower", 0)
    loads.wait("upper", last)
    for k, side in both:
        outs[k][:, 2 * width :] = rounded(dot(inv[side.edge], coupling[side.outward, side.edge]))
    loads.wait("basis", 0, last, 1, last - 1)
    loads.wait("inverse", 1, last - 1)
    inner = [rounded(dot(inv[side.inner], base[side.inner])) for k, side in both]
    for k, side in both:
        outs[k][:, :width] = rounded(dot(inv[side.edge], base[side.edge]))
    loads.wait("upper", 0)
    loads.wait("lower", last)
    rhs = []
    for k, side in both:
        value = dot(coupling[side.inward, side.edge], inner[k])
        rhs.append(rounded(base[side.edge].astype(F32) + value))
    for k, side in both:
        value = dot(inv[side.edge], rhs[k])
        outs[k][:, width : 2 * width] = rounded(value)
        local[k] = value


def array_shapes(count, size, width):
    return (
        jax.ShapeDtypeStruct((count, size, size), BF16),
        jax.ShapeDtypeStruct((2, count, size, size), BF16),
        jax.ShapeDtypeStruct((count, size, width), BF16),
    )


def first_edges(inverses, lower, upper, basis):
    count, size, width = basis.shape
    out = jax.ShapeDtypeStruct((size, 2 * width + size), BF16)
    return pl.pallas_call(
        functools.partial(first_edges_kernel, count),
        out_shape=(
            out,
            out,
            jax.ShapeDtypeStruct((2, size, width), F32),
            *array_shapes(count, size, width),
        ),
        in_specs=[HBM] * 4,
        out_specs=(VM,) * 6,
        scratch_shapes=[pltpu.SemaphoreType.DMA((12,))],
        compiler_params=params(),
        name="first_edges",
    )(*(in_hbm(x) for x in (inverses, lower, upper, basis)))


def ahead_blocks(count):
    return range(3, count - 3)


def right_side(b, coupling, base, left, right):
    value = dot(coupling[0, b], left) + dot(coupling[1, b], right)
    return rounded(base[b].astype(F32) + value)


def two_sweeps(count, inv, coupling, base, state, held, rhs, known, todo, ready=lambda b: None):
    for b in todo:
        ready(b)
        rhs[b] = right_side(b, coupling, base, state[b - 1], state[b + 1])
    for b in todo:
        held[b] = rounded(dot(inv[b], rhs[b]))
    for b in range(2, count - 2):
        rhs[b] = right_side(b, coupling, base, held[b - 1], held[b + 1])
    for k, side in enumerate(sides(count)):
        for j, (b, further) in enumerate(((side.edge, side.inner), (side.inner, side.third))):
            known[2 * k + j] = base[b].astype(F32) + dot(coupling[side.inward, b], held[further])


def first_pair_kernel(
    count, weight, inverses, lower, upper, basis, inv_in, coupling_in, base_in, cross, chip,
    inv, coupling, base, middle, known, ahead, state, held, rhs, sem,
):
    width = base.shape[-1]
    inside = range(1, count - 1)
    deep = range(2, count - 2)
    loads = Loads((inverses, lower, upper, basis), (inv, coupling, base), sem)
    for b in deep:
        loads.begin("basis", b)
        loads.begin("inverse", b)
    for b in inside:
        loads.begin("lower", b)
        loads.begin("upper", b)
    for side, payload in zip(sides(count), (cross, chip)):
        state[side.edge] = payload[:, :width]
    for b in (1, count - 2, *deep):
        if b in deep:
            loads.wait("basis", b)
            loads.wait("inverse", b)
        state[b] = rounded(dot(inv[b], base[b]))

    def ready(b):
        loads.wait("lower", b)
        loads.wait("upper", b)

    two_sweeps(count, inv, coupling, base, state, held, rhs, known, inside, ready)
    for b in deep:
        middle[b - 2] = rounded(dot(inv[b], rhs[b]))
    for b in ahead_blocks(count):
        rhs[b] = right_side(b, coupling, base, middle[b - 3], middle[b - 1])
    for b in ahead_blocks(count):
        ahead[b - 3] = rounded(dot(inv[b], rhs[b]))


def pair_cost(count, size, width):
    return cost(12 * (count - 2) * size * size * width, 6 * count * size * size)


def first_pair(weight, arguments, arrays, cross, chip):
    count, size, width = arrays[2].shape
    return pl.pallas_call(
        functools.partial(first_pair_kernel, count),
        out_shape=(
            *array_shapes(count, size, width),
            jax.ShapeDtypeStruct((count - 4, size, width), BF16),
            jax.ShapeDtypeStruct((4, size, width), F32),
            jax.ShapeDtypeStruct((count - 6, size, width), BF16),
        ),
        in_specs=[SM] + [HBM] * 4 + [VM] * 5,
        out_specs=(VM,) * 6,
        scratch_shapes=[pltpu.VMEM((count, size, width), BF16)] * 3
        + [pltpu.SemaphoreType.DMA((4 * count,))],
        input_output_aliases={5: 0, 6: 1, 7: 2},
        compiler_params=params(),
        cost_estimate=pair_cost(count, size, width),
        name="first_pair",
    )(weight, *(in_hbm(x) for x in arguments), *arrays, cross, chip)


def last_pair_kernel(
    count, weight, inv, coupling, base, cross, chip, inner, previous, ahead, middle, known,
    state, held, rhs,
):
    width = base.shape[-1]
    for k, (side, payload) in enumerate(zip(sides(count), (cross, chip))):
        state[side.edge] = payload[:, :width]
        state[side.inner] = inner[k]
    for b in range(2, count - 2):
        state[b] = previous[b - 2]
    for b in ahead_blocks(count):
        held[b] = ahead[b - 3]
    todo = [b for b in range(1, count - 1) if b not in ahead_blocks(count)]
    two_sweeps(count, inv, coupling, base, state, held, rhs, known, todo)
    for b in range(2, count - 2):
        middle[b - 2] = rounded(weight[0] * dot(inv[b], rhs[b]))


def last_pair(weight, *operands):
    count, size, width = operands[2].shape
    return pl.pallas_call(
        functools.partial(last_pair_kernel, count),
        out_shape=(
            jax.ShapeDtypeStruct((count - 4, size, width), BF16),
            jax.ShapeDtypeStruct((4, size, width), F32),
        ),
        in_specs=[SM] + [VM] * len(operands),
        out_specs=(VM, VM),
        scratch_shapes=[pltpu.VMEM((count, size, width), BF16)] * 3,
        compiler_params=params(),
        cost_estimate=pair_cost(count, size, width),
        name="last_pair",
    )(weight, *operands)


def absorbed(count, inv, coupling, known, pieces, local, scale=lambda value: value):
    width = known.shape[-1]
    both = list(enumerate(sides(count)))
    values = []
    for k, side in both:
        joint, halo_joint, own, halo = pieces[k]
        halo_next = halo[:, width : 2 * width].astype(F32) + dot(
            halo_joint[:, 2 * width :], own[:, :width]
        )
        edge_next = local[k] + dot(joint[:, 2 * width :], halo[:, :width])
        values.append((rounded(halo_next), rounded(edge_next)))
    rhs = []
    for j in (1, 0):
        for k, side in both:
            b = side.inner if j else side.edge
            value = known[2 * k + j] + dot(coupling[side.outward, b], values[k][j])
            rhs.append((b, rounded(value)))
    inner_a, inner_b, edge_a, edge_b = [
        rounded(scale(dot(inv[b], value))) for b, value in rhs
    ]
    return (edge_a, edge_b), (inner_a, inner_b)


def meet_kernel(
    count, inv, coupling, base, known, cross, chip, local, from_cross, from_chip,
    cross_out, chip_out, local_out, inner_out,
):
    width = known.shape[-1]
    pieces = ((cross, from_cross, cross, from_cross), (chip, from_chip, chip, from_chip))
    edge, inner = absorbed(count, inv, coupling, known, pieces, local)
    both = list(enumerate(sides(count)))
    outs = (cross_out, chip_out)
    rhs = []
    for k, side in both:
        value = base[side.edge].astype(F32) + dot(coupling[side.inward, side.edge], inner[k])
        rhs.append(rounded(value))
        outs[k][:, :width] = edge[k]
        inner_out[k] = inner[k]
    for k, side in both:
        value = dot(inv[side.edge], rhs[k])
        outs[k][:, width:] = rounded(value)
        local_out[k] = value


def meet(*operands):
    count, size, width = operands[2].shape
    out = jax.ShapeDtypeStruct((size, 2 * width), BF16)
    return pl.pallas_call(
        functools.partial(meet_kernel, count),
        out_shape=(
            out,
            out,
            jax.ShapeDtypeStruct((2, size, width), F32),
            jax.ShapeDtypeStruct((2, size, width), BF16),
        ),
        in_specs=[VM] * len(operands),
        out_specs=(VM, VM, VM, VM),
        compiler_params=params(),
        cost_estimate=cost(32 * size * size * width, 24 * size * size),
        name="meet",
    )(*operands)


def finish_kernel(
    count, weight, inv, coupling, known, middle, cross_joint, chip_joint, from_cross_joint,
    from_chip_joint, cross, chip, local, from_cross, from_chip, out,
):
    pieces = (
        (cross_joint, from_cross_joint, cross, from_cross),
        (chip_joint, from_chip_joint, chip, from_chip),
    )
    for b in range(2, count - 2):
        out[b] = middle[b - 2]
    edge, inner = absorbed(
        count, inv, coupling, known, pieces, local, lambda value: weight[0] * value
    )
    for k, side in enumerate(sides(count)):
        out[side.edge] = edge[k]
        out[side.inner] = inner[k]


def finish(weight, *operands):
    count, size, _ = operands[0].shape
    width = operands[2].shape[-1]
    return pl.pallas_call(
        functools.partial(finish_kernel, count),
        out_shape=jax.ShapeDtypeStruct((count, size, width), BF16),
        in_specs=[SM] + [VM] * len(operands),
        out_specs=VM,
        compiler_params=params(),
        cost_estimate=cost(24 * size * size * width, 24 * size * size),
        name="finish",
    )(weight, *operands)


def gram_kernel(received, filtered, gram):
    total = received[0].astype(F32)
    for p in range(1, received.shape[0]):
        total = total + received[p].astype(F32)
    filtered[...] = total
    value = lax.dot_general(
        total, total, (((0,), (0,)), ((), ())), precision=HI, preferred_element_type=F32
    )
    gram[...] = value.reshape(gram.shape)


def partial_gram(received, parts):
    poles, size, width = received.shape
    return pl.pallas_call(
        gram_kernel,
        out_shape=(
            jax.ShapeDtypeStruct((size, width), F32),
            jax.ShapeDtypeStruct((parts, width // parts, width), F32),
        ),
        in_specs=[VM],
        out_specs=(VM, VM),
        compiler_params=params(),
        name="gram",
    )(received)


def eliminate(value, work, inverse):
    n = value.shape[-1]
    subs = lax.broadcasted_iota(jnp.int32, (8, 2 * n), 0)
    work[:, :n] = value
    work[:, n:] = (
        lax.broadcasted_iota(jnp.int32, (n, n), 0) == lax.broadcasted_iota(jnp.int32, (n, n), 1)
    ).astype(F32)
    for p in range(n // 8):
        rows = work[8 * p : 8 * p + 8, :]
        for j in range(8):
            column = rows[:, 8 * p + j : 8 * p + j + 1]
            scale = lax.rsqrt(column[j : j + 1])
            pivot = rows[j : j + 1] * scale
            rows = jnp.where(
                subs == j, pivot, jnp.where(subs > j, rows - (column * scale) * pivot, rows)
            )
        work[8 * p : 8 * p + 8, :] = rows
        if 8 * p + 8 < n:
            change = lax.dot_general(
                rows[:, :n], rows, (((0,), (0,)), ((), ())), precision=HI, preferred_element_type=F32
            )
            work[8 * p + 8 :, :] = work[8 * p + 8 :, :] - change[8 * p + 8 :, :]
    inverse[...] = work[:, n:]


def orthonormal_kernel(total_rows, gram, filtered, out, work, inverse):
    n = out.shape[-1]
    value = gram[...].reshape(n, n) / total_rows
    rows = lax.broadcasted_iota(jnp.int32, (n, n), 0)
    cols = lax.broadcasted_iota(jnp.int32, (n, n), 1)
    same = rows == cols

    def phi(x):
        return jnp.where(rows > cols, x, jnp.where(same, 0.5 * x, 0.0))

    def exact(a, b):
        return jnp.dot(a, b, precision=HI, preferred_element_type=F32)

    def short(a, b):
        return dot(rounded(a), rounded(b))

    diagonal = jnp.where(same, value, 0.0)
    across = lax.rsqrt(jnp.sum(diagonal, axis=0, keepdims=True))
    down = lax.rsqrt(jnp.sum(diagonal, axis=1, keepdims=True))
    excess = jnp.where(same, 0.0, value * across * down)
    first = jnp.where(rows > cols, excess, 0.0)
    first_t = excess - first
    product = exact(first, excess)
    second_excess = -product - exact(first_t - product, first_t)
    second = phi(second_excess)
    second_t = second_excess - second
    product = short(second, second_excess)
    third_excess = -product - short(second_t - product, second_t)
    third = phi(third_excess)
    factor = exact(second, first) - first - second
    factor = jnp.where(same, 1.0 + factor, factor)
    factor = factor - short(third, factor)
    inverse[...] = factor * across
    error = jnp.sum(third_excess * third_excess)

    @pl.when(jnp.logical_not(error < 1e-7))
    def _():
        eliminate(value, work, inverse)

    out[...] = lax.dot_general(
        filtered[...], inverse[...], (((1,), (1,)), ((), ())), precision=HI, preferred_element_type=F32
    )


def orthonormal(gram, filtered, total_rows):
    n = filtered.shape[-1]
    return pl.pallas_call(
        functools.partial(orthonormal_kernel, float(total_rows)),
        out_shape=jax.ShapeDtypeStruct(filtered.shape, F32),
        in_specs=[VM, VM],
        out_specs=VM,
        scratch_shapes=[pltpu.VMEM((n, 2 * n), F32), pltpu.VMEM((n, n), F32)],
        compiler_params=params(),
        name="orthonormal",
    )(gram, filtered)


POLE = ("x_hi", "y")
ROW = ("x_lo", "z", "core")
PLANE = ("x_hi", "y", "x_lo")
LINE = ("z", "core")


def swapped(cross, chip):
    peers = lax.axis_size(ROW)
    links = [(i, i + 1) for i in range(1, peers - 1, 2)]
    pairs = [(i, i + 1) for i in range(0, peers, 2)]
    return tuple(
        lax.ppermute(value, ROW, joined + [(j, i) for i, j in joined])
        for value, joined in ((cross, links), (chip, pairs))
    )


def exchange(value, axes):
    return lax.all_to_all(value, axes, split_axis=0, concat_axis=0, tiled=True)


def shards(basis, inverses, lower, upper, pole_weights):
    rows, width = basis.shape
    count, size = inverses.shape[1:3]
    arguments = (
        inverses.reshape(count, size, size), lower, upper, basis.reshape(count, size, width)
    )
    cross, chip, local, *arrays = first_edges(*arguments)
    joints = (cross, chip)
    halo_joints = swapped(cross, chip)
    inv, coupling, base, middle, known, ahead = first_pair(
        pole_weights, arguments, arrays, cross, chip
    )
    cross, chip, local, inner = meet(inv, coupling, base, known, cross, chip, local, *halo_joints)
    halos = swapped(cross, chip)
    middle, known = last_pair(
        pole_weights, inv, coupling, base, cross, chip, inner, middle, ahead
    )
    solved = finish(
        pole_weights, inv, coupling, known, middle, *joints, *halo_joints, cross, chip, local, *halos
    )
    received = exchange(solved, POLE)
    plane = lax.axis_size(PLANE)
    filtered, gram = partial_gram(received, plane)
    gram = exchange(gram, PLANE).sum(0, keepdims=True)
    line = lax.axis_size(LINE)
    gram = exchange(jnp.broadcast_to(gram, (line, *gram.shape[1:])), LINE).sum(0, keepdims=True)
    gram = exchange(jnp.broadcast_to(gram, (plane, *gram.shape[1:])), PLANE)
    return orthonormal(gram, filtered, rows * lax.axis_size(ROW))


def solution(mesh):
    devices = mesh.devices.reshape(2, 4, 2, 8, 2)
    inner = Mesh(devices, ("x_hi", "y", "x_lo", "z", "core"))
    return jax.shard_map(
        shards,
        mesh=inner,
        in_specs=(
            P(ROW, None),
            P(POLE, ROW, None, None),
            P(ROW, None, None),
            P(ROW, None, None),
            P(POLE),
        ),
        out_specs=P(ROW + POLE, None),
        check_vma=False,
    )
```

```python
import functools

import jax
import jax.numpy as jnp
from jax import lax
from jax.experimental import pallas as pl
from jax.experimental.pallas import tpu as pltpu
from jax.sharding import Mesh, PartitionSpec as P

F32 = jnp.float32
BF16 = jnp.bfloat16
HI = lax.Precision.HIGHEST
VM = pl.BlockSpec(memory_space=pltpu.VMEM)
HBM = pl.BlockSpec(memory_space=pltpu.HBM)
SM = pl.BlockSpec(memory_space=pltpu.SMEM)
LIMIT = 16 << 20


def dot(a, b):
    return jnp.dot(a, b, preferred_element_type=F32)


def in_hbm(value):
    return pltpu.with_memory_space_constraint(value, pltpu.HBM)


def params():
    return pltpu.CompilerParams(vmem_limit_bytes=LIMIT)


def cost(flops, moved):
    return pl.CostEstimate(flops=int(flops), bytes_accessed=int(moved), transcendentals=0)


class Side:
    def __init__(self, which, count):
        self.low = lax.axis_index("core") == which
        self.edge = jnp.where(self.low, 0, count - 1)
        self.inner = jnp.where(self.low, 1, count - 2)
        self.third = jnp.where(self.low, 2, count - 3)
        self.outward = jnp.where(self.low, 0, 1)
        self.inward = 1 - self.outward


def sides(count):
    return Side(0, count), Side(1, count)


def rounded(value):
    return value.astype(BF16)


class Loads:
    def __init__(self, pairs, sem):
        self.pairs = pairs
        self.sem = sem
        self.copies = {}

    def begin(self, name, *blocks):
        source, target = self.pairs[name]
        for b in blocks:
            copy = pltpu.make_async_copy(source.at[b], target.at[b], self.sem.at[len(self.copies)])
            self.copies[name, b] = copy
            copy.start()

    def wait(self, name, *blocks):
        for b in blocks:
            self.copies[name, b].wait()


def first_edges_kernel(
    count, inverses, lower, upper, basis, cross, chip, local, coupling, inv, base, sem
):
    width = base.shape[-1]
    last = count - 1
    loads = Loads(
        {
            "inverse": (inverses, inv),
            "basis": (basis, base),
            "lower": (lower, coupling.at[0]),
            "upper": (upper, coupling.at[1]),
        },
        sem,
    )
    loads.begin("inverse", 0, last)
    loads.begin("lower", 0)
    loads.begin("upper", last)
    loads.begin("basis", 0, last, 1, last - 1)
    loads.begin("inverse", 1, last - 1)
    loads.begin("upper", 0)
    loads.begin("lower", last)
    both = list(enumerate(sides(count)))
    outs = (cross, chip)
    loads.wait("inverse", 0, last)
    loads.wait("lower", 0)
    loads.wait("upper", last)
    for k, side in both:
        outs[k][:, 2 * width :] = rounded(dot(inv[side.edge], coupling[side.outward, side.edge]))
    loads.wait("basis", 0, last, 1, last - 1)
    loads.wait("inverse", 1, last - 1)
    inner = [rounded(dot(inv[side.inner], base[side.inner])) for k, side in both]
    for k, side in both:
        outs[k][:, :width] = rounded(dot(inv[side.edge], base[side.edge]))
    loads.wait("upper", 0)
    loads.wait("lower", last)
    rhs = []
    for k, side in both:
        value = dot(coupling[side.inward, side.edge], inner[k])
        rhs.append(rounded(base[side.edge].astype(F32) + value))
    for k, side in both:
        value = dot(inv[side.edge], rhs[k])
        outs[k][:, width : 2 * width] = rounded(value)
        local[k] = value


def first_edges(inverses, lower, upper, basis):
    count, size, width = basis.shape
    out = jax.ShapeDtypeStruct((size, 2 * width + size), BF16)
    return pl.pallas_call(
        functools.partial(first_edges_kernel, count),
        out_shape=(
            out,
            out,
            jax.ShapeDtypeStruct((2, size, width), F32),
            jax.ShapeDtypeStruct((2, count, size, size), BF16),
        ),
        in_specs=[HBM] * 4,
        out_specs=(VM,) * 4,
        scratch_shapes=[
            pltpu.VMEM((count, size, size), BF16),
            pltpu.VMEM((count, size, width), BF16),
            pltpu.SemaphoreType.DMA((12,)),
        ],
        compiler_params=params(),
        name="first_edges",
    )(*(in_hbm(x) for x in (inverses, lower, upper, basis)))


def ahead_blocks(count):
    return range(3, count - 3)


def right_side(b, coupling, base, left, right):
    value = dot(coupling[0, b], left) + dot(coupling[1, b], right)
    return rounded(base[b].astype(F32) + value)


def two_sweeps(count, inv, coupling, base, state, held, rhs, known, todo, ready=lambda b: None):
    for b in todo:
        ready(b)
        rhs[b] = right_side(b, coupling, base, state[b - 1], state[b + 1])
    for b in todo:
        held[b] = rounded(dot(inv[b], rhs[b]))
    for b in range(2, count - 2):
        rhs[b] = right_side(b, coupling, base, held[b - 1], held[b + 1])
    for k, side in enumerate(sides(count)):
        for j, (b, further) in enumerate(((side.edge, side.inner), (side.inner, side.third))):
            known[2 * k + j] = base[b].astype(F32) + dot(coupling[side.inward, b], held[further])


def first_pair_kernel(
    count, weight, lower, upper, coupling_in, inv, base, cross, chip, coupling, middle, known,
    ahead, factor, state, held, rhs, sem,
):
    width = base.shape[-1]
    inside = range(1, count - 1)
    deep = range(2, count - 2)
    factor[...] = jnp.full(factor.shape, weight[0], F32)
    loads = Loads({"lower": (lower, coupling.at[0]), "upper": (upper, coupling.at[1])}, sem)
    for b in inside:
        loads.begin("lower", b)
        loads.begin("upper", b)
    for side, payload in zip(sides(count), (cross, chip)):
        state[side.edge] = payload[:, :width]
    for b in inside:
        state[b] = rounded(dot(inv[b], base[b]))

    def ready(b):
        loads.wait("lower", b)
        loads.wait("upper", b)

    two_sweeps(count, inv, coupling, base, state, held, rhs, known, inside, ready)
    for b in deep:
        middle[b - 2] = rounded(dot(inv[b], rhs[b]))
    for b in ahead_blocks(count):
        rhs[b] = right_side(b, coupling, base, middle[b - 3], middle[b - 1])
    for b in ahead_blocks(count):
        ahead[b - 3] = rounded(dot(inv[b], rhs[b]))


def pair_cost(count, size, width):
    return cost(12 * (count - 2) * size * size * width, 6 * count * size * size)


def first_pair(weight, lower, upper, coupling, inv, base, cross, chip):
    count, size, width = base.shape
    return pl.pallas_call(
        functools.partial(first_pair_kernel, count),
        out_shape=(
            jax.ShapeDtypeStruct(coupling.shape, BF16),
            jax.ShapeDtypeStruct((count - 4, size, width), BF16),
            jax.ShapeDtypeStruct((4, size, width), F32),
            jax.ShapeDtypeStruct((count - 6, size, width), BF16),
            jax.ShapeDtypeStruct((8, width), F32),
        ),
        in_specs=[SM] + [HBM] * 2 + [VM] * 5,
        out_specs=(VM,) * 5,
        scratch_shapes=[pltpu.VMEM((count, size, width), BF16)] * 3
        + [pltpu.SemaphoreType.DMA((2 * count,))],
        input_output_aliases={3: 0},
        compiler_params=params(),
        cost_estimate=pair_cost(count, size, width),
        name="first_pair",
    )(weight, in_hbm(lower), in_hbm(upper), coupling, inv, base, cross, chip)


def last_pair_kernel(
    count, weight, inv, coupling, base, cross, chip, inner, previous, ahead, from_cross_joint,
    from_chip_joint, middle, known, change, state, held, rhs,
):
    width = base.shape[-1]
    for k, (own, halo_joint) in enumerate(((cross, from_cross_joint), (chip, from_chip_joint))):
        change[k] = dot(halo_joint[:, 2 * width :], own[:, :width])
    for k, (side, payload) in enumerate(zip(sides(count), (cross, chip))):
        state[side.edge] = payload[:, :width]
        state[side.inner] = inner[k]
    for b in range(2, count - 2):
        state[b] = previous[b - 2]
    for b in ahead_blocks(count):
        held[b] = ahead[b - 3]
    todo = [b for b in range(1, count - 1) if b not in ahead_blocks(count)]
    two_sweeps(count, inv, coupling, base, state, held, rhs, known, todo)
    for b in range(2, count - 2):
        middle[b - 2] = rounded(weight[:1] * dot(inv[b], rhs[b]))


def last_pair(weight, *operands):
    count, size, width = operands[2].shape
    return pl.pallas_call(
        functools.partial(last_pair_kernel, count),
        out_shape=(
            jax.ShapeDtypeStruct((count - 4, size, width), BF16),
            jax.ShapeDtypeStruct((4, size, width), F32),
            jax.ShapeDtypeStruct((2, size, width), F32),
        ),
        in_specs=[VM] * (1 + len(operands)),
        out_specs=(VM,) * 3,
        scratch_shapes=[pltpu.VMEM((count, size, width), BF16)] * 3,
        compiler_params=params(),
        cost_estimate=pair_cost(count, size, width),
        name="last_pair",
    )(weight, *operands)


def absorbed(count, inv, coupling, known, pieces, local, scale=lambda value: value):
    width = known.shape[-1]
    both = list(enumerate(sides(count)))
    values = []
    for k, side in both:
        joint, halo_change, halo = pieces[k]
        halo_next = halo[:, width : 2 * width].astype(F32) + halo_change
        edge_next = local[k] + dot(joint[:, 2 * width :], halo[:, :width])
        values.append((rounded(halo_next), rounded(edge_next)))
    rhs = []
    for j in (1, 0):
        for k, side in both:
            b = side.inner if j else side.edge
            value = known[2 * k + j] + dot(coupling[side.outward, b], values[k][j])
            rhs.append((b, rounded(value)))
    inner_a, inner_b, edge_a, edge_b = [
        rounded(scale(dot(inv[b], value))) for b, value in rhs
    ]
    return (edge_a, edge_b), (inner_a, inner_b)


def meet_kernel(
    count, inv, coupling, base, known, cross, chip, local, from_cross, from_chip,
    cross_out, chip_out, local_out, inner_out,
):
    width = known.shape[-1]
    pieces = [
        (own, dot(halo[:, 2 * width :], own[:, :width]), halo)
        for own, halo in ((cross, from_cross), (chip, from_chip))
    ]
    edge, inner = absorbed(count, inv, coupling, known, pieces, local)
    both = list(enumerate(sides(count)))
    outs = (cross_out, chip_out)
    rhs = []
    for k, side in both:
        value = base[side.edge].astype(F32) + dot(coupling[side.inward, side.edge], inner[k])
        rhs.append(rounded(value))
        outs[k][:, :width] = edge[k]
        inner_out[k] = inner[k]
    for k, side in both:
        value = dot(inv[side.edge], rhs[k])
        outs[k][:, width:] = rounded(value)
        local_out[k] = value


def meet(*operands):
    count, size, width = operands[2].shape
    out = jax.ShapeDtypeStruct((size, 2 * width), BF16)
    return pl.pallas_call(
        functools.partial(meet_kernel, count),
        out_shape=(
            out,
            out,
            jax.ShapeDtypeStruct((2, size, width), F32),
            jax.ShapeDtypeStruct((2, size, width), BF16),
        ),
        in_specs=[VM] * len(operands),
        out_specs=(VM, VM, VM, VM),
        compiler_params=params(),
        cost_estimate=cost(32 * size * size * width, 24 * size * size),
        name="meet",
    )(*operands)


def finish_kernel(
    count, weight, inv, coupling, known, change, middle, cross_joint, chip_joint, local,
    from_cross, from_chip, out,
):
    pieces = ((cross_joint, change[0], from_cross), (chip_joint, change[1], from_chip))
    for b in range(2, count - 2):
        out[b] = middle[b - 2]
    edge, inner = absorbed(
        count, inv, coupling, known, pieces, local, lambda value: weight[:1] * value
    )
    for k, side in enumerate(sides(count)):
        out[side.edge] = edge[k]
        out[side.inner] = inner[k]


def finish(weight, *operands):
    count, size, _ = operands[0].shape
    width = operands[2].shape[-1]
    return pl.pallas_call(
        functools.partial(finish_kernel, count),
        out_shape=jax.ShapeDtypeStruct((count, size, width), BF16),
        in_specs=[VM] * (1 + len(operands)),
        out_specs=VM,
        compiler_params=params(),
        cost_estimate=cost(24 * size * size * width, 24 * size * size),
        name="finish",
    )(weight, *operands)


def gram_kernel(received, filtered, gram):
    total = received[0].astype(F32)
    for p in range(1, received.shape[0]):
        total = total + received[p].astype(F32)
    filtered[...] = total
    value = lax.dot_general(
        total, total, (((0,), (0,)), ((), ())), precision=HI, preferred_element_type=F32
    )
    gram[...] = value.reshape(gram.shape)


def partial_gram(received, parts):
    poles, size, width = received.shape
    return pl.pallas_call(
        gram_kernel,
        out_shape=(
            jax.ShapeDtypeStruct((size, width), F32),
            jax.ShapeDtypeStruct((parts, width // parts, width), F32),
        ),
        in_specs=[VM],
        out_specs=(VM, VM),
        compiler_params=params(),
        name="gram",
    )(received)


def eliminate(value, work, inverse):
    n = value.shape[-1]
    subs = lax.broadcasted_iota(jnp.int32, (8, 2 * n), 0)
    work[:, :n] = value
    work[:, n:] = (
        lax.broadcasted_iota(jnp.int32, (n, n), 0) == lax.broadcasted_iota(jnp.int32, (n, n), 1)
    ).astype(F32)
    for p in range(n // 8):
        rows = work[8 * p : 8 * p + 8, :]
        for j in range(8):
            column = rows[:, 8 * p + j : 8 * p + j + 1]
            scale = lax.rsqrt(column[j : j + 1])
            pivot = rows[j : j + 1] * scale
            rows = jnp.where(
                subs == j, pivot, jnp.where(subs > j, rows - (column * scale) * pivot, rows)
            )
        work[8 * p : 8 * p + 8, :] = rows
        if 8 * p + 8 < n:
            change = lax.dot_general(
                rows[:, :n], rows, (((0,), (0,)), ((), ())), precision=HI, preferred_element_type=F32
            )
            work[8 * p + 8 :, :] = work[8 * p + 8 :, :] - change[8 * p + 8 :, :]
    inverse[...] = work[:, n:]


def split_product(a, b):
    a_high, b_high = rounded(a), rounded(b)
    a_low = rounded(a - a_high.astype(F32))
    b_low = rounded(b - b_high.astype(F32))
    left = jnp.concatenate([a_high, a_low], axis=1)
    right = jnp.concatenate([b_high, b_high], axis=1)
    over = (((1,), (1,)), ((), ()))
    return lax.dot_general(left, right, over, preferred_element_type=F32) + lax.dot_general(
        a_high, b_low, over, preferred_element_type=F32
    )


def orthonormal_kernel(total_rows, gram, filtered, out, work, inverse):
    n = out.shape[-1]
    value = gram[...].reshape(n, n) / total_rows
    rows = lax.broadcasted_iota(jnp.int32, (n, n), 0)
    cols = lax.broadcasted_iota(jnp.int32, (n, n), 1)
    same = rows == cols

    def phi(x):
        return jnp.where(rows > cols, x, jnp.where(same, 0.5 * x, 0.0))

    def exact(a, b):
        return jnp.dot(a, b, precision=HI, preferred_element_type=F32)

    def short(a, b):
        return dot(rounded(a), rounded(b))

    diagonal = jnp.where(same, value, 0.0)
    across = lax.rsqrt(jnp.sum(diagonal, axis=0, keepdims=True))
    down = lax.rsqrt(jnp.sum(diagonal, axis=1, keepdims=True))
    excess = jnp.where(same, 0.0, value * across * down)
    first = jnp.where(rows > cols, excess, 0.0)
    first_t = excess - first
    product = exact(first, excess)
    second_excess = -product - exact(first_t - product, first_t)
    second = phi(second_excess)
    second_t = second_excess - second
    product = short(second, second_excess)
    third_excess = -product - short(second_t - product, second_t)
    third = phi(third_excess)
    factor = exact(second, first) - first - second
    factor = jnp.where(same, 1.0 + factor, factor)
    factor = factor - short(third, factor)
    inverse[...] = factor * across
    error = jnp.sum(third_excess * third_excess)

    @pl.when(jnp.logical_not(error < 1e-7))
    def _():
        eliminate(value, work, inverse)

    out[...] = split_product(filtered[...], inverse[...])


def orthonormal(gram, filtered, total_rows):
    n = filtered.shape[-1]
    return pl.pallas_call(
        functools.partial(orthonormal_kernel, float(total_rows)),
        out_shape=jax.ShapeDtypeStruct(filtered.shape, F32),
        in_specs=[VM, VM],
        out_specs=VM,
        scratch_shapes=[pltpu.VMEM((n, 2 * n), F32), pltpu.VMEM((n, n), F32)],
        compiler_params=params(),
        name="orthonormal",
    )(gram, filtered)


POLE = ("x_hi", "y")
ROW = ("x_lo", "z", "core")
PLANE = ("x_hi", "y", "x_lo")
LINE = ("z", "core")


def swapped(cross, chip):
    peers = lax.axis_size(ROW)
    links = [(i, i + 1) for i in range(1, peers - 1, 2)]
    pairs = [(i, i + 1) for i in range(0, peers, 2)]
    return tuple(
        lax.ppermute(value, ROW, joined + [(j, i) for i, j in joined])
        for value, joined in ((cross, links), (chip, pairs))
    )


def exchange(value, axes):
    return lax.all_to_all(value, axes, split_axis=0, concat_axis=0, tiled=True)


def shards(basis, inverses, lower, upper, pole_weights):
    rows, width = basis.shape
    count, size = inverses.shape[1:3]
    inv = inverses.reshape(count, size, size)
    base = basis.reshape(count, size, width)
    cross, chip, local, coupling = first_edges(inv, lower, upper, base)
    joints = (cross, chip)
    halo_joints = swapped(cross, chip)
    coupling, middle, known, ahead, weight = first_pair(
        pole_weights, lower, upper, coupling, inv, base, cross, chip
    )
    cross, chip, local, inner = meet(inv, coupling, base, known, cross, chip, local, *halo_joints)
    halos = swapped(cross, chip)
    middle, known, change = last_pair(
        weight, inv, coupling, base, cross, chip, inner, middle, ahead, *halo_joints
    )
    solved = finish(
        weight, inv, coupling, known, change, middle, *joints, local, *halos
    )
    received = exchange(solved, POLE)
    plane = lax.axis_size(PLANE)
    filtered, gram = partial_gram(received, plane)
    gram = exchange(gram, PLANE).sum(0, keepdims=True)
    line = lax.axis_size(LINE)
    gram = exchange(jnp.broadcast_to(gram, (line, *gram.shape[1:])), LINE).sum(0, keepdims=True)
    gram = exchange(jnp.broadcast_to(gram, (plane, *gram.shape[1:])), PLANE)
    return orthonormal(gram, filtered, rows * lax.axis_size(ROW))


def solution(mesh):
    devices = mesh.devices.reshape(2, 4, 2, 8, 2)
    inner = Mesh(devices, ("x_hi", "y", "x_lo", "z", "core"))
    return jax.shard_map(
        shards,
        mesh=inner,
        in_specs=(
            P(ROW, None),
            P(POLE, ROW, None, None),
            P(ROW, None, None),
            P(ROW, None, None),
            P(POLE),
        ),
        out_specs=P(ROW + POLE, None),
        check_vma=False,
    )
```

```python
import functools

import jax
import jax.numpy as jnp
from jax import lax
from jax.experimental import pallas as pl
from jax.experimental.pallas import tpu as pltpu
from jax.sharding import Mesh, PartitionSpec as P

F32 = jnp.float32
BF16 = jnp.bfloat16
HI = lax.Precision.HIGHEST
VM = pl.BlockSpec(memory_space=pltpu.VMEM)
HBM = pl.BlockSpec(memory_space=pltpu.HBM)
SM = pl.BlockSpec(memory_space=pltpu.SMEM)
LIMIT = 16 << 20


def dot(a, b):
    return jnp.dot(a, b, preferred_element_type=F32)


def in_hbm(value):
    return pltpu.with_memory_space_constraint(value, pltpu.HBM)


def params():
    return pltpu.CompilerParams(vmem_limit_bytes=LIMIT)


def cost(flops, moved):
    return pl.CostEstimate(flops=int(flops), bytes_accessed=int(moved), transcendentals=0)


class Side:
    def __init__(self, which, count):
        self.low = lax.axis_index("core") == which
        self.edge = jnp.where(self.low, 0, count - 1)
        self.inner = jnp.where(self.low, 1, count - 2)
        self.third = jnp.where(self.low, 2, count - 3)
        self.outward = jnp.where(self.low, 0, 1)
        self.inward = 1 - self.outward


def sides(count):
    return Side(0, count), Side(1, count)


def rounded(value):
    return value.astype(BF16)


class Loads:
    def __init__(self, pairs, sem):
        self.pairs = pairs
        self.sem = sem
        self.copies = {}

    def begin(self, name, *blocks):
        source, target = self.pairs[name]
        for b in blocks:
            copy = pltpu.make_async_copy(source.at[b], target.at[b], self.sem.at[len(self.copies)])
            self.copies[name, b] = copy
            copy.start()

    def wait(self, name, *blocks):
        for b in blocks:
            self.copies[name, b].wait()


def first_edges_kernel(
    count, inverses, lower, upper, basis, cross, chip, local, coupling, inv, base, sem
):
    width = base.shape[-1]
    last = count - 1
    loads = Loads(
        {
            "inverse": (inverses, inv),
            "basis": (basis, base),
            "lower": (lower, coupling.at[0]),
            "upper": (upper, coupling.at[1]),
        },
        sem,
    )
    loads.begin("inverse", 0, last)
    loads.begin("lower", 0)
    loads.begin("upper", last)
    loads.begin("basis", 0, last, 1, last - 1)
    loads.begin("inverse", 1, last - 1)
    loads.begin("upper", 0)
    loads.begin("lower", last)
    both = list(enumerate(sides(count)))
    outs = (cross, chip)
    loads.wait("inverse", 0, last)
    loads.wait("lower", 0)
    loads.wait("upper", last)
    for k, side in both:
        outs[k][:, 2 * width :] = rounded(dot(inv[side.edge], coupling[side.outward, side.edge]))
    loads.wait("basis", 0, last, 1, last - 1)
    loads.wait("inverse", 1, last - 1)
    inner = [rounded(dot(inv[side.inner], base[side.inner])) for k, side in both]
    for k, side in both:
        outs[k][:, :width] = rounded(dot(inv[side.edge], base[side.edge]))
    loads.wait("upper", 0)
    loads.wait("lower", last)
    rhs = []
    for k, side in both:
        value = dot(coupling[side.inward, side.edge], inner[k])
        rhs.append(rounded(base[side.edge].astype(F32) + value))
    for k, side in both:
        value = dot(inv[side.edge], rhs[k])
        outs[k][:, width : 2 * width] = rounded(value)
        local[k] = value


def first_edges(inverses, lower, upper, basis):
    count, size, width = basis.shape
    out = jax.ShapeDtypeStruct((size, 2 * width + size), BF16)
    return pl.pallas_call(
        functools.partial(first_edges_kernel, count),
        out_shape=(
            out,
            out,
            jax.ShapeDtypeStruct((2, size, width), F32),
            jax.ShapeDtypeStruct((2, count, size, size), BF16),
        ),
        in_specs=[HBM] * 4,
        out_specs=(VM,) * 4,
        scratch_shapes=[
            pltpu.VMEM((count, size, size), BF16),
            pltpu.VMEM((count, size, width), BF16),
            pltpu.SemaphoreType.DMA((12,)),
        ],
        compiler_params=params(),
        name="first_edges",
    )(*(in_hbm(x) for x in (inverses, lower, upper, basis)))


def ahead_blocks(count):
    return range(3, count - 3)


def right_side(b, coupling, base, left, right):
    value = dot(coupling[0, b], left) + dot(coupling[1, b], right)
    return rounded(base[b].astype(F32) + value)


def two_sweeps(count, inv, coupling, base, state, held, rhs, known, todo, ready=lambda b: None):
    for b in todo:
        ready(b)
        rhs[b] = right_side(b, coupling, base, state[b - 1], state[b + 1])
    for b in todo:
        held[b] = rounded(dot(inv[b], rhs[b]))
    for b in range(2, count - 2):
        rhs[b] = right_side(b, coupling, base, held[b - 1], held[b + 1])
    for k, side in enumerate(sides(count)):
        for j, (b, further) in enumerate(((side.edge, side.inner), (side.inner, side.third))):
            known[2 * k + j] = base[b].astype(F32) + dot(coupling[side.inward, b], held[further])


def first_pair_kernel(
    count, weight, lower, upper, coupling_in, inv, base, cross, chip, coupling, middle, known,
    ahead, factor, state, held, rhs, sem,
):
    width = base.shape[-1]
    inside = range(1, count - 1)
    deep = range(2, count - 2)
    factor[...] = jnp.full(factor.shape, weight[0], F32)
    loads = Loads({"lower": (lower, coupling.at[0]), "upper": (upper, coupling.at[1])}, sem)
    for b in inside:
        loads.begin("lower", b)
        loads.begin("upper", b)
    for side, payload in zip(sides(count), (cross, chip)):
        state[side.edge] = payload[:, :width]
    for b in inside:
        state[b] = rounded(dot(inv[b], base[b]))

    def ready(b):
        loads.wait("lower", b)
        loads.wait("upper", b)

    two_sweeps(count, inv, coupling, base, state, held, rhs, known, inside, ready)
    for b in deep:
        middle[b - 2] = rounded(dot(inv[b], rhs[b]))
    for b in ahead_blocks(count):
        rhs[b] = right_side(b, coupling, base, middle[b - 3], middle[b - 1])
    for b in ahead_blocks(count):
        ahead[b - 3] = rounded(dot(inv[b], rhs[b]))


def pair_cost(count, size, width):
    return cost(12 * (count - 2) * size * size * width, 6 * count * size * size)


def first_pair(weight, lower, upper, coupling, inv, base, cross, chip):
    count, size, width = base.shape
    return pl.pallas_call(
        functools.partial(first_pair_kernel, count),
        out_shape=(
            jax.ShapeDtypeStruct(coupling.shape, BF16),
            jax.ShapeDtypeStruct((count - 4, size, width), BF16),
            jax.ShapeDtypeStruct((4, size, width), F32),
            jax.ShapeDtypeStruct((count - 6, size, width), BF16),
            jax.ShapeDtypeStruct((8, width), F32),
        ),
        in_specs=[SM] + [HBM] * 2 + [VM] * 5,
        out_specs=(VM,) * 5,
        scratch_shapes=[pltpu.VMEM((count, size, width), BF16)] * 3
        + [pltpu.SemaphoreType.DMA((2 * count,))],
        input_output_aliases={3: 0},
        compiler_params=params(),
        cost_estimate=pair_cost(count, size, width),
        name="first_pair",
    )(weight, in_hbm(lower), in_hbm(upper), coupling, inv, base, cross, chip)


def last_pair_kernel(
    count, weight, inv, coupling, base, cross, chip, inner, previous, ahead, from_cross_joint,
    from_chip_joint, middle, known, change, state, held, rhs,
):
    width = base.shape[-1]
    for k, (own, halo_joint) in enumerate(((cross, from_cross_joint), (chip, from_chip_joint))):
        change[k] = dot(halo_joint[:, 2 * width :], own[:, :width])
    for k, (side, payload) in enumerate(zip(sides(count), (cross, chip))):
        state[side.edge] = payload[:, :width]
        state[side.inner] = inner[k]
    for b in range(2, count - 2):
        state[b] = previous[b - 2]
    for b in ahead_blocks(count):
        held[b] = ahead[b - 3]
    todo = [b for b in range(1, count - 1) if b not in ahead_blocks(count)]
    two_sweeps(count, inv, coupling, base, state, held, rhs, known, todo)
    for b in range(2, count - 2):
        middle[b - 2] = rounded(weight[:1] * dot(inv[b], rhs[b]))


def last_pair(weight, *operands):
    count, size, width = operands[2].shape
    return pl.pallas_call(
        functools.partial(last_pair_kernel, count),
        out_shape=(
            jax.ShapeDtypeStruct((count - 4, size, width), BF16),
            jax.ShapeDtypeStruct((4, size, width), F32),
            jax.ShapeDtypeStruct((2, size, width), F32),
        ),
        in_specs=[VM] * (1 + len(operands)),
        out_specs=(VM,) * 3,
        scratch_shapes=[pltpu.VMEM((count, size, width), BF16)] * 3,
        compiler_params=params(),
        cost_estimate=pair_cost(count, size, width),
        name="last_pair",
    )(weight, *operands)


def absorbed(count, inv, coupling, known, pieces, local, scale=lambda value: value):
    width = known.shape[-1]
    both = list(enumerate(sides(count)))
    values = []
    for k, side in both:
        joint, halo_change, halo = pieces[k]
        halo_next = halo[:, width : 2 * width].astype(F32) + halo_change
        edge_next = local[k] + dot(joint[:, 2 * width :], halo[:, :width])
        values.append((rounded(halo_next), rounded(edge_next)))
    rhs = []
    for j in (1, 0):
        for k, side in both:
            b = side.inner if j else side.edge
            value = known[2 * k + j] + dot(coupling[side.outward, b], values[k][j])
            rhs.append((b, rounded(value)))
    inner_a, inner_b, edge_a, edge_b = [
        rounded(scale(dot(inv[b], value))) for b, value in rhs
    ]
    return (edge_a, edge_b), (inner_a, inner_b)


def meet_kernel(
    count, inv, coupling, base, known, cross, chip, local, from_cross, from_chip,
    cross_out, chip_out, local_out, inner_out,
):
    width = known.shape[-1]
    pieces = [
        (own, dot(halo[:, 2 * width :], own[:, :width]), halo)
        for own, halo in ((cross, from_cross), (chip, from_chip))
    ]
    edge, inner = absorbed(count, inv, coupling, known, pieces, local)
    both = list(enumerate(sides(count)))
    outs = (cross_out, chip_out)
    rhs = []
    for k, side in both:
        value = base[side.edge].astype(F32) + dot(coupling[side.inward, side.edge], inner[k])
        rhs.append(rounded(value))
        outs[k][:, :width] = edge[k]
        inner_out[k] = inner[k]
    for k, side in both:
        value = dot(inv[side.edge], rhs[k])
        outs[k][:, width:] = rounded(value)
        local_out[k] = value


def meet(*operands):
    count, size, width = operands[2].shape
    out = jax.ShapeDtypeStruct((size, 2 * width), BF16)
    return pl.pallas_call(
        functools.partial(meet_kernel, count),
        out_shape=(
            out,
            out,
            jax.ShapeDtypeStruct((2, size, width), F32),
            jax.ShapeDtypeStruct((2, size, width), BF16),
        ),
        in_specs=[VM] * len(operands),
        out_specs=(VM, VM, VM, VM),
        compiler_params=params(),
        cost_estimate=cost(32 * size * size * width, 24 * size * size),
        name="meet",
    )(*operands)


def finish_kernel(
    count, weight, inv, coupling, known, change, middle, cross_joint, chip_joint, local,
    from_cross, from_chip, out,
):
    pieces = ((cross_joint, change[0], from_cross), (chip_joint, change[1], from_chip))
    for b in range(2, count - 2):
        out[b] = middle[b - 2]
    edge, inner = absorbed(
        count, inv, coupling, known, pieces, local, lambda value: weight[:1] * value
    )
    for k, side in enumerate(sides(count)):
        out[side.edge] = edge[k]
        out[side.inner] = inner[k]


def finish(weight, *operands):
    count, size, _ = operands[0].shape
    width = operands[2].shape[-1]
    return pl.pallas_call(
        functools.partial(finish_kernel, count),
        out_shape=jax.ShapeDtypeStruct((count, size, width), BF16),
        in_specs=[VM] * (1 + len(operands)),
        out_specs=VM,
        compiler_params=params(),
        cost_estimate=cost(24 * size * size * width, 24 * size * size),
        name="finish",
    )(weight, *operands)


def gram_kernel(received, filtered, gram):
    total = received[0].astype(F32)
    for p in range(1, received.shape[0]):
        total = total + received[p].astype(F32)
    filtered[...] = total
    value = lax.dot_general(
        total, total, (((0,), (0,)), ((), ())), precision=HI, preferred_element_type=F32
    )
    gram[...] = value.reshape(gram.shape)


def partial_gram(received, parts):
    poles, size, width = received.shape
    return pl.pallas_call(
        gram_kernel,
        out_shape=(
            jax.ShapeDtypeStruct((size, width), F32),
            jax.ShapeDtypeStruct((parts, width // parts, width), F32),
        ),
        in_specs=[VM],
        out_specs=(VM, VM),
        compiler_params=params(),
        name="gram",
    )(received)


def eliminate(value, work, inverse):
    n = value.shape[-1]
    subs = lax.broadcasted_iota(jnp.int32, (8, 2 * n), 0)
    work[:, :n] = value
    work[:, n:] = (
        lax.broadcasted_iota(jnp.int32, (n, n), 0) == lax.broadcasted_iota(jnp.int32, (n, n), 1)
    ).astype(F32)
    for p in range(n // 8):
        rows = work[8 * p : 8 * p + 8, :]
        for j in range(8):
            column = rows[:, 8 * p + j : 8 * p + j + 1]
            scale = lax.rsqrt(column[j : j + 1])
            pivot = rows[j : j + 1] * scale
            rows = jnp.where(
                subs == j, pivot, jnp.where(subs > j, rows - (column * scale) * pivot, rows)
            )
        work[8 * p : 8 * p + 8, :] = rows
        if 8 * p + 8 < n:
            change = lax.dot_general(
                rows[:, :n], rows, (((0,), (0,)), ((), ())), precision=HI, preferred_element_type=F32
            )
            work[8 * p + 8 :, :] = work[8 * p + 8 :, :] - change[8 * p + 8 :, :]
    inverse[...] = work[:, n:]


def split_product(a, b):
    a_high, b_high = rounded(a), rounded(b)
    a_low = rounded(a - a_high.astype(F32))
    b_low = rounded(b - b_high.astype(F32))
    left = jnp.concatenate([a_high, a_low], axis=1)
    right = jnp.concatenate([b_high, b_high], axis=1)
    over = (((1,), (1,)), ((), ()))
    return lax.dot_general(left, right, over, preferred_element_type=F32) + lax.dot_general(
        a_high, b_low, over, preferred_element_type=F32
    )


def orthonormal_kernel(total_rows, gram, filtered, out, work, inverse):
    n = out.shape[-1]
    value = gram[...].reshape(n, n) / total_rows
    rows = lax.broadcasted_iota(jnp.int32, (n, n), 0)
    cols = lax.broadcasted_iota(jnp.int32, (n, n), 1)
    same = rows == cols

    def phi(x):
        return jnp.where(rows > cols, x, jnp.where(same, 0.5 * x, 0.0))

    def exact(a, b):
        return jnp.dot(a, b, precision=HI, preferred_element_type=F32)

    def short(a, b):
        return dot(rounded(a), rounded(b))

    diagonal = jnp.where(same, value, 0.0)
    across = lax.rsqrt(jnp.sum(diagonal, axis=0, keepdims=True))
    down = lax.rsqrt(jnp.sum(diagonal, axis=1, keepdims=True))
    excess = jnp.where(same, 0.0, value * across * down)
    first = jnp.where(rows > cols, excess, 0.0)
    first_t = excess - first
    product = exact(first, excess)
    second_excess = -product - exact(first_t - product, first_t)
    second = phi(second_excess)
    second_t = second_excess - second
    product = short(second, second_excess)
    third_excess = -product - short(second_t - product, second_t)
    third = phi(third_excess)
    factor = exact(second, first) - first - second
    factor = jnp.where(same, 1.0 + factor, factor)
    factor = factor - short(third, factor)
    inverse[...] = factor * across
    error = jnp.sum(third_excess * third_excess)

    @pl.when(jnp.logical_not(error < 1e-7))
    def _():
        eliminate(value, work, inverse)

    out[...] = split_product(filtered[...], inverse[...])


def orthonormal(gram, filtered, total_rows):
    n = filtered.shape[-1]
    return pl.pallas_call(
        functools.partial(orthonormal_kernel, float(total_rows)),
        out_shape=jax.ShapeDtypeStruct(filtered.shape, F32),
        in_specs=[VM, VM],
        out_specs=VM,
        scratch_shapes=[pltpu.VMEM((n, 2 * n), F32), pltpu.VMEM((n, n), F32)],
        compiler_params=params(),
        name="orthonormal",
    )(gram, filtered)


POLE = ("x_hi", "y")
ROW = ("x_lo", "z", "core")
PLANE = ("y", "x_lo", "core")
LINE = ("x_hi", "z")


def swapped(cross, chip):
    peers = lax.axis_size(ROW)
    links = [(i, i + 1) for i in range(1, peers - 1, 2)]
    pairs = [(i, i + 1) for i in range(0, peers, 2)]
    return tuple(
        lax.ppermute(value, ROW, joined + [(j, i) for i, j in joined])
        for value, joined in ((cross, links), (chip, pairs))
    )


def exchange(value, axes):
    return lax.all_to_all(value, axes, split_axis=0, concat_axis=0, tiled=True)


def shards(basis, inverses, lower, upper, pole_weights):
    rows, width = basis.shape
    count, size = inverses.shape[1:3]
    inv = inverses.reshape(count, size, size)
    base = basis.reshape(count, size, width)
    cross, chip, local, coupling = first_edges(inv, lower, upper, base)
    joints = (cross, chip)
    halo_joints = swapped(cross, chip)
    coupling, middle, known, ahead, weight = first_pair(
        pole_weights, lower, upper, coupling, inv, base, cross, chip
    )
    cross, chip, local, inner = meet(inv, coupling, base, known, cross, chip, local, *halo_joints)
    halos = swapped(cross, chip)
    middle, known, change = last_pair(
        weight, inv, coupling, base, cross, chip, inner, middle, ahead, *halo_joints
    )
    solved = finish(
        weight, inv, coupling, known, change, middle, *joints, local, *halos
    )
    received = exchange(solved, POLE)
    plane = lax.axis_size(PLANE)
    filtered, gram = partial_gram(received, plane)
    gram = exchange(gram, PLANE).sum(0, keepdims=True)
    line = lax.axis_size(LINE)
    gram = exchange(jnp.broadcast_to(gram, (line, *gram.shape[1:])), LINE).sum(0, keepdims=True)
    gram = exchange(jnp.broadcast_to(gram, (plane, *gram.shape[1:])), PLANE)
    return orthonormal(gram, filtered, rows * lax.axis_size(ROW))


def solution(mesh):
    devices = mesh.devices.reshape(2, 4, 2, 8, 2)
    inner = Mesh(devices, ("x_hi", "y", "x_lo", "z", "core"))
    return jax.shard_map(
        shards,
        mesh=inner,
        in_specs=(
            P(ROW, None),
            P(POLE, ROW, None, None),
            P(ROW, None, None),
            P(ROW, None, None),
            P(POLE),
        ),
        out_specs=P(ROW + POLE, None),
        check_vma=False,
    )
```

```python
import functools

import jax
import jax.numpy as jnp
from jax import lax
from jax.experimental import pallas as pl
from jax.experimental.pallas import tpu as pltpu
from jax.sharding import Mesh, PartitionSpec as P

F32 = jnp.float32
BF16 = jnp.bfloat16
HI = lax.Precision.HIGHEST
VM = pl.BlockSpec(memory_space=pltpu.VMEM)
HBM = pl.BlockSpec(memory_space=pltpu.HBM)
SM = pl.BlockSpec(memory_space=pltpu.SMEM)
LIMIT = 16 << 20


def dot(a, b):
    return jnp.dot(a, b, preferred_element_type=F32)


def in_hbm(value):
    return pltpu.with_memory_space_constraint(value, pltpu.HBM)


def params():
    return pltpu.CompilerParams(vmem_limit_bytes=LIMIT)


def cost(flops, moved):
    return pl.CostEstimate(flops=int(flops), bytes_accessed=int(moved), transcendentals=0)


class Side:
    def __init__(self, which, count):
        self.low = lax.axis_index("core") == which
        self.edge = jnp.where(self.low, 0, count - 1)
        self.inner = jnp.where(self.low, 1, count - 2)
        self.third = jnp.where(self.low, 2, count - 3)
        self.outward = jnp.where(self.low, 0, 1)
        self.inward = 1 - self.outward


def sides(count):
    return Side(0, count), Side(1, count)


def rounded(value):
    return value.astype(BF16)


class Loads:
    def __init__(self, pairs, sem):
        self.pairs = pairs
        self.sem = sem
        self.copies = {}

    def begin(self, name, *blocks):
        source, target = self.pairs[name]
        for b in blocks:
            copy = pltpu.make_async_copy(source.at[b], target.at[b], self.sem.at[len(self.copies)])
            self.copies[name, b] = copy
            copy.start()

    def wait(self, name, *blocks):
        for b in blocks:
            self.copies[name, b].wait()


def first_edges_kernel(
    count, inverses, lower, upper, basis, cross, chip, local, coupling, inv, base, sem
):
    width = base.shape[-1]
    last = count - 1
    loads = Loads(
        {
            "inverse": (inverses, inv),
            "basis": (basis, base),
            "lower": (lower, coupling.at[0]),
            "upper": (upper, coupling.at[1]),
        },
        sem,
    )
    loads.begin("inverse", 0, last)
    loads.begin("lower", 0)
    loads.begin("upper", last)
    loads.begin("basis", 0, last, 1, last - 1)
    loads.begin("inverse", 1, last - 1)
    loads.begin("upper", 0)
    loads.begin("lower", last)
    both = list(enumerate(sides(count)))
    outs = (cross, chip)
    loads.wait("inverse", 0, last)
    loads.wait("lower", 0)
    loads.wait("upper", last)
    for k, side in both:
        outs[k][:, 2 * width :] = rounded(dot(inv[side.edge], coupling[side.outward, side.edge]))
    loads.wait("basis", 0, last, 1, last - 1)
    loads.wait("inverse", 1, last - 1)
    inner = [rounded(dot(inv[side.inner], base[side.inner])) for k, side in both]
    for k, side in both:
        outs[k][:, :width] = rounded(dot(inv[side.edge], base[side.edge]))
    loads.wait("upper", 0)
    loads.wait("lower", last)
    rhs = []
    for k, side in both:
        value = dot(coupling[side.inward, side.edge], inner[k])
        rhs.append(rounded(base[side.edge].astype(F32) + value))
    for k, side in both:
        value = dot(inv[side.edge], rhs[k])
        outs[k][:, width : 2 * width] = rounded(value)
        local[k] = value


def first_edges(inverses, lower, upper, basis):
    count, size, width = basis.shape
    out = jax.ShapeDtypeStruct((size, 2 * width + size), BF16)
    return pl.pallas_call(
        functools.partial(first_edges_kernel, count),
        out_shape=(
            out,
            out,
            jax.ShapeDtypeStruct((2, size, width), F32),
            jax.ShapeDtypeStruct((2, count, size, size), BF16),
        ),
        in_specs=[HBM] * 4,
        out_specs=(VM,) * 4,
        scratch_shapes=[
            pltpu.VMEM((count, size, size), BF16),
            pltpu.VMEM((count, size, width), BF16),
            pltpu.SemaphoreType.DMA((12,)),
        ],
        compiler_params=params(),
        name="first_edges",
    )(*(in_hbm(x) for x in (inverses, lower, upper, basis)))


def ahead_blocks(count):
    return range(3, count - 3)


def right_side(b, coupling, base, left, right):
    value = dot(coupling[0, b], left) + dot(coupling[1, b], right)
    return rounded(base[b].astype(F32) + value)


def two_sweeps(count, inv, coupling, base, state, held, rhs, known, todo, ready=lambda b: None):
    for b in todo:
        ready(b)
        rhs[b] = right_side(b, coupling, base, state[b - 1], state[b + 1])
    for b in todo:
        held[b] = rounded(dot(inv[b], rhs[b]))
    for b in range(2, count - 2):
        rhs[b] = right_side(b, coupling, base, held[b - 1], held[b + 1])
    for k, side in enumerate(sides(count)):
        for j, (b, further) in enumerate(((side.edge, side.inner), (side.inner, side.third))):
            known[2 * k + j] = base[b].astype(F32) + dot(coupling[side.inward, b], held[further])


def first_pair_kernel(
    count, weight, lower, upper, coupling_in, inv, base, cross, chip, coupling, middle, known,
    ahead, factor, state, held, rhs, sem,
):
    width = base.shape[-1]
    inside = range(1, count - 1)
    deep = range(2, count - 2)
    factor[...] = jnp.full(factor.shape, weight[0], F32)
    loads = Loads({"lower": (lower, coupling.at[0]), "upper": (upper, coupling.at[1])}, sem)
    for b in inside:
        loads.begin("lower", b)
        loads.begin("upper", b)
    for side, payload in zip(sides(count), (cross, chip)):
        state[side.edge] = payload[:, :width]
    for b in inside:
        state[b] = rounded(dot(inv[b], base[b]))

    def ready(b):
        loads.wait("lower", b)
        loads.wait("upper", b)

    two_sweeps(count, inv, coupling, base, state, held, rhs, known, inside, ready)
    for b in deep:
        middle[b - 2] = rounded(dot(inv[b], rhs[b]))
    for b in ahead_blocks(count):
        rhs[b] = right_side(b, coupling, base, middle[b - 3], middle[b - 1])
    for b in ahead_blocks(count):
        ahead[b - 3] = rounded(dot(inv[b], rhs[b]))


def pair_cost(count, size, width):
    return cost(12 * (count - 2) * size * size * width, 6 * count * size * size)


def first_pair(weight, lower, upper, coupling, inv, base, cross, chip):
    count, size, width = base.shape
    return pl.pallas_call(
        functools.partial(first_pair_kernel, count),
        out_shape=(
            jax.ShapeDtypeStruct(coupling.shape, BF16),
            jax.ShapeDtypeStruct((count - 4, size, width), BF16),
            jax.ShapeDtypeStruct((4, size, width), F32),
            jax.ShapeDtypeStruct((count - 6, size, width), BF16),
            jax.ShapeDtypeStruct((8, width), F32),
        ),
        in_specs=[SM] + [HBM] * 2 + [VM] * 5,
        out_specs=(VM,) * 5,
        scratch_shapes=[pltpu.VMEM((count, size, width), BF16)] * 3
        + [pltpu.SemaphoreType.DMA((2 * count,))],
        input_output_aliases={3: 0},
        compiler_params=params(),
        cost_estimate=pair_cost(count, size, width),
        name="first_pair",
    )(weight, in_hbm(lower), in_hbm(upper), coupling, inv, base, cross, chip)


def last_pair_kernel(
    count, weight, inv, coupling, base, cross, chip, inner, previous, ahead, from_cross_joint,
    from_chip_joint, middle, known, change, state, held, rhs,
):
    width = base.shape[-1]
    for k, (own, halo_joint) in enumerate(((cross, from_cross_joint), (chip, from_chip_joint))):
        change[k] = dot(halo_joint[:, 2 * width :], own[:, :width])
    for k, (side, payload) in enumerate(zip(sides(count), (cross, chip))):
        state[side.edge] = payload[:, :width]
        state[side.inner] = inner[k]
    for b in range(2, count - 2):
        state[b] = previous[b - 2]
    for b in ahead_blocks(count):
        held[b] = ahead[b - 3]
    todo = [b for b in range(1, count - 1) if b not in ahead_blocks(count)]
    two_sweeps(count, inv, coupling, base, state, held, rhs, known, todo)
    for b in range(2, count - 2):
        middle[b - 2] = rounded(weight[:1] * dot(inv[b], rhs[b]))


def last_pair(weight, *operands):
    count, size, width = operands[2].shape
    return pl.pallas_call(
        functools.partial(last_pair_kernel, count),
        out_shape=(
            jax.ShapeDtypeStruct((count - 4, size, width), BF16),
            jax.ShapeDtypeStruct((4, size, width), F32),
            jax.ShapeDtypeStruct((2, size, width), F32),
        ),
        in_specs=[VM] * (1 + len(operands)),
        out_specs=(VM,) * 3,
        scratch_shapes=[pltpu.VMEM((count, size, width), BF16)] * 3,
        compiler_params=params(),
        cost_estimate=pair_cost(count, size, width),
        name="last_pair",
    )(weight, *operands)


def absorbed(count, inv, coupling, known, pieces, local, scale=lambda value: value):
    width = known.shape[-1]
    both = list(enumerate(sides(count)))
    values = []
    for k, side in both:
        joint, halo_change, halo = pieces[k]
        halo_next = halo[:, width : 2 * width].astype(F32) + halo_change
        edge_next = local[k] + dot(joint[:, 2 * width :], halo[:, :width])
        values.append((rounded(halo_next), rounded(edge_next)))
    rhs = []
    for j in (1, 0):
        for k, side in both:
            b = side.inner if j else side.edge
            value = known[2 * k + j] + dot(coupling[side.outward, b], values[k][j])
            rhs.append((b, rounded(value)))
    inner_a, inner_b, edge_a, edge_b = [
        rounded(scale(dot(inv[b], value))) for b, value in rhs
    ]
    return (edge_a, edge_b), (inner_a, inner_b)


def meet_kernel(
    count, inv, coupling, base, known, cross, chip, local, from_cross, from_chip,
    cross_out, chip_out, local_out, inner_out,
):
    width = known.shape[-1]
    pieces = [
        (own, dot(halo[:, 2 * width :], own[:, :width]), halo)
        for own, halo in ((cross, from_cross), (chip, from_chip))
    ]
    edge, inner = absorbed(count, inv, coupling, known, pieces, local)
    both = list(enumerate(sides(count)))
    outs = (cross_out, chip_out)
    rhs = []
    for k, side in both:
        value = base[side.edge].astype(F32) + dot(coupling[side.inward, side.edge], inner[k])
        rhs.append(rounded(value))
        outs[k][:, :width] = edge[k]
        inner_out[k] = inner[k]
    for k, side in both:
        value = dot(inv[side.edge], rhs[k])
        outs[k][:, width:] = rounded(value)
        local_out[k] = value


def meet(*operands):
    count, size, width = operands[2].shape
    out = jax.ShapeDtypeStruct((size, 2 * width), BF16)
    return pl.pallas_call(
        functools.partial(meet_kernel, count),
        out_shape=(
            out,
            out,
            jax.ShapeDtypeStruct((2, size, width), F32),
            jax.ShapeDtypeStruct((2, size, width), BF16),
        ),
        in_specs=[VM] * len(operands),
        out_specs=(VM, VM, VM, VM),
        compiler_params=params(),
        cost_estimate=cost(32 * size * size * width, 24 * size * size),
        name="meet",
    )(*operands)


def finish_kernel(
    count, weight, inv, coupling, known, change, middle, cross_joint, chip_joint, local,
    from_cross, from_chip, out,
):
    pieces = ((cross_joint, change[0], from_cross), (chip_joint, change[1], from_chip))
    for b in range(2, count - 2):
        out[b] = middle[b - 2]
    edge, inner = absorbed(
        count, inv, coupling, known, pieces, local, lambda value: weight[:1] * value
    )
    for k, side in enumerate(sides(count)):
        out[side.edge] = edge[k]
        out[side.inner] = inner[k]


def finish(weight, *operands):
    count, size, _ = operands[0].shape
    width = operands[2].shape[-1]
    return pl.pallas_call(
        functools.partial(finish_kernel, count),
        out_shape=jax.ShapeDtypeStruct((count, size, width), BF16),
        in_specs=[VM] * (1 + len(operands)),
        out_specs=VM,
        compiler_params=params(),
        cost_estimate=cost(24 * size * size * width, 24 * size * size),
        name="finish",
    )(weight, *operands)


def gram_kernel(received, filtered, gram):
    total = received[0].astype(F32)
    for p in range(1, received.shape[0]):
        total = total + received[p].astype(F32)
    filtered[...] = total
    value = lax.dot_general(
        total, total, (((0,), (0,)), ((), ())), precision=HI, preferred_element_type=F32
    )
    gram[...] = value.reshape(gram.shape)


def partial_gram(received, parts):
    poles, size, width = received.shape
    return pl.pallas_call(
        gram_kernel,
        out_shape=(
            jax.ShapeDtypeStruct((size, width), F32),
            jax.ShapeDtypeStruct((parts, width // parts, width), F32),
        ),
        in_specs=[VM],
        out_specs=(VM, VM),
        compiler_params=params(),
        name="gram",
    )(received)


def eliminate(value, work, inverse):
    n = value.shape[-1]
    subs = lax.broadcasted_iota(jnp.int32, (8, 2 * n), 0)
    work[:, :n] = value
    work[:, n:] = (
        lax.broadcasted_iota(jnp.int32, (n, n), 0) == lax.broadcasted_iota(jnp.int32, (n, n), 1)
    ).astype(F32)
    for p in range(n // 8):
        rows = work[8 * p : 8 * p + 8, :]
        for j in range(8):
            column = rows[:, 8 * p + j : 8 * p + j + 1]
            scale = lax.rsqrt(column[j : j + 1])
            pivot = rows[j : j + 1] * scale
            rows = jnp.where(
                subs == j, pivot, jnp.where(subs > j, rows - (column * scale) * pivot, rows)
            )
        work[8 * p : 8 * p + 8, :] = rows
        if 8 * p + 8 < n:
            change = lax.dot_general(
                rows[:, :n], rows, (((0,), (0,)), ((), ())), precision=HI, preferred_element_type=F32
            )
            work[8 * p + 8 :, :] = work[8 * p + 8 :, :] - change[8 * p + 8 :, :]
    inverse[...] = work[:, n:]


def split_product(a, b, axis=0):
    a_high, b_high = rounded(a), rounded(b)
    a_low = rounded(a - a_high.astype(F32))
    b_low = rounded(b - b_high.astype(F32))
    left = jnp.concatenate([a_high, a_low], axis=1)
    right = jnp.concatenate([b_high, b_high], axis=axis)
    over = (((1,), (axis,)), ((), ()))
    return lax.dot_general(left, right, over, preferred_element_type=F32) + lax.dot_general(
        a_high, b_low, over, preferred_element_type=F32
    )


def orthonormal_kernel(total_rows, gram, filtered, out, work, inverse):
    n = out.shape[-1]
    value = gram[...].reshape(n, n) / total_rows
    rows = lax.broadcasted_iota(jnp.int32, (n, n), 0)
    cols = lax.broadcasted_iota(jnp.int32, (n, n), 1)
    same = rows == cols

    def phi(x):
        return jnp.where(rows > cols, x, jnp.where(same, 0.5 * x, 0.0))

    def short(a, b):
        return dot(rounded(a), rounded(b))

    diagonal = jnp.where(same, value, 0.0)
    across = lax.rsqrt(jnp.sum(diagonal, axis=0, keepdims=True))
    down = lax.rsqrt(jnp.sum(diagonal, axis=1, keepdims=True))
    excess = jnp.where(same, 0.0, value * across * down)
    first = jnp.where(rows > cols, excess, 0.0)
    first_t = excess - first
    product = split_product(first, excess)
    second_excess = -product - split_product(first_t - product, first_t)
    second = phi(second_excess)
    second_t = second_excess - second
    product = short(second, second_excess)
    third_excess = -product - short(second_t - product, second_t)
    third = phi(third_excess)
    factor = split_product(second, first) - first - second
    factor = jnp.where(same, 1.0 + factor, factor)
    factor = factor - short(third, factor)
    inverse[...] = factor * across
    error = jnp.sum(third_excess * third_excess)

    @pl.when(jnp.logical_not(error < 1e-7))
    def _():
        eliminate(value, work, inverse)

    out[...] = split_product(filtered[...], inverse[...], 1)


def orthonormal(gram, filtered, total_rows):
    n = filtered.shape[-1]
    return pl.pallas_call(
        functools.partial(orthonormal_kernel, float(total_rows)),
        out_shape=jax.ShapeDtypeStruct(filtered.shape, F32),
        in_specs=[VM, VM],
        out_specs=VM,
        scratch_shapes=[pltpu.VMEM((n, 2 * n), F32), pltpu.VMEM((n, n), F32)],
        compiler_params=params(),
        name="orthonormal",
    )(gram, filtered)


POLE = ("x_hi", "y")
ROW = ("x_lo", "z", "core")
PLANE = ("y", "x_lo", "core")
LINE = ("x_hi", "z")


def swapped(cross, chip):
    peers = lax.axis_size(ROW)
    links = [(i, i + 1) for i in range(1, peers - 1, 2)]
    pairs = [(i, i + 1) for i in range(0, peers, 2)]
    return tuple(
        lax.ppermute(value, ROW, joined + [(j, i) for i, j in joined])
        for value, joined in ((cross, links), (chip, pairs))
    )


def exchange(value, axes):
    return lax.all_to_all(value, axes, split_axis=0, concat_axis=0, tiled=True)


def shards(basis, inverses, lower, upper, pole_weights):
    rows, width = basis.shape
    count, size = inverses.shape[1:3]
    inv = inverses.reshape(count, size, size)
    base = basis.reshape(count, size, width)
    cross, chip, local, coupling = first_edges(inv, lower, upper, base)
    joints = (cross, chip)
    halo_joints = swapped(cross, chip)
    coupling, middle, known, ahead, weight = first_pair(
        pole_weights, lower, upper, coupling, inv, base, cross, chip
    )
    cross, chip, local, inner = meet(inv, coupling, base, known, cross, chip, local, *halo_joints)
    halos = swapped(cross, chip)
    middle, known, change = last_pair(
        weight, inv, coupling, base, cross, chip, inner, middle, ahead, *halo_joints
    )
    solved = finish(
        weight, inv, coupling, known, change, middle, *joints, local, *halos
    )
    received = exchange(solved, POLE)
    plane = lax.axis_size(PLANE)
    filtered, gram = partial_gram(received, plane)
    gram = exchange(gram, PLANE).sum(0, keepdims=True)
    line = lax.axis_size(LINE)
    gram = exchange(jnp.broadcast_to(gram, (line, *gram.shape[1:])), LINE).sum(0, keepdims=True)
    gram = exchange(jnp.broadcast_to(gram, (plane, *gram.shape[1:])), PLANE)
    return orthonormal(gram, filtered, rows * lax.axis_size(ROW))


def solution(mesh):
    devices = mesh.devices.reshape(2, 4, 2, 8, 2)
    inner = Mesh(devices, ("x_hi", "y", "x_lo", "z", "core"))
    return jax.shard_map(
        shards,
        mesh=inner,
        in_specs=(
            P(ROW, None),
            P(POLE, ROW, None, None),
            P(ROW, None, None),
            P(ROW, None, None),
            P(POLE),
        ),
        out_specs=P(ROW + POLE, None),
        check_vma=False,
    )
```

```python
import functools

import jax
import jax.numpy as jnp
from jax import lax
from jax.experimental import pallas as pl
from jax.experimental.pallas import tpu as pltpu
from jax.sharding import Mesh, PartitionSpec as P

F32 = jnp.float32
BF16 = jnp.bfloat16
HI = lax.Precision.HIGHEST
VM = pl.BlockSpec(memory_space=pltpu.VMEM)
HBM = pl.BlockSpec(memory_space=pltpu.HBM)
SM = pl.BlockSpec(memory_space=pltpu.SMEM)
LIMIT = 16 << 20


def dot(a, b):
    return jnp.dot(a, b, preferred_element_type=F32)


def in_hbm(value):
    return pltpu.with_memory_space_constraint(value, pltpu.HBM)


def params():
    return pltpu.CompilerParams(vmem_limit_bytes=LIMIT)


def cost(flops, moved):
    return pl.CostEstimate(flops=int(flops), bytes_accessed=int(moved), transcendentals=0)


class Side:
    def __init__(self, which, count):
        self.low = lax.axis_index("core") == which
        self.edge = jnp.where(self.low, 0, count - 1)
        self.inner = jnp.where(self.low, 1, count - 2)
        self.third = jnp.where(self.low, 2, count - 3)
        self.outward = jnp.where(self.low, 0, 1)
        self.inward = 1 - self.outward


def sides(count):
    return Side(0, count), Side(1, count)


def rounded(value):
    return value.astype(BF16)


class Loads:
    def __init__(self, pairs, sem):
        self.pairs = pairs
        self.sem = sem
        self.copies = {}

    def begin(self, name, *blocks):
        source, target = self.pairs[name]
        for b in blocks:
            copy = pltpu.make_async_copy(source.at[b], target.at[b], self.sem.at[len(self.copies)])
            self.copies[name, b] = copy
            copy.start()

    def wait(self, name, *blocks):
        for b in blocks:
            self.copies[name, b].wait()


def first_edges_kernel(
    count, inverses, lower, upper, basis, cross, chip, local, coupling, inv, base, sem
):
    width = base.shape[-1]
    last = count - 1
    loads = Loads(
        {
            "inverse": (inverses, inv),
            "basis": (basis, base),
            "lower": (lower, coupling.at[0]),
            "upper": (upper, coupling.at[1]),
        },
        sem,
    )
    loads.begin("inverse", 0, last)
    loads.begin("lower", 0)
    loads.begin("upper", last)
    loads.begin("basis", 0, last, 1, last - 1)
    loads.begin("inverse", 1, last - 1)
    loads.begin("upper", 0)
    loads.begin("lower", last)
    both = list(enumerate(sides(count)))
    outs = (cross, chip)
    loads.wait("inverse", 0, last)
    loads.wait("lower", 0)
    loads.wait("upper", last)
    for k, side in both:
        outs[k][:, 2 * width :] = rounded(dot(inv[side.edge], coupling[side.outward, side.edge]))
    loads.wait("basis", 0, last, 1, last - 1)
    loads.wait("inverse", 1, last - 1)
    inner = [rounded(dot(inv[side.inner], base[side.inner])) for k, side in both]
    for k, side in both:
        outs[k][:, :width] = rounded(dot(inv[side.edge], base[side.edge]))
    loads.wait("upper", 0)
    loads.wait("lower", last)
    rhs = []
    for k, side in both:
        value = dot(coupling[side.inward, side.edge], inner[k])
        rhs.append(rounded(base[side.edge].astype(F32) + value))
    for k, side in both:
        value = dot(inv[side.edge], rhs[k])
        outs[k][:, width : 2 * width] = rounded(value)
        local[k] = value


def first_edges(inverses, lower, upper, basis):
    count, size, width = basis.shape
    out = jax.ShapeDtypeStruct((size, 2 * width + size), BF16)
    return pl.pallas_call(
        functools.partial(first_edges_kernel, count),
        out_shape=(
            out,
            out,
            jax.ShapeDtypeStruct((2, size, width), F32),
            jax.ShapeDtypeStruct((2, count, size, size), BF16),
        ),
        in_specs=[HBM] * 4,
        out_specs=(VM,) * 4,
        scratch_shapes=[
            pltpu.VMEM((count, size, size), BF16),
            pltpu.VMEM((count, size, width), BF16),
            pltpu.SemaphoreType.DMA((12,)),
        ],
        compiler_params=params(),
        name="first_edges",
    )(*(in_hbm(x) for x in (inverses, lower, upper, basis)))


def ahead_blocks(count):
    return range(3, count - 3)


def right_side(b, coupling, base, left, right):
    both = jnp.concatenate([coupling[0, b], coupling[1, b]], axis=1)
    value = dot(both, jnp.concatenate([left, right], axis=0))
    return rounded(base[b].astype(F32) + value)


def two_sweeps(count, inv, coupling, base, state, held, rhs, known, todo, ready=lambda b: None):
    for b in todo:
        ready(b)
        rhs[b] = right_side(b, coupling, base, state[b - 1], state[b + 1])
    for b in todo:
        held[b] = rounded(dot(inv[b], rhs[b]))
    for b in range(2, count - 2):
        rhs[b] = right_side(b, coupling, base, held[b - 1], held[b + 1])
    for k, side in enumerate(sides(count)):
        for j, (b, further) in enumerate(((side.edge, side.inner), (side.inner, side.third))):
            known[2 * k + j] = base[b].astype(F32) + dot(coupling[side.inward, b], held[further])


def first_pair_kernel(
    count, weight, lower, upper, coupling_in, inv, base, cross, chip, coupling, middle, known,
    ahead, factor, state, held, rhs, sem,
):
    width = base.shape[-1]
    inside = range(1, count - 1)
    deep = range(2, count - 2)
    factor[...] = jnp.full(factor.shape, weight[0], F32)
    loads = Loads({"lower": (lower, coupling.at[0]), "upper": (upper, coupling.at[1])}, sem)
    for b in inside:
        loads.begin("lower", b)
        loads.begin("upper", b)
    for side, payload in zip(sides(count), (cross, chip)):
        state[side.edge] = payload[:, :width]
    for b in inside:
        state[b] = rounded(dot(inv[b], base[b]))

    def ready(b):
        loads.wait("lower", b)
        loads.wait("upper", b)

    two_sweeps(count, inv, coupling, base, state, held, rhs, known, inside, ready)
    for b in deep:
        middle[b - 2] = rounded(dot(inv[b], rhs[b]))
    for b in ahead_blocks(count):
        rhs[b] = right_side(b, coupling, base, middle[b - 3], middle[b - 1])
    for b in ahead_blocks(count):
        ahead[b - 3] = rounded(dot(inv[b], rhs[b]))


def pair_cost(count, size, width):
    return cost(12 * (count - 2) * size * size * width, 6 * count * size * size)


def first_pair(weight, lower, upper, coupling, inv, base, cross, chip):
    count, size, width = base.shape
    return pl.pallas_call(
        functools.partial(first_pair_kernel, count),
        out_shape=(
            jax.ShapeDtypeStruct(coupling.shape, BF16),
            jax.ShapeDtypeStruct((count - 4, size, width), BF16),
            jax.ShapeDtypeStruct((4, size, width), F32),
            jax.ShapeDtypeStruct((count - 6, size, width), BF16),
            jax.ShapeDtypeStruct((8, width), F32),
        ),
        in_specs=[SM] + [HBM] * 2 + [VM] * 5,
        out_specs=(VM,) * 5,
        scratch_shapes=[pltpu.VMEM((count, size, width), BF16)] * 3
        + [pltpu.SemaphoreType.DMA((2 * count,))],
        input_output_aliases={3: 0},
        compiler_params=params(),
        cost_estimate=pair_cost(count, size, width),
        name="first_pair",
    )(weight, in_hbm(lower), in_hbm(upper), coupling, inv, base, cross, chip)


def last_pair_kernel(
    count, weight, inv, coupling, base, cross, chip, inner, previous, ahead, from_cross_joint,
    from_chip_joint, middle, known, change, state, held, rhs,
):
    width = base.shape[-1]
    for k, (own, halo_joint) in enumerate(((cross, from_cross_joint), (chip, from_chip_joint))):
        change[k] = dot(halo_joint[:, 2 * width :], own[:, :width])
    for k, (side, payload) in enumerate(zip(sides(count), (cross, chip))):
        state[side.edge] = payload[:, :width]
        state[side.inner] = inner[k]
    for b in range(2, count - 2):
        state[b] = previous[b - 2]
    for b in ahead_blocks(count):
        held[b] = ahead[b - 3]
    todo = [b for b in range(1, count - 1) if b not in ahead_blocks(count)]
    two_sweeps(count, inv, coupling, base, state, held, rhs, known, todo)
    for b in range(2, count - 2):
        middle[b - 2] = rounded(weight[:1] * dot(inv[b], rhs[b]))


def last_pair(weight, *operands):
    count, size, width = operands[2].shape
    return pl.pallas_call(
        functools.partial(last_pair_kernel, count),
        out_shape=(
            jax.ShapeDtypeStruct((count - 4, size, width), BF16),
            jax.ShapeDtypeStruct((4, size, width), F32),
            jax.ShapeDtypeStruct((2, size, width), F32),
        ),
        in_specs=[VM] * (1 + len(operands)),
        out_specs=(VM,) * 3,
        scratch_shapes=[pltpu.VMEM((count, size, width), BF16)] * 3,
        compiler_params=params(),
        cost_estimate=pair_cost(count, size, width),
        name="last_pair",
    )(weight, *operands)


def absorbed(count, inv, coupling, known, pieces, local, scale=lambda value: value):
    width = known.shape[-1]
    both = list(enumerate(sides(count)))
    values = []
    for k, side in both:
        joint, halo_change, halo = pieces[k]
        halo_next = halo[:, width : 2 * width].astype(F32) + halo_change
        edge_next = local[k] + dot(joint[:, 2 * width :], halo[:, :width])
        values.append((rounded(halo_next), rounded(edge_next)))
    rhs = []
    for j in (1, 0):
        for k, side in both:
            b = side.inner if j else side.edge
            value = known[2 * k + j] + dot(coupling[side.outward, b], values[k][j])
            rhs.append((b, rounded(value)))
    inner_a, inner_b, edge_a, edge_b = [
        rounded(scale(dot(inv[b], value))) for b, value in rhs
    ]
    return (edge_a, edge_b), (inner_a, inner_b)


def meet_kernel(
    count, inv, coupling, base, known, cross, chip, local, from_cross, from_chip,
    cross_out, chip_out, local_out, inner_out,
):
    width = known.shape[-1]
    pieces = [
        (own, dot(halo[:, 2 * width :], own[:, :width]), halo)
        for own, halo in ((cross, from_cross), (chip, from_chip))
    ]
    edge, inner = absorbed(count, inv, coupling, known, pieces, local)
    both = list(enumerate(sides(count)))
    outs = (cross_out, chip_out)
    rhs = []
    for k, side in both:
        value = base[side.edge].astype(F32) + dot(coupling[side.inward, side.edge], inner[k])
        rhs.append(rounded(value))
        outs[k][:, :width] = edge[k]
        inner_out[k] = inner[k]
    for k, side in both:
        value = dot(inv[side.edge], rhs[k])
        outs[k][:, width:] = rounded(value)
        local_out[k] = value


def meet(*operands):
    count, size, width = operands[2].shape
    out = jax.ShapeDtypeStruct((size, 2 * width), BF16)
    return pl.pallas_call(
        functools.partial(meet_kernel, count),
        out_shape=(
            out,
            out,
            jax.ShapeDtypeStruct((2, size, width), F32),
            jax.ShapeDtypeStruct((2, size, width), BF16),
        ),
        in_specs=[VM] * len(operands),
        out_specs=(VM, VM, VM, VM),
        compiler_params=params(),
        cost_estimate=cost(32 * size * size * width, 24 * size * size),
        name="meet",
    )(*operands)


def finish_kernel(
    count, weight, inv, coupling, known, change, middle, cross_joint, chip_joint, local,
    from_cross, from_chip, out,
):
    pieces = ((cross_joint, change[0], from_cross), (chip_joint, change[1], from_chip))
    for b in range(2, count - 2):
        out[b] = middle[b - 2]
    edge, inner = absorbed(
        count, inv, coupling, known, pieces, local, lambda value: weight[:1] * value
    )
    for k, side in enumerate(sides(count)):
        out[side.edge] = edge[k]
        out[side.inner] = inner[k]


def finish(weight, *operands):
    count, size, _ = operands[0].shape
    width = operands[2].shape[-1]
    return pl.pallas_call(
        functools.partial(finish_kernel, count),
        out_shape=jax.ShapeDtypeStruct((count, size, width), BF16),
        in_specs=[VM] * (1 + len(operands)),
        out_specs=VM,
        compiler_params=params(),
        cost_estimate=cost(24 * size * size * width, 24 * size * size),
        name="finish",
    )(weight, *operands)


def gram_kernel(received, filtered, gram):
    total = received[0].astype(F32)
    for p in range(1, received.shape[0]):
        total = total + received[p].astype(F32)
    filtered[...] = total
    value = lax.dot_general(
        total, total, (((0,), (0,)), ((), ())), precision=HI, preferred_element_type=F32
    )
    gram[...] = value.reshape(gram.shape)


def partial_gram(received, parts):
    poles, size, width = received.shape
    return pl.pallas_call(
        gram_kernel,
        out_shape=(
            jax.ShapeDtypeStruct((size, width), F32),
            jax.ShapeDtypeStruct((parts, width // parts, width), F32),
        ),
        in_specs=[VM],
        out_specs=(VM, VM),
        compiler_params=params(),
        name="gram",
    )(received)


def eliminate(value, work, inverse):
    n = value.shape[-1]
    subs = lax.broadcasted_iota(jnp.int32, (8, 2 * n), 0)
    work[:, :n] = value
    work[:, n:] = (
        lax.broadcasted_iota(jnp.int32, (n, n), 0) == lax.broadcasted_iota(jnp.int32, (n, n), 1)
    ).astype(F32)
    for p in range(n // 8):
        rows = work[8 * p : 8 * p + 8, :]
        for j in range(8):
            column = rows[:, 8 * p + j : 8 * p + j + 1]
            scale = lax.rsqrt(column[j : j + 1])
            pivot = rows[j : j + 1] * scale
            rows = jnp.where(
                subs == j, pivot, jnp.where(subs > j, rows - (column * scale) * pivot, rows)
            )
        work[8 * p : 8 * p + 8, :] = rows
        if 8 * p + 8 < n:
            change = lax.dot_general(
                rows[:, :n], rows, (((0,), (0,)), ((), ())), precision=HI, preferred_element_type=F32
            )
            work[8 * p + 8 :, :] = work[8 * p + 8 :, :] - change[8 * p + 8 :, :]
    inverse[...] = work[:, n:]


def split_product(a, b):
    a_high, b_high = rounded(a), rounded(b)
    a_low = rounded(a - a_high.astype(F32))
    b_low = rounded(b - b_high.astype(F32))
    left = jnp.concatenate([a_high, a_low], axis=1)
    right = jnp.concatenate([b_high, b_high], axis=1)
    over = (((1,), (1,)), ((), ()))
    return lax.dot_general(left, right, over, preferred_element_type=F32) + lax.dot_general(
        a_high, b_low, over, preferred_element_type=F32
    )


def orthonormal_kernel(total_rows, gram, filtered, out, work, inverse):
    n = out.shape[-1]
    value = gram[...].reshape(n, n) / total_rows
    rows = lax.broadcasted_iota(jnp.int32, (n, n), 0)
    cols = lax.broadcasted_iota(jnp.int32, (n, n), 1)
    same = rows == cols

    def phi(x):
        return jnp.where(rows > cols, x, jnp.where(same, 0.5 * x, 0.0))

    def exact(a, b):
        return jnp.dot(a, b, precision=HI, preferred_element_type=F32)

    def short(a, b):
        return dot(rounded(a), rounded(b))

    diagonal = jnp.where(same, value, 0.0)
    across = lax.rsqrt(jnp.sum(diagonal, axis=0, keepdims=True))
    down = lax.rsqrt(jnp.sum(diagonal, axis=1, keepdims=True))
    excess = jnp.where(same, 0.0, value * across * down)
    first = jnp.where(rows > cols, excess, 0.0)
    first_t = excess - first
    product = exact(first, excess)
    second_excess = -product - exact(first_t - product, first_t)
    second = phi(second_excess)
    second_t = second_excess - second
    product = short(second, second_excess)
    third_excess = -product - short(second_t - product, second_t)
    third = phi(third_excess)
    factor = exact(second, first) - first - second
    factor = jnp.where(same, 1.0 + factor, factor)
    factor = factor - short(third, factor)
    inverse[...] = factor * across
    error = jnp.sum(third_excess * third_excess)

    @pl.when(jnp.logical_not(error < 1e-7))
    def _():
        eliminate(value, work, inverse)

    out[...] = split_product(filtered[...], inverse[...])


def orthonormal(gram, filtered, total_rows):
    n = filtered.shape[-1]
    return pl.pallas_call(
        functools.partial(orthonormal_kernel, float(total_rows)),
        out_shape=jax.ShapeDtypeStruct(filtered.shape, F32),
        in_specs=[VM, VM],
        out_specs=VM,
        scratch_shapes=[pltpu.VMEM((n, 2 * n), F32), pltpu.VMEM((n, n), F32)],
        compiler_params=params(),
        name="orthonormal",
    )(gram, filtered)


POLE = ("x_hi", "y")
ROW = ("x_lo", "z", "core")
PLANE = ("x_hi", "y", "x_lo")
LINE = ("z", "core")


def swapped(cross, chip):
    peers = lax.axis_size(ROW)
    links = [(i, i + 1) for i in range(1, peers - 1, 2)]
    pairs = [(i, i + 1) for i in range(0, peers, 2)]
    return tuple(
        lax.ppermute(value, ROW, joined + [(j, i) for i, j in joined])
        for value, joined in ((cross, links), (chip, pairs))
    )


def exchange(value, axes):
    return lax.all_to_all(value, axes, split_axis=0, concat_axis=0, tiled=True)


def shards(basis, inverses, lower, upper, pole_weights):
    rows, width = basis.shape
    count, size = inverses.shape[1:3]
    inv = inverses.reshape(count, size, size)
    base = basis.reshape(count, size, width)
    cross, chip, local, coupling = first_edges(inv, lower, upper, base)
    joints = (cross, chip)
    halo_joints = swapped(cross, chip)
    coupling, middle, known, ahead, weight = first_pair(
        pole_weights, lower, upper, coupling, inv, base, cross, chip
    )
    cross, chip, local, inner = meet(inv, coupling, base, known, cross, chip, local, *halo_joints)
    halos = swapped(cross, chip)
    middle, known, change = last_pair(
        weight, inv, coupling, base, cross, chip, inner, middle, ahead, *halo_joints
    )
    solved = finish(
        weight, inv, coupling, known, change, middle, *joints, local, *halos
    )
    received = exchange(solved, POLE)
    plane = lax.axis_size(PLANE)
    filtered, gram = partial_gram(received, plane)
    gram = exchange(gram, PLANE).sum(0, keepdims=True)
    line = lax.axis_size(LINE)
    gram = exchange(jnp.broadcast_to(gram, (line, *gram.shape[1:])), LINE).sum(0, keepdims=True)
    gram = exchange(jnp.broadcast_to(gram, (plane, *gram.shape[1:])), PLANE)
    return orthonormal(gram, filtered, rows * lax.axis_size(ROW))


def solution(mesh):
    devices = mesh.devices.reshape(2, 4, 2, 8, 2)
    inner = Mesh(devices, ("x_hi", "y", "x_lo", "z", "core"))
    return jax.shard_map(
        shards,
        mesh=inner,
        in_specs=(
            P(ROW, None),
            P(POLE, ROW, None, None),
            P(ROW, None, None),
            P(ROW, None, None),
            P(POLE),
        ),
        out_specs=P(ROW + POLE, None),
        check_vma=False,
    )
```

```python
import functools

import jax
import jax.numpy as jnp
from jax import lax
from jax.experimental import pallas as pl
from jax.experimental.pallas import tpu as pltpu
from jax.sharding import Mesh, PartitionSpec as P

F32 = jnp.float32
BF16 = jnp.bfloat16
HI = lax.Precision.HIGHEST
VM = pl.BlockSpec(memory_space=pltpu.VMEM)
HBM = pl.BlockSpec(memory_space=pltpu.HBM)
SM = pl.BlockSpec(memory_space=pltpu.SMEM)
LIMIT = 16 << 20


def dot(a, b):
    return jnp.dot(a, b, preferred_element_type=F32)


def in_hbm(value):
    return pltpu.with_memory_space_constraint(value, pltpu.HBM)


def params():
    return pltpu.CompilerParams(vmem_limit_bytes=LIMIT)


def cost(flops, moved):
    return pl.CostEstimate(flops=int(flops), bytes_accessed=int(moved), transcendentals=0)


class Side:
    def __init__(self, which, count):
        self.low = lax.axis_index("core") == which
        self.edge = jnp.where(self.low, 0, count - 1)
        self.inner = jnp.where(self.low, 1, count - 2)
        self.third = jnp.where(self.low, 2, count - 3)
        self.outward = jnp.where(self.low, 0, 1)
        self.inward = 1 - self.outward


def sides(count):
    return Side(0, count), Side(1, count)


def rounded(value):
    return value.astype(BF16)


class Loads:
    def __init__(self, pairs, sem):
        self.pairs = pairs
        self.sem = sem
        self.copies = {}

    def begin(self, name, *blocks):
        source, target = self.pairs[name]
        for b in blocks:
            copy = pltpu.make_async_copy(source.at[b], target.at[b], self.sem.at[len(self.copies)])
            self.copies[name, b] = copy
            copy.start()

    def wait(self, name, *blocks):
        for b in blocks:
            self.copies[name, b].wait()


def first_edges_kernel(
    count, inverses, lower, upper, basis, cross, chip, local, coupling, inv, base, sem
):
    width = base.shape[-1]
    last = count - 1
    loads = Loads(
        {
            "inverse": (inverses, inv),
            "basis": (basis, base),
            "lower": (lower, coupling.at[0]),
            "upper": (upper, coupling.at[1]),
        },
        sem,
    )
    loads.begin("inverse", 0, last)
    loads.begin("lower", 0)
    loads.begin("upper", last)
    loads.begin("basis", 0, last, 1, last - 1)
    loads.begin("inverse", 1, last - 1)
    loads.begin("upper", 0)
    loads.begin("lower", last)
    for name in ("lower", "upper"):
        loads.begin(name, *early_blocks(count))
    both = list(enumerate(sides(count)))
    outs = (cross, chip)
    loads.wait("inverse", 0, last)
    loads.wait("lower", 0)
    loads.wait("upper", last)
    for k, side in both:
        outs[k][:, 2 * width :] = rounded(dot(inv[side.edge], coupling[side.outward, side.edge]))
    loads.wait("basis", 0, last, 1, last - 1)
    loads.wait("inverse", 1, last - 1)
    inner = [rounded(dot(inv[side.inner], base[side.inner])) for k, side in both]
    for k, side in both:
        outs[k][:, :width] = rounded(dot(inv[side.edge], base[side.edge]))
    loads.wait("upper", 0)
    loads.wait("lower", last)
    rhs = []
    for k, side in both:
        value = dot(coupling[side.inward, side.edge], inner[k])
        rhs.append(rounded(base[side.edge].astype(F32) + value))
    for k, side in both:
        value = dot(inv[side.edge], rhs[k])
        outs[k][:, width : 2 * width] = rounded(value)
        local[k] = value
    for name in ("lower", "upper"):
        loads.wait(name, *early_blocks(count))


def early_blocks(count):
    return range(1, count // 2 - 1)


def first_edges(inverses, lower, upper, basis):
    count, size, width = basis.shape
    out = jax.ShapeDtypeStruct((size, 2 * width + size), BF16)
    return pl.pallas_call(
        functools.partial(first_edges_kernel, count),
        out_shape=(
            out,
            out,
            jax.ShapeDtypeStruct((2, size, width), F32),
            jax.ShapeDtypeStruct((2, count, size, size), BF16),
        ),
        in_specs=[HBM] * 4,
        out_specs=(VM,) * 4,
        scratch_shapes=[
            pltpu.VMEM((count, size, size), BF16),
            pltpu.VMEM((count, size, width), BF16),
            pltpu.SemaphoreType.DMA((12 + count,)),
        ],
        compiler_params=params(),
        name="first_edges",
    )(*(in_hbm(x) for x in (inverses, lower, upper, basis)))


def ahead_blocks(count):
    return range(3, count - 3)


def right_side(b, coupling, base, left, right):
    value = dot(coupling[0, b], left) + dot(coupling[1, b], right)
    return rounded(base[b].astype(F32) + value)


def two_sweeps(count, inv, coupling, base, state, held, rhs, known, todo, ready=lambda b: None):
    for b in todo:
        ready(b)
        rhs[b] = right_side(b, coupling, base, state[b - 1], state[b + 1])
    for b in todo:
        held[b] = rounded(dot(inv[b], rhs[b]))
    for b in range(2, count - 2):
        rhs[b] = right_side(b, coupling, base, held[b - 1], held[b + 1])
    for k, side in enumerate(sides(count)):
        for j, (b, further) in enumerate(((side.edge, side.inner), (side.inner, side.third))):
            known[2 * k + j] = base[b].astype(F32) + dot(coupling[side.inward, b], held[further])


def first_pair_kernel(
    count, weight, lower, upper, coupling_in, inv, base, cross, chip, coupling, middle, known,
    ahead, factor, state, held, rhs, sem,
):
    width = base.shape[-1]
    inside = range(1, count - 1)
    deep = range(2, count - 2)
    factor[...] = jnp.full(factor.shape, weight[0], F32)
    loads = Loads({"lower": (lower, coupling.at[0]), "upper": (upper, coupling.at[1])}, sem)
    late = [b for b in inside if b not in early_blocks(count)]
    for b in late:
        loads.begin("lower", b)
        loads.begin("upper", b)
    for side, payload in zip(sides(count), (cross, chip)):
        state[side.edge] = payload[:, :width]
    for b in inside:
        state[b] = rounded(dot(inv[b], base[b]))

    def ready(b):
        if b in late:
            loads.wait("lower", b)
            loads.wait("upper", b)

    two_sweeps(count, inv, coupling, base, state, held, rhs, known, inside, ready)
    for b in deep:
        middle[b - 2] = rounded(dot(inv[b], rhs[b]))
    for b in ahead_blocks(count):
        rhs[b] = right_side(b, coupling, base, middle[b - 3], middle[b - 1])
    for b in ahead_blocks(count):
        ahead[b - 3] = rounded(dot(inv[b], rhs[b]))


def pair_cost(count, size, width):
    return cost(12 * (count - 2) * size * size * width, 6 * count * size * size)


def first_pair(weight, lower, upper, coupling, inv, base, cross, chip):
    count, size, width = base.shape
    return pl.pallas_call(
        functools.partial(first_pair_kernel, count),
        out_shape=(
            jax.ShapeDtypeStruct(coupling.shape, BF16),
            jax.ShapeDtypeStruct((count - 4, size, width), BF16),
            jax.ShapeDtypeStruct((4, size, width), F32),
            jax.ShapeDtypeStruct((count - 6, size, width), BF16),
            jax.ShapeDtypeStruct((8, width), F32),
        ),
        in_specs=[SM] + [HBM] * 2 + [VM] * 5,
        out_specs=(VM,) * 5,
        scratch_shapes=[pltpu.VMEM((count, size, width), BF16)] * 3
        + [pltpu.SemaphoreType.DMA((2 * count,))],
        input_output_aliases={3: 0},
        compiler_params=params(),
        cost_estimate=pair_cost(count, size, width),
        name="first_pair",
    )(weight, in_hbm(lower), in_hbm(upper), coupling, inv, base, cross, chip)


def last_pair_kernel(
    count, weight, inv, coupling, base, cross, chip, inner, previous, ahead, from_cross_joint,
    from_chip_joint, middle, known, change, state, held, rhs,
):
    width = base.shape[-1]
    for k, (own, halo_joint) in enumerate(((cross, from_cross_joint), (chip, from_chip_joint))):
        change[k] = dot(halo_joint[:, 2 * width :], own[:, :width])
    for k, (side, payload) in enumerate(zip(sides(count), (cross, chip))):
        state[side.edge] = payload[:, :width]
        state[side.inner] = inner[k]
    for b in range(2, count - 2):
        state[b] = previous[b - 2]
    for b in ahead_blocks(count):
        held[b] = ahead[b - 3]
    todo = [b for b in range(1, count - 1) if b not in ahead_blocks(count)]
    two_sweeps(count, inv, coupling, base, state, held, rhs, known, todo)
    for b in range(2, count - 2):
        middle[b - 2] = rounded(weight[:1] * dot(inv[b], rhs[b]))


def last_pair(weight, *operands):
    count, size, width = operands[2].shape
    return pl.pallas_call(
        functools.partial(last_pair_kernel, count),
        out_shape=(
            jax.ShapeDtypeStruct((count - 4, size, width), BF16),
            jax.ShapeDtypeStruct((4, size, width), F32),
            jax.ShapeDtypeStruct((2, size, width), F32),
        ),
        in_specs=[VM] * (1 + len(operands)),
        out_specs=(VM,) * 3,
        scratch_shapes=[pltpu.VMEM((count, size, width), BF16)] * 3,
        compiler_params=params(),
        cost_estimate=pair_cost(count, size, width),
        name="last_pair",
    )(weight, *operands)


def absorbed(count, inv, coupling, known, pieces, local, scale=lambda value: value):
    width = known.shape[-1]
    both = list(enumerate(sides(count)))
    values = []
    for k, side in both:
        joint, halo_change, halo = pieces[k]
        halo_next = halo[:, width : 2 * width].astype(F32) + halo_change
        edge_next = local[k] + dot(joint[:, 2 * width :], halo[:, :width])
        values.append((rounded(halo_next), rounded(edge_next)))
    rhs = []
    for j in (1, 0):
        for k, side in both:
            b = side.inner if j else side.edge
            value = known[2 * k + j] + dot(coupling[side.outward, b], values[k][j])
            rhs.append((b, rounded(value)))
    inner_a, inner_b, edge_a, edge_b = [
        rounded(scale(dot(inv[b], value))) for b, value in rhs
    ]
    return (edge_a, edge_b), (inner_a, inner_b)


def meet_kernel(
    count, inv, coupling, base, known, cross, chip, local, from_cross, from_chip,
    cross_out, chip_out, local_out, inner_out,
):
    width = known.shape[-1]
    pieces = [
        (own, dot(halo[:, 2 * width :], own[:, :width]), halo)
        for own, halo in ((cross, from_cross), (chip, from_chip))
    ]
    edge, inner = absorbed(count, inv, coupling, known, pieces, local)
    both = list(enumerate(sides(count)))
    outs = (cross_out, chip_out)
    rhs = []
    for k, side in both:
        value = base[side.edge].astype(F32) + dot(coupling[side.inward, side.edge], inner[k])
        rhs.append(rounded(value))
        outs[k][:, :width] = edge[k]
        inner_out[k] = inner[k]
    for k, side in both:
        value = dot(inv[side.edge], rhs[k])
        outs[k][:, width:] = rounded(value)
        local_out[k] = value


def meet(*operands):
    count, size, width = operands[2].shape
    out = jax.ShapeDtypeStruct((size, 2 * width), BF16)
    return pl.pallas_call(
        functools.partial(meet_kernel, count),
        out_shape=(
            out,
            out,
            jax.ShapeDtypeStruct((2, size, width), F32),
            jax.ShapeDtypeStruct((2, size, width), BF16),
        ),
        in_specs=[VM] * len(operands),
        out_specs=(VM, VM, VM, VM),
        compiler_params=params(),
        cost_estimate=cost(32 * size * size * width, 24 * size * size),
        name="meet",
    )(*operands)


def finish_kernel(
    count, weight, inv, coupling, known, change, middle, cross_joint, chip_joint, local,
    from_cross, from_chip, out,
):
    pieces = ((cross_joint, change[0], from_cross), (chip_joint, change[1], from_chip))
    for b in range(2, count - 2):
        out[b] = middle[b - 2]
    edge, inner = absorbed(
        count, inv, coupling, known, pieces, local, lambda value: weight[:1] * value
    )
    for k, side in enumerate(sides(count)):
        out[side.edge] = edge[k]
        out[side.inner] = inner[k]


def finish(weight, *operands):
    count, size, _ = operands[0].shape
    width = operands[2].shape[-1]
    return pl.pallas_call(
        functools.partial(finish_kernel, count),
        out_shape=jax.ShapeDtypeStruct((count, size, width), BF16),
        in_specs=[VM] * (1 + len(operands)),
        out_specs=VM,
        compiler_params=params(),
        cost_estimate=cost(24 * size * size * width, 24 * size * size),
        name="finish",
    )(weight, *operands)


def gram_kernel(received, filtered, gram):
    total = received[0].astype(F32)
    for p in range(1, received.shape[0]):
        total = total + received[p].astype(F32)
    filtered[...] = total
    value = lax.dot_general(
        total, total, (((0,), (0,)), ((), ())), precision=HI, preferred_element_type=F32
    )
    gram[...] = value.reshape(gram.shape)


def partial_gram(received, parts):
    poles, size, width = received.shape
    return pl.pallas_call(
        gram_kernel,
        out_shape=(
            jax.ShapeDtypeStruct((size, width), F32),
            jax.ShapeDtypeStruct((parts, width // parts, width), F32),
        ),
        in_specs=[VM],
        out_specs=(VM, VM),
        compiler_params=params(),
        name="gram",
    )(received)


def eliminate(value, work, inverse):
    n = value.shape[-1]
    subs = lax.broadcasted_iota(jnp.int32, (8, 2 * n), 0)
    work[:, :n] = value
    work[:, n:] = (
        lax.broadcasted_iota(jnp.int32, (n, n), 0) == lax.broadcasted_iota(jnp.int32, (n, n), 1)
    ).astype(F32)
    for p in range(n // 8):
        rows = work[8 * p : 8 * p + 8, :]
        for j in range(8):
            column = rows[:, 8 * p + j : 8 * p + j + 1]
            scale = lax.rsqrt(column[j : j + 1])
            pivot = rows[j : j + 1] * scale
            rows = jnp.where(
                subs == j, pivot, jnp.where(subs > j, rows - (column * scale) * pivot, rows)
            )
        work[8 * p : 8 * p + 8, :] = rows
        if 8 * p + 8 < n:
            change = lax.dot_general(
                rows[:, :n], rows, (((0,), (0,)), ((), ())), precision=HI, preferred_element_type=F32
            )
            work[8 * p + 8 :, :] = work[8 * p + 8 :, :] - change[8 * p + 8 :, :]
    inverse[...] = work[:, n:]


def split_product(a, b):
    a_high, b_high = rounded(a), rounded(b)
    a_low = rounded(a - a_high.astype(F32))
    b_low = rounded(b - b_high.astype(F32))
    left = jnp.concatenate([a_high, a_low], axis=1)
    right = jnp.concatenate([b_high, b_high], axis=1)
    over = (((1,), (1,)), ((), ()))
    return lax.dot_general(left, right, over, preferred_element_type=F32) + lax.dot_general(
        a_high, b_low, over, preferred_element_type=F32
    )


def orthonormal_kernel(total_rows, gram, filtered, out, work, inverse):
    n = out.shape[-1]
    value = gram[...].reshape(n, n) / total_rows
    rows = lax.broadcasted_iota(jnp.int32, (n, n), 0)
    cols = lax.broadcasted_iota(jnp.int32, (n, n), 1)
    same = rows == cols

    def phi(x):
        return jnp.where(rows > cols, x, jnp.where(same, 0.5 * x, 0.0))

    def exact(a, b):
        return jnp.dot(a, b, precision=HI, preferred_element_type=F32)

    def short(a, b):
        return dot(rounded(a), rounded(b))

    diagonal = jnp.where(same, value, 0.0)
    across = lax.rsqrt(jnp.sum(diagonal, axis=0, keepdims=True))
    down = lax.rsqrt(jnp.sum(diagonal, axis=1, keepdims=True))
    excess = jnp.where(same, 0.0, value * across * down)
    first = jnp.where(rows > cols, excess, 0.0)
    first_t = excess - first
    product = exact(first, excess)
    second_excess = -product - exact(first_t - product, first_t)
    second = phi(second_excess)
    second_t = second_excess - second
    product = short(second, second_excess)
    third_excess = -product - short(second_t - product, second_t)
    third = phi(third_excess)
    factor = exact(second, first) - first - second
    factor = jnp.where(same, 1.0 + factor, factor)
    factor = factor - short(third, factor)
    inverse[...] = factor * across
    error = jnp.sum(third_excess * third_excess)

    @pl.when(jnp.logical_not(error < 1e-7))
    def _():
        eliminate(value, work, inverse)

    out[...] = split_product(filtered[...], inverse[...])


def orthonormal(gram, filtered, total_rows):
    n = filtered.shape[-1]
    return pl.pallas_call(
        functools.partial(orthonormal_kernel, float(total_rows)),
        out_shape=jax.ShapeDtypeStruct(filtered.shape, F32),
        in_specs=[VM, VM],
        out_specs=VM,
        scratch_shapes=[pltpu.VMEM((n, 2 * n), F32), pltpu.VMEM((n, n), F32)],
        compiler_params=params(),
        name="orthonormal",
    )(gram, filtered)


POLE = ("x_hi", "y")
ROW = ("x_lo", "z", "core")
PLANE = ("x_hi", "y", "x_lo")
LINE = ("z", "core")


def swapped(cross, chip):
    peers = lax.axis_size(ROW)
    links = [(i, i + 1) for i in range(1, peers - 1, 2)]
    pairs = [(i, i + 1) for i in range(0, peers, 2)]
    return tuple(
        lax.ppermute(value, ROW, joined + [(j, i) for i, j in joined])
        for value, joined in ((cross, links), (chip, pairs))
    )


def exchange(value, axes):
    return lax.all_to_all(value, axes, split_axis=0, concat_axis=0, tiled=True)


def shards(basis, inverses, lower, upper, pole_weights):
    rows, width = basis.shape
    count, size = inverses.shape[1:3]
    inv = inverses.reshape(count, size, size)
    base = basis.reshape(count, size, width)
    cross, chip, local, coupling = first_edges(inv, lower, upper, base)
    joints = (cross, chip)
    halo_joints = swapped(cross, chip)
    coupling, middle, known, ahead, weight = first_pair(
        pole_weights, lower, upper, coupling, inv, base, cross, chip
    )
    cross, chip, local, inner = meet(inv, coupling, base, known, cross, chip, local, *halo_joints)
    halos = swapped(cross, chip)
    middle, known, change = last_pair(
        weight, inv, coupling, base, cross, chip, inner, middle, ahead, *halo_joints
    )
    solved = finish(
        weight, inv, coupling, known, change, middle, *joints, local, *halos
    )
    received = exchange(solved, POLE)
    plane = lax.axis_size(PLANE)
    filtered, gram = partial_gram(received, plane)
    gram = exchange(gram, PLANE).sum(0, keepdims=True)
    line = lax.axis_size(LINE)
    gram = exchange(jnp.broadcast_to(gram, (line, *gram.shape[1:])), LINE).sum(0, keepdims=True)
    gram = exchange(jnp.broadcast_to(gram, (plane, *gram.shape[1:])), PLANE)
    return orthonormal(gram, filtered, rows * lax.axis_size(ROW))


def solution(mesh):
    devices = mesh.devices.reshape(2, 4, 2, 8, 2)
    inner = Mesh(devices, ("x_hi", "y", "x_lo", "z", "core"))
    return jax.shard_map(
        shards,
        mesh=inner,
        in_specs=(
            P(ROW, None),
            P(POLE, ROW, None, None),
            P(ROW, None, None),
            P(ROW, None, None),
            P(POLE),
        ),
        out_specs=P(ROW + POLE, None),
        check_vma=False,
    )
```
